32 devices in a mesh: fsdp: 4 (over y, core), ctx: 2 (over x), tp: 4 (over z).
Axes of the slice: x: 2, y: 2, z: 4, core: 2. Of those that a mesh axis runs over, the one named last changes fastest.
Arguments:
- hidden_in: bfloat16 [16, 1024, 768], P('fsdp', 'ctx'), may hold values from -6 to 6
- prev_logits: bfloat16 [16, 12, 1024, 1024], P('fsdp', 'tp', 'ctx'), may hold values from -6 to 6
- w_query: bfloat16 [768, 768], P('fsdp', 'tp'), may hold values from -0.21875 to 0.21875
- w_key: bfloat16 [768, 768], P('fsdp', 'tp'), may hold values from -0.21875 to 0.21875
- w_value: bfloat16 [768, 768], P('fsdp', 'tp'), may hold values from -0.21875 to 0.21875
- w_out: bfloat16 [768, 768], P('fsdp', 'tp'), may hold values from -1.75 to 1.75
- w_inner: bfloat16 [768, 3072], P('fsdp', 'tp'), may hold values from -0.21875 to 0.21875
- w_outer: bfloat16 [768, 3072], P('fsdp', 'tp'), may hold values from -0.109375 to 0.109375
- b_query: float32 [768], P('tp'), may hold values from -3 to 3
- b_value: float32 [768], P('tp'), may hold values from -3 to 3
- b_out: float32 [768], replicated, may hold values from -3 to 3
- b_inner: float32 [3072], P('tp'), may hold values from -3 to 3
- b_outer: float32 [768], replicated, may hold values from -3 to 3
- gain_attn: float32 [768], replicated, may hold values from 0.25 to 1.75
- shift_attn: float32 [768], replicated, may hold values from -3 to 3
- gain_ffn: float32 [768], replicated, may hold values from 0.25 to 1.75
- shift_ffn: float32 [768], replicated, may hold values from -3 to 3
- d_output: bfloat16 [16, 1024, 768], P('fsdp', 'ctx'), may hold values from -6 to 6
- d_logits: bfloat16 [16, 12, 1024, 1024], P('fsdp', 'tp', 'ctx'), may hold values from -6 to 6
Outputs:
- output: bfloat16 [16, 1024, 768], P('fsdp', 'ctx')
- new_logits: bfloat16 [16, 12, 1024, 1024], P('fsdp', 'tp', 'ctx')
- d_hidden: float32 [16, 1024, 768], P('fsdp', 'ctx')
- d_prev: bfloat16 [16, 12, 1024, 1024], P('fsdp', 'tp', 'ctx')
- d_w_query: float32 [768, 768], P('fsdp', 'tp')
- d_w_key: float32 [768, 768], P('fsdp', 'tp')
- d_w_value: float32 [768, 768], P('fsdp', 'tp')
- d_w_out: float32 [768, 768], P('fsdp', 'tp')
- d_w_inner: float32 [768, 3072], P('fsdp', 'tp')
- d_w_outer: float32 [768, 3072], P('fsdp', 'tp')
- d_b_query: float32 [768], P('tp')
- d_b_value: float32 [768], P('tp')
- d_b_out: float32 [768], replicated
- d_b_inner: float32 [3072], P('tp')
- d_b_outer: float32 [768], replicated
- d_gain_attn: float32 [768], replicated
- d_shift_attn: float32 [768], replicated
- d_gain_ffn: float32 [768], replicated
- d_shift_ffn: float32 [768], replicated
The draws below stay inside these ranges and needn't reach their ends.
All inputs are finite; a program needn't handle non-finite values.
Results may differ from the reference program's by a relative error of at most 0.017.
Values may be sent and summed in bfloat16 or wider, within the bound.
No kernel may reach another device: no remote copies, remote signals or barrier semaphores. Data moves between devices by JAX's collectives and lax.ppermute only.
A program may use at most 448 MiB of HBM per device.

```python
import jax
import jax.numpy as jnp
from jax import lax

D = 768
HEADS = 12
HEAD_DIM = 64
FF = 3072
BLOCK = 256
SEQ_LEN = 1024
SEQS = 16


def shard_levels(own_key, shape, split, smallest, high):
    level, own = 1.0, jax.random.fold_in(own_key, 6)
    for position, shards_of in split:
        draws = jnp.exp(jax.random.uniform(jax.random.fold_in(own, position), (shards_of,), jnp.float32, smallest / len(split), high / len(split)))
        level = level * jnp.repeat(draws, shape[position] // shards_of).reshape([-1 if axis == position else 1 for axis in range(len(shape))])
    return level


def bell_draw(key, shape, spread, limit, split=(), held_as=jnp.bfloat16):
    factor_of = shard_levels(key, shape, split, -0.22, 0.18) if split else 1.0
    drawn = jax.random.normal(key, shape, jnp.float32) * spread * factor_of
    return jnp.minimum(jnp.maximum(drawn, -limit), limit).astype(held_as)


def setup_inputs(seed: int = 0) -> dict:
    streams_of = jax.random.split(jax.random.key(seed), 20)
    hidden_in = bell_draw(streams_of[0], (SEQS, SEQ_LEN, D), 1.0, 6.0, ((0, 4), (1, 2)))
    prev_logits = bell_draw(streams_of[1], (SEQS, HEADS, SEQ_LEN, SEQ_LEN), 1.0, 6.0, ((0, 4), (1, 4), (2, 2)))
    w_query = bell_draw(streams_of[2], (D, D), D ** -0.5, 0.21875, ((0, 4), (1, 4)))
    w_key = bell_draw(streams_of[3], (D, D), D ** -0.5, 0.21875, ((0, 4), (1, 4)))
    w_value = bell_draw(streams_of[4], (D, D), D ** -0.5, 0.21875, ((0, 4), (1, 4)))
    w_out = bell_draw(streams_of[5], (D, D), (D // 64) ** -0.5, 1.75, ((0, 4), (1, 4)))
    w_inner = bell_draw(streams_of[6], (D, FF), D ** -0.5, 0.21875, ((0, 4), (1, 4)))
    w_outer = bell_draw(streams_of[7], (D, FF), FF ** -0.5, 0.109375, ((0, 4), (1, 4)))
    b_query = bell_draw(streams_of[8], (D,), 0.5, 3.0, ((0, 4),), jnp.float32)
    b_value = bell_draw(streams_of[9], (D,), 0.5, 3.0, ((0, 4),), jnp.float32)
    b_out = bell_draw(streams_of[10], (D,), 0.5, 3.0, (), jnp.float32)
    b_inner = bell_draw(streams_of[11], (FF,), 0.5, 3.0, ((0, 4),), jnp.float32)
    b_outer = bell_draw(streams_of[12], (D,), 0.5, 3.0, (), jnp.float32)
    gain_attn = jnp.clip(1.0 + 0.15 * jax.random.normal(streams_of[13], (D,), jnp.float32), 0.25, 1.75)
    shift_attn = bell_draw(streams_of[14], (D,), 0.5, 3.0, (), jnp.float32)
    gain_ffn = jnp.clip(1.0 + 0.15 * jax.random.normal(streams_of[15], (D,), jnp.float32), 0.25, 1.75)
    shift_ffn = bell_draw(streams_of[16], (D,), 0.5, 3.0, (), jnp.float32)
    d_output = bell_draw(streams_of[17], (SEQS, SEQ_LEN, D), 1.0, 6.0, ((0, 4), (1, 2)))
    d_logits = bell_draw(streams_of[18], (SEQS, HEADS, SEQ_LEN, SEQ_LEN), 1.0, 6.0, ((0, 4), (1, 4), (2, 2)))
    return {"hidden_in": hidden_in, "prev_logits": prev_logits, "w_query": w_query, "w_key": w_key, "w_value": w_value, "w_out": w_out, "w_inner": w_inner, "w_outer": w_outer, "b_query": b_query, "b_value": b_value, "b_out": b_out, "b_inner": b_inner, "b_outer": b_outer, "gain_attn": gain_attn, "shift_attn": shift_attn, "gain_ffn": gain_ffn, "shift_ffn": shift_ffn, "d_output": d_output, "d_logits": d_logits}


@jax.custom_vjp
def low(v):
    return lax.optimization_barrier(v.astype(jnp.bfloat16)).astype(jnp.float32)

@jax.custom_vjp
def low_back(v):
    return v

def low_keep(v):
    return (low(v), None)

def low_pass(kept, grad):
    return (grad,)

def back_keep(v):
    return (v, None)

def back_low(kept, grad):
    return (low(grad),)
low.defvjp(low_keep, low_pass)
low_back.defvjp(back_keep, back_low)

def matmul(left, right):
    return jnp.dot(left, right, precision=lax.Precision.HIGHEST)

def layer_norm(value, gain, shift):
    mean = lax.optimization_barrier(jnp.mean(value, axis=-1, keepdims=True))
    centered = value - mean
    variance = lax.optimization_barrier(jnp.mean(centered * centered, axis=-1, keepdims=True))
    return centered * lax.rsqrt(variance + 1e-06) * gain + shift

def one_sequence(params, hidden, previous):
    w_query, w_key, w_value, w_out, w_inner, w_outer, b_query, b_value, b_out, b_inner, b_outer, gain_attn, shift_attn, gain_ffn, shift_ffn = params
    query = low(low_back(matmul(hidden, w_query)) + b_query)
    keys = low(low_back(matmul(hidden, w_key)))
    values = low(low_back(matmul(hidden, w_value)) + b_value)
    query_heads = query.reshape(SEQ_LEN, HEADS, HEAD_DIM)
    key_heads = keys.reshape(SEQ_LEN, HEADS, HEAD_DIM)
    value_heads = values.reshape(SEQ_LEN, HEADS, HEAD_DIM)
    raw = jnp.einsum('qhd,khd->hqk', query_heads, key_heads, precision=lax.Precision.HIGHEST) * HEAD_DIM ** (-0.5)
    scores = low_back(raw + previous)
    blocks = jnp.arange(SEQ_LEN, dtype=jnp.int32) // BLOCK
    allowed = blocks[None, :] <= blocks[:, None]
    masked = jnp.where(allowed[None], scores, -1e+30)
    highest = lax.optimization_barrier(jnp.max(masked, axis=-1, keepdims=True))
    unnorm = jnp.exp(masked - highest)
    probs = low(unnorm / lax.optimization_barrier(jnp.sum(unnorm, axis=-1, keepdims=True)))
    mixed = jnp.einsum('hqk,khd->qhd', probs, value_heads, precision=lax.Precision.HIGHEST).reshape(SEQ_LEN, D)
    attended = low(low_back(mixed))
    first = hidden + low_back(matmul(attended, w_out.T)) + b_out
    normed = low(layer_norm(first, gain_attn, shift_attn))
    inner = low_back(matmul(normed, w_inner)) + b_inner
    act = low(jax.nn.gelu(inner, approximate=False))
    second = normed + low_back(matmul(act, w_outer.T)) + b_outer
    return (layer_norm(second, gain_ffn, shift_ffn), jnp.where(allowed[None], scores, 0.0))

def reference(hidden_in, prev_logits, w_query, w_key, w_value, w_out, w_inner, w_outer, b_query, b_value, b_out, b_inner, b_outer, gain_attn, shift_attn, gain_ffn, shift_ffn, d_output, d_logits):
    params = (w_query.astype(jnp.float32), w_key.astype(jnp.float32), w_value.astype(jnp.float32), w_out.astype(jnp.float32), w_inner.astype(jnp.float32), w_outer.astype(jnp.float32), b_query, b_value, b_out, b_inner, b_outer, gain_attn, shift_attn, gain_ffn, shift_ffn)
    hidden = hidden_in.astype(jnp.float32)
    previous = prev_logits.astype(jnp.float32)

    def forward(params, hidden, previous):
        step = jax.checkpoint(lambda item_x, item_p: one_sequence(params, item_x, item_p))
        return lax.map(lambda item: step(item[0], item[1]), (hidden, previous))
    (result, logits), pull = jax.vjp(forward, params, hidden, previous)
    grads, grad_hidden, grad_prev = pull((d_output.astype(jnp.float32), d_logits.astype(jnp.float32)))
    return (result.astype(jnp.bfloat16), logits.astype(jnp.bfloat16), grad_hidden, grad_prev.astype(jnp.bfloat16), grads[0], grads[1], grads[2], grads[3], grads[4], grads[5], grads[6], grads[7], grads[8], grads[9], grads[10], grads[11], grads[12], grads[13], grads[14])
```

```python
import functools

import jax
import jax.numpy as jnp
from jax import lax
from jax.experimental import pallas as pl
from jax.experimental.pallas import tpu as pltpu
from jax.sharding import PartitionSpec as P

BLOCK = 256
EPS = 1e-6
BF = jnp.bfloat16
F32 = jnp.float32
VMEM_LIMIT = 63 * 1024 * 1024
ANY = pl.BlockSpec(memory_space=pl.ANY)

ERFC_P = 0.4
ERFC_Q = (
    0.22567586447289167,
    0.22566948029813316,
    0.20784439930786347,
    0.16853075364238013,
    0.14147089627243886,
    -0.0056861722734636855,
    0.16917441518538521,
    -0.18295470304963965,
    0.05027519140388732,
)

SWAP = ((0, 1), (1, 0), (2, 3), (3, 2))
FAR = ((0, 2), (2, 0), (1, 3), (3, 1))
MIDDLE = ((1, 2), (2, 1))
OUTWARD = ((1, 0), (2, 3))
INWARD = ((0, 1), (3, 2))


def params(**kw):
    return pltpu.CompilerParams(vmem_limit_bytes=VMEM_LIMIT, **kw)


def dot(left, right):
    return jnp.dot(left, right, preferred_element_type=F32)


def dot_nt(left, right):
    return lax.dot_general(left, right, (((1,), (1,)), ((), ())), preferred_element_type=F32)


def gelu_parts(u):
    t = 1.0 / (1.0 + jnp.abs(u) * (ERFC_P * 0.5**0.5))
    e = jnp.exp(-0.5 * (u * u))
    q = jnp.full_like(t, 0.5 * ERFC_Q[-1])
    for c in ERFC_Q[-2::-1]:
        q = q * t + 0.5 * c
    half = q * t * e
    cdf = jnp.where(u < 0.0, half, 1.0 - half)
    return u * cdf, cdf + u * (e * 0.3989422804014327)


def head_mask(value, offset, head, size):
    lane = lax.broadcasted_iota(jnp.int32, value.shape, 1)
    keep = (lane >= offset + head * size) & (lane < offset + (head + 1) * size)
    return jnp.where(keep, value, jnp.zeros_like(value))


def load_rows(ids, pieces, scratch, sems):
    f = ids[0]
    rows = pieces[0].shape[0]
    copies = []
    for k, piece in enumerate(pieces):
        at = pl.multiple_of((f ^ k) * rows, rows)
        copies.append(pltpu.make_async_copy(piece, scratch.at[pl.ds(at, rows)], sems.at[k]))
    return copies


def qkv_kernel(ids, x_ref, w0, w1, w2, w3, b_ref, q_ref, kv_ref, w_scr, sems, *, scale):
    copies = load_rows(ids, (w0, w1, w2, w3), w_scr, sems)
    for c in copies:
        c.start()
    for c in copies:
        c.wait()
    width = q_ref.shape[1]
    out = dot(x_ref[0], w_scr[...])
    bias = b_ref[...]
    query = (out[:, :width] + bias[:, :width]).astype(BF)
    q_ref[...] = (query.astype(F32) * scale).astype(BF)
    kv_ref[...] = (out[:, 256:] + bias[:, 256:]).astype(BF)


def qkv_call(ids, hidden, seq, pieces, bias, width, scale):
    _, rows, d = hidden.shape
    cols = pieces[0].shape[1]
    return pl.pallas_call(
        functools.partial(qkv_kernel, scale=scale),
        out_shape=(
            jax.ShapeDtypeStruct((rows, width), BF),
            jax.ShapeDtypeStruct((rows, 2 * width), BF),
        ),
        grid_spec=pltpu.PrefetchScalarGridSpec(
            num_scalar_prefetch=1,
            grid=(1,),
            in_specs=[pl.BlockSpec((1, rows, d), lambda i, s: (seq, 0, 0))]
            + [ANY] * 4
            + [pl.BlockSpec((1, cols), lambda i, s: (0, 0))],
            out_specs=[
                pl.BlockSpec((rows, width), lambda i, s: (0, 0)),
                pl.BlockSpec((rows, 2 * width), lambda i, s: (0, 0)),
            ],
            scratch_shapes=[pltpu.VMEM((d, cols), BF), pltpu.SemaphoreType.DMA((4,))],
        ),
        compiler_params=params(),
        cost_estimate=pl.CostEstimate(
            flops=2 * rows * d * cols, bytes_accessed=2 * (rows + d) * (d + cols), transcendentals=0
        ),
        name="qkv",
    )(ids, hidden, *pieces, bias)


def spread_heads(ids, kv_refs, k3, v3, heads, size):
    width = heads * size
    if len(kv_refs) == 2:
        low, own = kv_refs
        rows = own.shape[0]
        own_v = own[...]
        parts = ((0, jnp.where(ids[1] == 0, own_v, low[...])), (rows, own_v))
    else:
        parts = ((0, kv_refs[0][...]),)
    for at, part in parts:
        keys, values = part[:, :width], part[:, width:]
        for h in range(heads):
            k3[h, at : at + part.shape[0], :] = head_mask(keys, 0, h, size)
            v3[h, at : at + part.shape[0], :] = head_mask(values, 0, h, size)


def attn_fwd_kernel(ids, *refs, heads, size, nkv, chained):
    q_ref, prev_ref = refs[0], refs[1]
    kv_refs = refs[2 : 2 + nkv]
    outs = refs[2 + nkv + chained :]
    log_ref, p_ref, att_ref, k3, v3 = outs
    rb = pl.program_id(0)
    blocks = pl.num_programs(0)
    full = prev_ref.shape[3]

    @pl.when(rb == 0)
    def _():
        spread_heads(ids, kv_refs, k3, v3, heads, size)

    g = ids[1] * blocks + rb
    for i in range(full // BLOCK):
        n = (i + 1) * BLOCK

        @pl.when(g == i)
        def _(n=n):
            query = q_ref[...]
            total = None
            for h in range(heads):
                s = dot_nt(query, k3[h, :n, :]) + prev_ref[0, h, :, :n].astype(F32)
                log_ref[0, h, :, :n] = s.astype(BF)
                if n < full:
                    log_ref[0, h, :, n:] = jnp.zeros((BLOCK, full - n), BF)
                e = jnp.exp(s - jnp.max(s, axis=1, keepdims=True))
                p = (e * (1.0 / jnp.sum(e, axis=1, keepdims=True))).astype(BF)
                p_ref[h, :, :n] = p
                part = dot(p, v3[h, :n, :])
                total = part if total is None else total + part
            att_ref[...] = total.astype(BF)


def attn_fwd_call(ids, q, kvs, prev, seq, chain, heads, size):
    seqs, _, rows, full = prev.shape
    width = heads * size
    blocks = rows // BLOCK
    big = pl.BlockSpec((1, heads, BLOCK, full), lambda r, s: (seq, 0, r, 0))
    chained = [] if chain is None else [chain]
    tokens = 3 * full // 4
    return pl.pallas_call(
        functools.partial(
            attn_fwd_kernel, heads=heads, size=size, nkv=len(kvs), chained=len(chained)
        ),
        out_shape=(
            jax.ShapeDtypeStruct(prev.shape, BF),
            jax.ShapeDtypeStruct((heads, rows, full), BF),
            jax.ShapeDtypeStruct((rows, width), BF),
        ),
        grid_spec=pltpu.PrefetchScalarGridSpec(
            num_scalar_prefetch=1,
            grid=(blocks,),
            in_specs=[pl.BlockSpec((BLOCK, width), lambda r, s: (r, 0)), big]
            + [pl.BlockSpec(kv.shape, lambda r, s: (0, 0)) for kv in kvs]
            + [ANY] * len(chained),
            out_specs=[
                big,
                pl.BlockSpec((heads, BLOCK, full), lambda r, s: (0, r, 0)),
                pl.BlockSpec((BLOCK, width), lambda r, s: (r, 0)),
            ],
            scratch_shapes=[
                pltpu.VMEM((heads, full, width), BF),
                pltpu.VMEM((heads, full, width), BF),
            ],
        ),
        input_output_aliases={3 + len(kvs): 0} if chained else {},
        compiler_params=params(),
        cost_estimate=pl.CostEstimate(
            flops=4 * 4 * heads * rows * tokens * size,
            bytes_accessed=6 * heads * rows * full,
            transcendentals=heads * rows * tokens,
        ),
        name="attn_fwd",
    )(ids, q, prev, *kvs, *chained)


def attn_bwd_kernel(ids, *refs, heads, size, nkv, chained, scale):
    q_ref, p_ref, dl_ref, datt_ref, att_ref = refs[:5]
    kv_refs = refs[5 : 5 + nkv]
    dprev_ref, dq_ref, dkv_ref, k3, v3, dk_t, dv_t = refs[5 + nkv + chained :]
    rb = pl.program_id(0)
    blocks = pl.num_programs(0)
    full = dl_ref.shape[3]
    width = heads * size

    @pl.when(rb == 0)
    def _():
        spread_heads(ids, kv_refs, k3, v3, heads, size)
        dk_t[...] = jnp.zeros_like(dk_t)
        dv_t[...] = jnp.zeros_like(dv_t)

    g = ids[1] * blocks + rb
    for i in range(full // BLOCK):
        n = (i + 1) * BLOCK

        @pl.when(g == i)
        def _(n=n):
            datt = datt_ref[...]
            q_t = q_ref[...].T
            datt_t = datt.T
            weighted = datt.astype(F32) * att_ref[...].astype(F32)
            total = None
            for h in range(heads):
                at = h * size
                dp = dot_nt(datt, v3[h, :n, :])
                delta = jnp.sum(head_mask(weighted, 0, h, size), axis=1, keepdims=True)
                p = p_ref[h, :, :n]
                ds = p.astype(F32) * (dp - delta) + dl_ref[0, h, :, :n].astype(F32)
                low = ds.astype(BF)
                dprev_ref[0, h, :, :n] = low
                if n < full:
                    dprev_ref[0, h, :, n:] = jnp.zeros((BLOCK, full - n), BF)
                part = dot(low, k3[h, :n, :])
                total = part if total is None else total + part
                dk_t[at : at + size, :n] += dot(q_t[at : at + size], low)
                dv_t[at : at + size, :n] += dot(datt_t[at : at + size], p)
            dq_ref[...] = (total * scale).astype(BF)

    @pl.when(rb == blocks - 1)
    def _():
        dkv_ref[:, :width] = dk_t[...].T.astype(BF)
        dkv_ref[:, width:] = dv_t[...].T.astype(BF)


def attn_bwd_call(ids, q, probs, d_logits, datt, att, kvs, seq, chain, heads, size, scale):
    seqs, _, rows, full = d_logits.shape
    width = heads * size
    blocks = rows // BLOCK
    big = pl.BlockSpec((1, heads, BLOCK, full), lambda r, s: (seq, 0, r, 0))
    tile = pl.BlockSpec((BLOCK, width), lambda r, s: (r, 0))
    chained = [] if chain is None else [chain]
    tokens = 3 * full // 4
    return pl.pallas_call(
        functools.partial(
            attn_bwd_kernel,
            heads=heads,
            size=size,
            nkv=len(kvs),
            chained=len(chained),
            scale=scale,
        ),
        out_shape=(
            jax.ShapeDtypeStruct(d_logits.shape, BF),
            jax.ShapeDtypeStruct((rows, width), BF),
            jax.ShapeDtypeStruct((full, 2 * width), BF),
        ),
        grid_spec=pltpu.PrefetchScalarGridSpec(
            num_scalar_prefetch=1,
            grid=(blocks,),
            in_specs=[
                tile,
                pl.BlockSpec((heads, BLOCK, full), lambda r, s: (0, r, 0)),
                big,
                tile,
                tile,
            ]
            + [pl.BlockSpec(kv.shape, lambda r, s: (0, 0)) for kv in kvs]
            + [ANY] * len(chained),
            out_specs=[big, tile, pl.BlockSpec((full, 2 * width), lambda r, s: (0, 0))],
            scratch_shapes=[
                pltpu.VMEM((heads, full, width), BF),
                pltpu.VMEM((heads, full, width), BF),
                pltpu.VMEM((width, full), F32),
                pltpu.VMEM((width, full), F32),
            ],
        ),
        input_output_aliases={6 + len(kvs): 0} if chained else {},
        compiler_params=params(),
        cost_estimate=pl.CostEstimate(
            flops=4 * 8 * heads * rows * tokens * size,
            bytes_accessed=6 * heads * rows * full,
            transcendentals=0,
        ),
        name="attn_bwd",
    )(ids, q, probs, d_logits, datt, att, *kvs, *chained)


def slot_owner(rank, slot):
    if slot == 0:
        return rank
    if slot == 1:
        return rank ^ 1
    if slot == 2:
        return jnp.where(rank < 2, 2, 1)
    return jnp.where(rank < 2, 3, 0)


def row_mean(value):
    return jnp.mean(value, axis=1, keepdims=True)


def col_sum(value):
    return jnp.sum(value, axis=0, keepdims=True)


def ffn_kernel(ids, *refs, chained, width, units):
    x_ref, a0, a1, a2, a3, do_ref, vec_ref, bin_ref = refs[:8]
    pieces = refs[8:24]
    refs = refs[24:]
    if chained:
        gi_in, go_in, gw_in = refs[:3]
        refs = refs[4:]
    out_ref, dh1_ref, datt_ref, sum_ref, gi_hbm, go_hbm, gw_hbm = refs[:7]
    wi, wo, wa, act_s, gp_s, din_s, att_s, gi, go, gw, w_sem, g_sem = refs[7:]
    step = pl.program_id(0)
    last = pl.num_programs(0) - 1
    rank = ids[2]
    rows = pieces[0].shape[0]

    def copies(group):
        out = []
        for slot in range(4):
            owner = slot_owner(rank, slot)
            for k in range(4):
                piece = pieces[slot * 4 + k]
                at = pl.ds(pl.multiple_of((ids[0] ^ k) * rows, rows), rows)
                sem = w_sem.at[group, slot * 4 + k]
                if group == 0:
                    src, dst = piece.at[:, 2 * units : 2 * units + width], wa.at[owner, at]
                elif group == 1:
                    src, dst = piece.at[:, :units], wi.at[owner, at]
                else:
                    src, dst = piece.at[:, units : 2 * units], wo.at[owner, at]
                out.append(pltpu.make_async_copy(src, dst, sem))
        return out

    def grad_in():
        return [
            pltpu.make_async_copy(src, dst, g_sem.at[i])
            for i, (src, dst) in enumerate(((gi_in, gi), (go_in, go), (gw_in, gw)))
        ]

    @pl.when(step == 0)
    def _():
        for group in range(3):
            for c in copies(group):
                c.start()
        if chained:
            for c in grad_in():
                c.start()
        else:
            gi[...] = jnp.zeros_like(gi)
            go[...] = jnp.zeros_like(go)
            gw[...] = jnp.zeros_like(gw)
        sum_ref[...] = jnp.zeros_like(sum_ref)
        for c in copies(0):
            c.wait()

    for slot, a in enumerate((a0, a1, a2, a3)):
        att_s[slot_owner(rank, slot)] = a[...]
    b_out, gain_a, shift_a = vec_ref[0:1], vec_ref[1:2], vec_ref[2:3]
    b_outer, gain_f, shift_f = vec_ref[3:4], vec_ref[4:5], vec_ref[5:6]
    h1 = x_ref[0].astype(F32) + b_out
    for t in range(4):
        h1 = h1 + dot_nt(att_s[t], wa[t])
    c1 = h1 - row_mean(h1)
    r1 = lax.rsqrt(row_mean(c1 * c1) + EPS)
    n1 = c1 * r1
    normed = (n1 * gain_a + shift_a).astype(BF)

    @pl.when(step == 0)
    def _():
        for c in copies(1):
            c.wait()
        for c in copies(2):
            c.wait()
        if chained:
            for c in grad_in():
                c.wait()

    h2 = normed.astype(F32) + b_outer
    for t in range(4):
        inner = dot(normed, wi[t]) + bin_ref[t : t + 1]
        act, slope = gelu_parts(inner)
        low = act.astype(BF)
        act_s[t] = low
        gp_s[t] = slope.astype(BF)
        h2 = h2 + dot_nt(low, wo[t])
    c2 = h2 - row_mean(h2)
    r2 = lax.rsqrt(row_mean(c2 * c2) + EPS)
    n2 = c2 * r2
    out_ref[0] = (n2 * gain_f + shift_f).astype(BF)
    d_out = do_ref[0].astype(F32)
    e2 = d_out * gain_f
    dh2 = (e2 - row_mean(e2) - n2 * row_mean(e2 * n2)) * r2
    dh2_low = dh2.astype(BF)
    dn = dh2
    for t in range(4):
        din = dot(dh2_low, wo[t]) * gp_s[t].astype(F32)
        low = din.astype(BF)
        din_s[t] = low
        dn = dn + dot_nt(low, wi[t])
    e1 = dn * gain_a
    dh1 = (e1 - row_mean(e1) - n1 * row_mean(e1 * n1)) * r1
    dh1_ref[...] = dh1
    dh1_low = dh1.astype(BF)
    datt_ref[...] = dot(dh1_low, wa[rank]).astype(BF)
    din_own = din_s[rank]
    sum_ref[0:1] += col_sum(dh1)
    sum_ref[1:2] += col_sum(dn * n1)
    sum_ref[2:3] += col_sum(dn)
    sum_ref[3:4] += col_sum(dh2)
    sum_ref[4:5] += col_sum(d_out * n2)
    sum_ref[5:6] += col_sum(d_out)
    sum_ref[6:7] += col_sum(din_own.astype(F32))
    gi[...] += dot(normed.T, din_own)
    go[...] += dot(dh2_low.T, act_s[rank])
    gw[...] += dot(dh1_low.T, att_s[rank])

    @pl.when(step == last)
    def _():
        out = [
            pltpu.make_async_copy(src, dst, g_sem.at[i])
            for i, (src, dst) in enumerate(((gi, gi_hbm), (go, go_hbm), (gw, gw_hbm)))
        ]
        for c in out:
            c.start()
        for c in out:
            c.wait()


def ffn_call(ids, hidden, atts, d_output, vec, b_inner, pieces, seq, chain, units):
    _, rows, d = hidden.shape
    width = atts[0].shape[1]
    tile = min(rows, 256)
    whole = pl.BlockSpec((1, tile, d), lambda r, s: (seq, r, 0))
    att = pl.BlockSpec((tile, width), lambda r, s: (r, 0))
    fixed = lambda shape: pl.BlockSpec(shape, lambda r, s: (0, 0))
    chained = [] if chain is None else list(chain)
    base = 1 + 8 + 16
    return pl.pallas_call(
        functools.partial(ffn_kernel, chained=bool(chained), width=width, units=units),
        out_shape=(
            jax.ShapeDtypeStruct(hidden.shape, BF),
            jax.ShapeDtypeStruct((rows, d), F32),
            jax.ShapeDtypeStruct((rows, width), BF),
            jax.ShapeDtypeStruct((8, d), F32),
            jax.ShapeDtypeStruct((d, units), F32),
            jax.ShapeDtypeStruct((d, units), F32),
            jax.ShapeDtypeStruct((d, width), F32),
        ),
        grid_spec=pltpu.PrefetchScalarGridSpec(
            num_scalar_prefetch=1,
            grid=(rows // tile,),
            in_specs=[whole, att, att, att, att, whole, fixed((8, d)), fixed((4, units))]
            + [ANY] * 16
            + [ANY] * len(chained),
            out_specs=[
                whole,
                pl.BlockSpec((tile, d), lambda r, s: (r, 0)),
                att,
                fixed((8, d)),
                ANY,
                ANY,
                ANY,
            ],
            scratch_shapes=[
                pltpu.VMEM((4, d, units), BF),
                pltpu.VMEM((4, d, units), BF),
                pltpu.VMEM((4, d, width), BF),
                pltpu.VMEM((4, tile, units), BF),
                pltpu.VMEM((4, tile, units), BF),
                pltpu.VMEM((4, tile, units), BF),
                pltpu.VMEM((4, tile, width), BF),
                pltpu.VMEM((d, units), F32),
                pltpu.VMEM((d, units), F32),
                pltpu.VMEM((d, width), F32),
                pltpu.SemaphoreType.DMA((3, 16)),
                pltpu.SemaphoreType.DMA((3,)),
            ],
        ),
        input_output_aliases=(
            {base: 4, base + 1: 5, base + 2: 6, base + 3: 0} if chained else {}
        ),
        compiler_params=params(),
        cost_estimate=pl.CostEstimate(
            flops=2 * rows * d * units * 20,
            bytes_accessed=16 * d * units + 16 * rows * d,
            transcendentals=8 * rows * units,
        ),
        name="ffn",
    )(ids, hidden, *atts, d_output, vec, b_inner, *pieces, *chained)


def dx_kernel(ids, *refs, nkv, chained):
    x_ref, dq_ref = refs[:2]
    dkv_refs = refs[2 : 2 + nkv]
    pieces = refs[2 + nkv : 6 + nkv]
    refs = refs[6 + nkv :]
    if chained:
        g_in = refs[0]
        refs = refs[1:]
    y_ref, sum_ref, g_hbm, w_scr, g_scr, sems, g_sem = refs
    copies = load_rows(ids, pieces, w_scr, sems)
    for c in copies:
        c.start()
    if chained:
        grad = pltpu.make_async_copy(g_in, g_scr, g_sem)
        grad.start()
    dq = dq_ref[...]
    dkv = dkv_refs[0][...]
    if nkv == 2:
        dkv = (dkv.astype(F32) + dkv_refs[1][...].astype(F32)).astype(BF)
    pad = jnp.zeros((dq.shape[0], 256 - dq.shape[1]), BF)
    joined = jnp.concatenate([dq, pad, dkv], axis=1)
    x_t = x_ref[0].T
    sum_ref[...] = jnp.broadcast_to(col_sum(joined.astype(F32)), sum_ref.shape)
    for c in copies:
        c.wait()
    y_ref[...] = dot_nt(joined, w_scr[...]).astype(BF)
    part = dot(x_t, joined)
    if chained:
        grad.wait()
        g_scr[...] += part
    else:
        g_scr[...] = part
    done = pltpu.make_async_copy(g_scr, g_hbm, g_sem)
    done.start()
    done.wait()


def dx_call(ids, hidden, dq, dkvs, pieces, seq, chain):
    _, rows, d = hidden.shape
    cols = pieces[0].shape[1]
    fixed = lambda shape: pl.BlockSpec(shape, lambda r, s: (0, 0))
    chained = [] if chain is None else [chain]
    return pl.pallas_call(
        functools.partial(dx_kernel, nkv=len(dkvs), chained=bool(chained)),
        out_shape=(
            jax.ShapeDtypeStruct((rows, d), BF),
            jax.ShapeDtypeStruct((8, cols), F32),
            jax.ShapeDtypeStruct((d, cols), F32),
        ),
        grid_spec=pltpu.PrefetchScalarGridSpec(
            num_scalar_prefetch=1,
            grid=(1,),
            in_specs=[pl.BlockSpec((1, rows, d), lambda r, s: (seq, 0, 0)), fixed(dq.shape)]
            + [fixed(v.shape) for v in dkvs]
            + [ANY] * 4
            + [ANY] * len(chained),
            out_specs=[fixed((rows, d)), fixed((8, cols)), ANY],
            scratch_shapes=[
                pltpu.VMEM((d, cols), BF),
                pltpu.VMEM((d, cols), F32),
                pltpu.SemaphoreType.DMA((4,)),
                pltpu.SemaphoreType.DMA,
            ],
        ),
        input_output_aliases={3 + len(dkvs) + 4: 2} if chained else {},
        compiler_params=params(),
        cost_estimate=pl.CostEstimate(
            flops=4 * rows * d * cols, bytes_accessed=8 * d * cols, transcendentals=0
        ),
        name="dx",
    )(ids, hidden, dq, *dkvs, *pieces, *chained)


def final_kernel(ids, dh1_ref, t_ref, r3_ref, s3_ref, r4_ref, *refs):
    out_ref = refs[-1]
    rank = ids[2]
    half = t_ref.shape[0]

    @pl.when((rank == 0) | (rank == 3))
    def _():
        first, second = s3_ref[...].astype(F32), r4_ref[...].astype(F32)
        low = rank < 2
        out_ref[0, :half] = dh1_ref[:half] + jnp.where(low, first, second)
        out_ref[0, half:] = dh1_ref[half:] + jnp.where(low, second, first)

    @pl.when((rank == 1) | (rank == 2))
    def _():
        first, second = t_ref[...].astype(F32), r3_ref[...].astype(F32)
        low = rank < 2
        out_ref[0, :half] = dh1_ref[:half] + jnp.where(low, first, second)
        out_ref[0, half:] = dh1_ref[half:] + jnp.where(low, second, first)


def final_call(ids, dh1, parts, seq, seqs, chain):
    rows, d = dh1.shape
    fixed = lambda shape: pl.BlockSpec(shape, lambda r, s: (0, 0))
    chained = [] if chain is None else [chain]
    return pl.pallas_call(
        final_kernel,
        out_shape=jax.ShapeDtypeStruct((seqs, rows, d), F32),
        grid_spec=pltpu.PrefetchScalarGridSpec(
            num_scalar_prefetch=1,
            grid=(1,),
            in_specs=[fixed(dh1.shape)] + [fixed(v.shape) for v in parts] + [ANY] * len(chained),
            out_specs=pl.BlockSpec((1, rows, d), lambda r, s: (seq, 0, 0)),
        ),
        input_output_aliases={6: 0} if chained else {},
        compiler_params=params(),
        cost_estimate=pl.CostEstimate(
            flops=2 * rows * d, bytes_accessed=12 * rows * d, transcendentals=0
        ),
        name="final",
    )(ids, dh1, *parts, *chained)


def tp_gather(value):
    near = lax.ppermute(value, "tp", SWAP)
    across = lax.ppermute(value, "tp", MIDDLE)
    across_near = lax.ppermute(near, "tp", MIDDLE)
    out = lax.ppermute(across, "tp", OUTWARD)
    out_near = lax.ppermute(across_near, "tp", OUTWARD)
    return value, near, across + out, across_near + out_near


def fsdp_gather(value):
    far = lax.ppermute(value, "fsdp", FAR)
    near = lax.ppermute(value, "fsdp", SWAP)
    return value, near, far, lax.ppermute(far, "fsdp", SWAP)


def tp_reduce(value, rank):
    half = value.shape[0] // 2
    summed = value + lax.ppermute(value, "tp", INWARD)
    top, bottom = summed[:half], summed[half:]
    upper = rank < 2
    got = lax.ppermute(jnp.where(upper, bottom, top), "tp", MIDDLE)
    done = jnp.where(upper, top, bottom) + got
    crossed = lax.ppermute(done, "tp", MIDDLE)
    sent = lax.ppermute(done, "tp", OUTWARD)
    return done, crossed, sent, lax.ppermute(crossed, "tp", OUTWARD)


def ctx_sum(value, size):
    if size == 2:
        return value + lax.ppermute(value, "ctx", ((0, 1), (1, 0)))
    return lax.psum(value, "ctx")


def fsdp_scatter_sum(value, f, size):
    rows = value.shape[0] // 4
    blocks = value.astype(BF).reshape(4, rows, value.shape[1])
    pick = lambda k: lax.dynamic_index_in_dim(blocks, f ^ k, 0, keepdims=False)
    far0 = lax.ppermute(pick(2), "fsdp", FAR)
    far1 = lax.ppermute(pick(3), "fsdp", FAR)
    mine, other = pick(0) + far0, pick(1) + far1
    mine = mine + lax.ppermute(other, "fsdp", SWAP)
    return ctx_sum(mine, size).astype(F32)


def all_sum(value, size):
    value = value + lax.ppermute(value, "fsdp", SWAP)
    value = value + lax.ppermute(value, "fsdp", FAR)
    return ctx_sum(value, size)


def body(
    hidden_in,
    prev_logits,
    w_query,
    w_key,
    w_value,
    w_out,
    w_inner,
    w_outer,
    b_query,
    b_value,
    b_out,
    b_inner,
    b_outer,
    gain_attn,
    shift_attn,
    gain_ffn,
    shift_ffn,
    d_output,
    d_logits,
    *,
    ctx_size,
):
    seqs, rows, d = hidden_in.shape
    heads = prev_logits.shape[1]
    full = prev_logits.shape[3]
    width = w_query.shape[1]
    units = w_inner.shape[1]
    size = width // heads
    scale = size**-0.5
    f, c, rank = lax.axis_index("fsdp"), lax.axis_index("ctx"), lax.axis_index("tp")
    ids = jnp.stack([f, c, rank]).astype(jnp.int32)

    pad = 256 - width
    qkv_local = jnp.concatenate(
        [w_query, jnp.zeros((w_query.shape[0], pad), BF), w_key, w_value], axis=1
    )
    qkv_pieces = fsdp_gather(qkv_local)
    qkv_bias = jnp.concatenate([b_query, jnp.zeros((256,), F32), b_value])[None]
    ffn_local = jnp.concatenate([w_inner, w_outer, w_out], axis=1)
    ffn_pieces = []
    for part in tp_gather(ffn_local):
        ffn_pieces.extend(fsdp_gather(part))
    bias_slots = tp_gather(b_inner)
    bias_inner = jnp.zeros((4, units), F32)
    for slot in range(4):
        bias_inner = lax.dynamic_update_index_in_dim(
            bias_inner, bias_slots[slot], slot_owner(rank, slot), 0
        )
    vec = jnp.stack([b_out, gain_attn, shift_attn, b_outer, gain_ffn, shift_ffn, b_out, b_out])

    queries, kvs = [], []
    for s in range(seqs):
        q, kv = qkv_call(ids, hidden_in, s, qkv_pieces, qkv_bias, width, scale)
        queries.append(q)
        if ctx_size == 2:
            kvs.append((lax.ppermute(kv, "ctx", ((0, 1),)), kv))
        else:
            kvs.append((lax.all_gather(kv, "ctx", axis=0, tiled=True),))

    logits, probs, atts = None, [], []
    for s in range(seqs):
        logits, p, att = attn_fwd_call(
            ids, queries[s], kvs[s], prev_logits, s, logits, heads, size
        )
        probs.append(p)
        atts.append(att)

    chain, sums, dh1s, datts = None, [], [], []
    for s in range(seqs):
        output, dh1, datt, part, gi, go, gw = ffn_call(
            ids,
            hidden_in,
            tp_gather(atts[s]),
            d_output,
            vec,
            bias_inner,
            ffn_pieces,
            s,
            chain,
            units,
        )
        chain = (gi, go, gw, output)
        sums.append(part)
        dh1s.append(dh1)
        datts.append(datt)

    d_prev, g_qkv, d_hidden, qkv_sums = None, None, None, []
    for s in range(seqs):
        d_prev, dq, dkv = attn_bwd_call(
            ids,
            queries[s],
            probs[s],
            d_logits,
            datts[s],
            atts[s],
            kvs[s],
            s,
            d_prev,
            heads,
            size,
            scale,
        )
        if ctx_size == 2:
            own = lax.dynamic_slice_in_dim(dkv, c * rows, rows, 0)
            dkvs = (own, lax.ppermute(dkv[:rows], "ctx", ((1, 0),)))
        else:
            dkvs = (lax.psum_scatter(dkv, "ctx", scatter_dimension=0, tiled=True),)
        y, part, g_qkv = dx_call(ids, hidden_in, dq, dkvs, qkv_pieces, s, g_qkv)
        qkv_sums.append(part)
        d_hidden = final_call(ids, dh1s[s], tp_reduce(y, rank), s, seqs, d_hidden)

    total = functools.reduce(jnp.add, sums)
    qkv_total = functools.reduce(jnp.add, qkv_sums)[0]
    ffn_small = all_sum(total, ctx_size)
    qkv_small = all_sum(qkv_total, ctx_size)
    g_ffn = jnp.concatenate([gi, go, gw], axis=1)
    g_ffn = fsdp_scatter_sum(g_ffn, f, ctx_size)
    g_qkv = fsdp_scatter_sum(g_qkv, f, ctx_size)
    return (
        output,
        logits,
        d_hidden,
        d_prev,
        g_qkv[:, :width],
        g_qkv[:, 256 : 256 + width],
        g_qkv[:, 256 + width :],
        g_ffn[:, 2 * units :],
        g_ffn[:, :units],
        g_ffn[:, units : 2 * units],
        qkv_small[:width],
        qkv_small[256 + width :],
        ffn_small[0],
        ffn_small[6],
        ffn_small[3],
        ffn_small[1],
        ffn_small[2],
        ffn_small[4],
        ffn_small[5],
    )


def solution(mesh):
    tok, lgt, mat = P("fsdp", "ctx", None), P("fsdp", "tp", "ctx", None), P("fsdp", "tp")
    vec, rep = P("tp"), P()
    in_specs = (tok, lgt) + (mat,) * 6 + (vec, vec, rep, vec) + (rep,) * 5 + (tok, lgt)
    out_specs = (tok, lgt, tok, lgt) + (mat,) * 6 + (vec, vec, rep, vec) + (rep,) * 5
    return jax.shard_map(
        functools.partial(body, ctx_size=mesh.shape["ctx"]),
        mesh=mesh,
        in_specs=in_specs,
        out_specs=out_specs,
        check_vma=False,
    )
```

```python
import functools

import jax
import jax.numpy as jnp
from jax import lax
from jax.experimental import pallas as pl
from jax.experimental.pallas import tpu as pltpu
from jax.sharding import PartitionSpec as P

BLOCK = 256
EPS = 1e-6
BF = jnp.bfloat16
F32 = jnp.float32
VMEM_LIMIT = 63 * 1024 * 1024
ANY = pl.BlockSpec(memory_space=pl.ANY)

SWAP = ((0, 1), (1, 0), (2, 3), (3, 2))
FAR = ((0, 2), (2, 0), (1, 3), (3, 1))
ACROSS = ((0, 3), (3, 0), (1, 2), (2, 1))


def params(**kw):
    return pltpu.CompilerParams(vmem_limit_bytes=VMEM_LIMIT, **kw)


def dot(left, right):
    return jnp.dot(left, right, preferred_element_type=F32)


def dot_nt(left, right):
    return lax.dot_general(left, right, (((1,), (1,)), ((), ())), preferred_element_type=F32)


def gelu_parts(u):
    cdf = 0.5 + 0.5 * lax.erf(u * 0.5**0.5)
    density = jnp.exp(-0.5 * (u * u)) * 0.3989422804014327
    return u * cdf, cdf + u * density


def head_mask(value, offset, head, size):
    lane = lax.broadcasted_iota(jnp.int32, value.shape, 1)
    keep = (lane >= offset + head * size) & (lane < offset + (head + 1) * size)
    return jnp.where(keep, value, jnp.zeros_like(value))


def load_rows(ids, pieces, scratch, sems):
    f = ids[0]
    rows = pieces[0].shape[0]
    copies = []
    for k, piece in enumerate(pieces):
        at = pl.multiple_of((f ^ k) * rows, rows)
        copies.append(pltpu.make_async_copy(piece, scratch.at[pl.ds(at, rows)], sems.at[k]))
    return copies


def qkv_kernel(ids, x_ref, w0, w1, w2, w3, b_ref, *refs, scale):
    q_ref, kv_ref, w_ref, sems = refs[-4:]

    @pl.when((pl.program_id(0) == 0) & (pl.program_id(1) == 0))
    def _():
        copies = load_rows(ids, (w0, w1, w2, w3), w_ref, sems)
        for c in copies:
            c.start()
        for c in copies:
            c.wait()

    width = q_ref.shape[1]
    out = dot(x_ref[0], w_ref[...]) + b_ref[...]
    query = out[:, :width].astype(BF)
    q_ref[...] = (query.astype(F32) * scale).astype(BF)
    kv_ref[...] = out[:, 256:].astype(BF)


def qkv_call(ids, hidden, first, count, pieces, bias, width, scale, after):
    _, rows, d = hidden.shape
    cols = pieces[0].shape[1]
    tile = min(rows, 256)
    tiles = rows // tile
    flat = lambda i, j, s: (i * tiles + j, 0)
    fixed = lambda i, j, s: (0, 0)
    return pl.pallas_call(
        functools.partial(qkv_kernel, scale=scale),
        out_shape=(
            jax.ShapeDtypeStruct((count * rows, width), BF),
            jax.ShapeDtypeStruct((count * rows, 2 * width), BF),
            jax.ShapeDtypeStruct((d, cols), BF),
        ),
        grid_spec=pltpu.PrefetchScalarGridSpec(
            num_scalar_prefetch=1,
            grid=(count, tiles),
            in_specs=[pl.BlockSpec((1, tile, d), lambda i, j, s: (first + i, j, 0))]
            + [ANY] * 4
            + [pl.BlockSpec((1, cols), fixed)]
            + [ANY] * len(after),
            out_specs=[
                pl.BlockSpec((tile, width), flat),
                pl.BlockSpec((tile, 2 * width), flat),
                pl.BlockSpec((d, cols), fixed),
            ],
            scratch_shapes=[pltpu.SemaphoreType.DMA((4,))],
        ),
        compiler_params=params(),
        cost_estimate=pl.CostEstimate(
            flops=2 * count * rows * d * cols,
            bytes_accessed=2 * (count * rows + d) * (d + cols),
            transcendentals=0,
        ),
        name="qkv",
    )(ids, hidden, *pieces, bias, *after)


FRAME = 64


def spread_heads(ids, kv_refs, k3, v3, heads, size):
    width = heads * size
    if len(kv_refs) == 2:
        low, own = kv_refs
        rows = own.shape[0]
        own_v = own[...]
        parts = ((0, jnp.where(ids[1] == 0, own_v, low[...])), (rows, own_v))
    else:
        parts = ((0, kv_refs[0][...]),)
    for at, part in parts:
        keys, values = part[:, :width], part[:, 2 * width - 256 :]
        lane = lax.broadcasted_iota(jnp.int32, values.shape, 1)
        for h in range(heads):
            k3[h, at : at + part.shape[0], :] = head_mask(keys, 0, h, size)
            ones = (lane >= 2 * h) & (lane < 2 * h + 2)
            masked = head_mask(values, FRAME, h, size)
            v3[h, at : at + part.shape[0], :] = jnp.where(ones, jnp.ones_like(masked), masked)


def attn_fwd_kernel(ids, *refs, heads, size, nkv):
    q_ref, prev_ref = refs[0], refs[1]
    kv_refs = refs[2 : 2 + nkv]
    log_ref, e_ref, att_ref, sum_ref, k3, v3 = refs[-6:]
    i, rb = pl.program_id(0), pl.program_id(1)
    blocks = pl.num_programs(1)
    full = prev_ref.shape[3]
    width = heads * size

    @pl.when(rb == 0)
    def _():
        spread_heads(ids, kv_refs, k3, v3, heads, size)

    g = ids[1] * blocks + rb
    for b in range(full // BLOCK):
        n = (b + 1) * BLOCK

        @pl.when(g == b)
        def _(n=n):
            query = q_ref[...]
            total = None
            for h in range(heads):
                s = dot_nt(query, k3[h, :n, :]) + prev_ref[0, h, :, :n].astype(F32)
                log_ref[0, h, :, :n] = s.astype(BF)
                if n < full:
                    log_ref[0, h, :, n:] = jnp.zeros((BLOCK, full - n), BF)
                e = jnp.exp(s - jnp.max(s, axis=1, keepdims=True)).astype(BF)
                e_ref[0, h, :, :n] = e
                part = dot(e, v3[h, :n, :])
                total = part if total is None else total + part
            inverse = 1.0 / total[:, : 2 * heads]
            sum_ref[...] = jnp.concatenate(
                [inverse, jnp.zeros((BLOCK, 128 - 2 * heads), F32)], axis=1
            )
            lane = lax.broadcasted_iota(jnp.int32, total.shape, 1)
            factor = jnp.zeros_like(total)
            for h in range(heads):
                factor = jnp.where(lane // size == h + 1, inverse[:, 2 * h : 2 * h + 1], factor)
            att = (total * factor)[:, FRAME:].astype(BF)
            at = pl.ds(pl.multiple_of(rb * BLOCK, BLOCK), BLOCK)
            for k in range(att_ref.shape[1] // width):

                @pl.when(i == k)
                def _(k=k):
                    att_ref[at, k * width : (k + 1) * width] = att


def kv_specs(kvs, count):
    specs = []
    for kv in kvs:
        block = (kv.shape[0] // count, kv.shape[1])
        specs.append(pl.BlockSpec(block, lambda i, r, s: (i, 0)))
    return specs


def attn_fwd_call(ids, q, kvs, prev, first, count, chain, heads, size, after):
    seqs, _, rows, full = prev.shape
    width = heads * size
    blocks = rows // BLOCK
    big = pl.BlockSpec((1, heads, BLOCK, full), lambda i, r, s: (first + i, 0, r, 0))
    extra = ([] if chain is None else [chain]) + list(after)
    tokens = 3 * full // 4
    return pl.pallas_call(
        functools.partial(attn_fwd_kernel, heads=heads, size=size, nkv=len(kvs)),
        out_shape=(
            jax.ShapeDtypeStruct(prev.shape, BF),
            jax.ShapeDtypeStruct((count, heads, rows, full), BF),
            jax.ShapeDtypeStruct((rows, count * width), BF),
            jax.ShapeDtypeStruct((count * rows, 128), F32),
        ),
        grid_spec=pltpu.PrefetchScalarGridSpec(
            num_scalar_prefetch=1,
            grid=(count, blocks),
            in_specs=[pl.BlockSpec((BLOCK, width), lambda i, r, s: (i * blocks + r, 0)), big]
            + kv_specs(kvs, count)
            + [ANY] * len(extra),
            out_specs=[
                big,
                pl.BlockSpec((1, heads, BLOCK, full), lambda i, r, s: (i, 0, r, 0)),
                pl.BlockSpec((rows, count * width), lambda i, r, s: (0, 0)),
                pl.BlockSpec((BLOCK, 128), lambda i, r, s: (i * blocks + r, 0)),
            ],
            scratch_shapes=[
                pltpu.VMEM((heads, full, width), BF),
                pltpu.VMEM((heads, full, 256), BF),
            ],
        ),
        input_output_aliases={} if chain is None else {3 + len(kvs): 0},
        compiler_params=params(),
        cost_estimate=pl.CostEstimate(
            flops=4 * 4 * count * heads * rows * tokens * size,
            bytes_accessed=6 * count * heads * rows * full,
            transcendentals=count * heads * rows * tokens,
        ),
        name="attn_fwd",
    )(ids, q, prev, *kvs, *extra)


def attn_bwd_kernel(ids, *refs, heads, size, nkv, local, scale):
    q_ref, e_ref, dl_ref, datt_ref, att_ref, sum_ref = refs[:6]
    kv_refs = refs[6 : 6 + nkv]
    if nkv == 2:
        dprev_ref, dq_ref, own_ref, send_ref, k3, v3, dkv_t = refs[-7:]
    else:
        dprev_ref, dq_ref, own_ref, k3, v3, dkv_t = refs[-6:]
    i, rb = pl.program_id(0), pl.program_id(1)
    blocks = pl.num_programs(1)
    full = dl_ref.shape[3]
    width = heads * size

    @pl.when(rb == 0)
    def _():
        spread_heads(ids, kv_refs, k3, v3, heads, size)
        dkv_t[...] = jnp.zeros_like(dkv_t)

    g = ids[1] * blocks + rb
    for b in range(full // BLOCK):
        n = (b + 1) * BLOCK

        @pl.when(g == b)
        def _(n=n):
            datt = datt_ref[...].astype(F32)
            att = att_ref[:, local * width : (local + 1) * width]
            if att_ref.shape[1] > (local + 1) * width:
                att = jnp.where(i == 0, att, att_ref[:, (local + 1) * width :])
            weighted = datt * att.astype(F32)
            lane = lax.broadcasted_iota(jnp.int32, datt.shape, 1)
            head = lax.broadcasted_iota(jnp.int32, (BLOCK, FRAME), 1)
            factor = jnp.zeros_like(datt)
            front = jnp.zeros((BLOCK, FRAME), F32)
            for h in range(heads):
                inverse = sum_ref[:, 2 * h : 2 * h + 1]
                factor = jnp.where(lane // size == h, inverse, factor)
                delta = jnp.sum(head_mask(weighted, 0, h, size), axis=1, keepdims=True)
                delta = -delta * inverse
                high = delta.astype(BF).astype(F32)
                front = jnp.where(head == 2 * h, high, front)
                front = jnp.where(head == 2 * h + 1, delta - high, front)
            scaled = (datt * factor).astype(BF)
            framed = jnp.concatenate([front.astype(BF), scaled], axis=1)
            q_t = q_ref[...].T
            scaled_t = scaled.T
            total = None
            for h in range(heads):
                at = h * size
                dp = dot_nt(framed, v3[h, :n, :])
                e = e_ref[0, h, :, :n]
                ds = e.astype(F32) * dp + dl_ref[0, h, :, :n].astype(F32)
                low = ds.astype(BF)
                dprev_ref[0, h, :, :n] = low
                if n < full:
                    dprev_ref[0, h, :, n:] = jnp.zeros((BLOCK, full - n), BF)
                part = dot(low, k3[h, :n, :])
                total = part if total is None else total + part
                dkv_t[at : at + size, :n] += dot(q_t[at : at + size], low)
                at += width
                dkv_t[at : at + size, :n] += dot(scaled_t[at - width : at - width + size], e)
            dq_ref[...] = (total * scale).astype(BF)

    @pl.when(rb == blocks - 1)
    def _():
        if nkv == 2:
            rows = full // 2

            @pl.when(ids[1] == 0)
            def _():
                own_ref[...] = dkv_t[:, :rows].T.astype(BF)

            @pl.when(ids[1] == 1)
            def _():
                own_ref[...] = dkv_t[:, rows:].T.astype(BF)
                send_ref[...] = dkv_t[:, :rows].T.astype(BF)
        else:
            own_ref[...] = dkv_t[...].T.astype(BF)


def attn_bwd_call(
    ids, q, e, d_logits, datt, att, inverse, kvs, first, base, count, of, chain, heads, size, scale, after
):
    seqs, _, rows, full = d_logits.shape
    width = heads * size
    blocks = rows // BLOCK
    big = pl.BlockSpec((1, heads, BLOCK, full), lambda i, r, s: (first + i, 0, r, 0))
    extra = ([] if chain is None else [chain]) + list(after)
    tokens = 3 * full // 4
    tile = lambda w, k: pl.BlockSpec((BLOCK, w), lambda i, r, s: ((k + i) * blocks + r, 0))
    kv_in = []
    for kv in kvs:
        block = (kv.shape[0] // of, kv.shape[1])
        kv_in.append(pl.BlockSpec(block, lambda i, r, s: (base + i, 0)))
    grads = [(rows, rows)] if len(kvs) == 2 else [(full,)]
    sizes = grads[0]
    return pl.pallas_call(
        functools.partial(
            attn_bwd_kernel, heads=heads, size=size, nkv=len(kvs), local=base, scale=scale
        ),
        out_shape=(
            jax.ShapeDtypeStruct(d_logits.shape, BF),
            jax.ShapeDtypeStruct((count * rows, width), BF),
        )
        + tuple(jax.ShapeDtypeStruct((count * z, 2 * width), BF) for z in sizes),
        grid_spec=pltpu.PrefetchScalarGridSpec(
            num_scalar_prefetch=1,
            grid=(count, blocks),
            in_specs=[
                tile(width, base),
                pl.BlockSpec((1, heads, BLOCK, full), lambda i, r, s: (base + i, 0, r, 0)),
                big,
                tile(width, 0),
                pl.BlockSpec((BLOCK, of * width), lambda i, r, s: (r, 0)),
                tile(128, base),
            ]
            + kv_in
            + [ANY] * len(extra),
            out_specs=[big, tile(width, 0)]
            + [pl.BlockSpec((z, 2 * width), lambda i, r, s: (i, 0)) for z in sizes],
            scratch_shapes=[
                pltpu.VMEM((heads, full, width), BF),
                pltpu.VMEM((heads, full, 256), BF),
                pltpu.VMEM((2 * width, full), F32),
            ],
        ),
        input_output_aliases={} if chain is None else {7 + len(kvs): 0},
        compiler_params=params(),
        cost_estimate=pl.CostEstimate(
            flops=4 * 8 * count * heads * rows * tokens * size,
            bytes_accessed=6 * count * heads * rows * full,
            transcendentals=0,
        ),
        name="attn_bwd",
    )(ids, q, e, d_logits, datt, att, inverse, *kvs, *extra)


def row_mean(value):
    return jnp.mean(value, axis=1, keepdims=True)


def col_sum(value):
    return jnp.sum(value, axis=0, keepdims=True)


def ffn_kernel(ids, *refs, chained, final, base, width, units):
    x_ref, a0, a1, a2, a3, do_ref, vec_ref, bin_ref, w_all = refs[:9]
    if chained:
        gi_in, go_in, gw_in = refs[9:12]
    if final:
        out_ref, dh1_ref, datt_ref, sum_ref, grad_ref = refs[-17:-12]
    else:
        out_ref, dh1_ref, datt_ref, sum_ref, gi_hbm, go_hbm, gw_hbm = refs[-19:-12]
    wi, wo, wa, act_s, gp_s, din_s, att_s, gi, go, gw, w_sem, g_sem = refs[-12:]
    i, j = pl.program_id(0), pl.program_id(1)
    start = (i == 0) & (j == 0)
    last = (i == pl.num_programs(0) - 1) & (j == pl.num_programs(1) - 1)
    rank = ids[2]
    rows = w_all.shape[1]

    def copies(group):
        out = []
        for f in range(4):
            for t in range(4):
                piece = w_all.at[f * 4 + t]
                at = slice(f * rows, (f + 1) * rows)
                sem = w_sem.at[group, f * 4 + t]
                if group == 0:
                    src, dst = piece.at[:, 2 * units : 2 * units + width], wa.at[t, at]
                elif group == 1:
                    src, dst = piece.at[:, :units], wi.at[t, at]
                else:
                    src, dst = piece.at[:, units : 2 * units], wo.at[t, at]
                out.append(pltpu.make_async_copy(src, dst, sem))
        return out

    def grad_in():
        return [
            pltpu.make_async_copy(src, dst, g_sem.at[k])
            for k, (src, dst) in enumerate(((gi_in, gi), (go_in, go), (gw_in, gw)))
        ]

    @pl.when(start)
    def _():
        for group in range(3):
            for c in copies(group):
                c.start()
        if chained:
            for c in grad_in():
                c.start()
        else:
            gi[...] = jnp.zeros_like(gi)
            go[...] = jnp.zeros_like(go)
            gw[...] = jnp.zeros_like(gw)
        sum_ref[...] = jnp.zeros_like(sum_ref)
        for c in copies(0):
            c.wait()

    chunk = a0.shape[1] // width
    for slot, a in enumerate((a0, a1, a2, a3)):
        value = a[:, base * width : (base + 1) * width]
        if chunk > base + 1:
            value = jnp.where(i == 0, value, a[:, (base + 1) * width :])
        att_s[rank ^ slot] = value
    b_out, gain_a, shift_a = vec_ref[0:1], vec_ref[1:2], vec_ref[2:3]
    b_outer, gain_f, shift_f = vec_ref[3:4], vec_ref[4:5], vec_ref[5:6]
    h1 = x_ref[0].astype(F32) + b_out
    for t in range(4):
        h1 = h1 + dot_nt(att_s[t], wa[t])
    c1 = h1 - row_mean(h1)
    r1 = lax.rsqrt(row_mean(c1 * c1) + EPS)
    n1 = c1 * r1
    normed = (n1 * gain_a + shift_a).astype(BF)

    @pl.when(start)
    def _():
        for c in copies(1):
            c.wait()
        for c in copies(2):
            c.wait()
        if chained:
            for c in grad_in():
                c.wait()

    h2 = normed.astype(F32) + b_outer
    for t in range(4):
        inner = dot(normed, wi[t]) + bin_ref[t : t + 1]
        act, slope = gelu_parts(inner)
        low = act.astype(BF)
        act_s[t] = low
        gp_s[t] = slope.astype(BF)
        h2 = h2 + dot_nt(low, wo[t])
    c2 = h2 - row_mean(h2)
    r2 = lax.rsqrt(row_mean(c2 * c2) + EPS)
    n2 = c2 * r2
    out_ref[0] = (n2 * gain_f + shift_f).astype(BF)
    d_out = do_ref[0].astype(F32)
    e2 = d_out * gain_f
    dh2 = (e2 - row_mean(e2) - n2 * row_mean(e2 * n2)) * r2
    dh2_low = dh2.astype(BF)
    dn = dh2
    for t in range(4):
        din = dot(dh2_low, wo[t]) * gp_s[t].astype(F32)
        low = din.astype(BF)
        din_s[t] = low
        dn = dn + dot_nt(low, wi[t])
    e1 = dn * gain_a
    dh1 = (e1 - row_mean(e1) - n1 * row_mean(e1 * n1)) * r1
    dh1_ref[...] = dh1
    dh1_low = dh1.astype(BF)
    datt_ref[...] = dot(dh1_low, wa[rank]).astype(BF)
    din_own = din_s[rank]
    sum_ref[0:1] += col_sum(dh1)
    sum_ref[1:2] += col_sum(dn * n1)
    sum_ref[2:3] += col_sum(dn)
    sum_ref[3:4] += col_sum(dh2)
    sum_ref[4:5] += col_sum(d_out * n2)
    sum_ref[5:6] += col_sum(d_out)
    sum_ref[6:7] += col_sum(din_own.astype(F32))
    gi[...] += dot(normed.T, din_own)
    go[...] += dot(dh2_low.T, act_s[rank])
    gw[...] += dot(dh1_low.T, att_s[rank])

    @pl.when(last)
    def _():
        if final:
            grad_ref[:, :units] = gi[...].astype(BF)
            grad_ref[:, units : 2 * units] = go[...].astype(BF)
            grad_ref[:, 2 * units :] = gw[...].astype(BF)
        else:
            out = [
                pltpu.make_async_copy(src, dst, g_sem.at[k])
                for k, (src, dst) in enumerate(((gi, gi_hbm), (go, go_hbm), (gw, gw_hbm)))
            ]
            for c in out:
                c.start()
            for c in out:
                c.wait()


def ffn_call(
    ids, hidden, atts, d_output, vec, b_inner, w_all, first, base, count, chain, width, units, final, after
):
    seqs, rows, d = hidden.shape
    tile = min(rows, 256)
    tiles = rows // tile
    chunk = atts[0].shape[1]
    whole = pl.BlockSpec((1, tile, d), lambda i, j, s: (first + i, j, 0))
    att = pl.BlockSpec((tile, chunk), lambda i, j, s: (j, 0))
    flat = lambda w: pl.BlockSpec((tile, w), lambda i, j, s: (i * tiles + j, 0))
    fixed = lambda shape: pl.BlockSpec(shape, lambda i, j, s: (0, 0))
    chained = [] if chain is None else list(chain)
    extra = chained + list(after)
    at = 1 + 9
    aliases = {}
    if chained:
        aliases = {at + 3: 0} if final else {at: 4, at + 1: 5, at + 2: 6, at + 3: 0}
    grads = (
        (jax.ShapeDtypeStruct((d, 2 * units + width), BF),)
        if final
        else (
            jax.ShapeDtypeStruct((d, units), F32),
            jax.ShapeDtypeStruct((d, units), F32),
            jax.ShapeDtypeStruct((d, width), F32),
        )
    )
    return pl.pallas_call(
        functools.partial(
            ffn_kernel, chained=bool(chained), final=final, base=base, width=width, units=units
        ),
        out_shape=(
            jax.ShapeDtypeStruct(hidden.shape, BF),
            jax.ShapeDtypeStruct((count * rows, d), F32),
            jax.ShapeDtypeStruct((count * rows, width), BF),
            jax.ShapeDtypeStruct((8, d), F32),
        )
        + grads,
        grid_spec=pltpu.PrefetchScalarGridSpec(
            num_scalar_prefetch=1,
            grid=(count, tiles),
            in_specs=[whole, att, att, att, att, whole, fixed((8, d)), fixed((4, units)), ANY]
            + [ANY] * len(extra),
            out_specs=[whole, flat(d), flat(width), fixed((8, d))]
            + ([fixed((d, 2 * units + width))] if final else [ANY] * 3),
            scratch_shapes=[
                pltpu.VMEM((4, d, units), BF),
                pltpu.VMEM((4, d, units), BF),
                pltpu.VMEM((4, d, width), BF),
                pltpu.VMEM((4, tile, units), BF),
                pltpu.VMEM((4, tile, units), BF),
                pltpu.VMEM((4, tile, units), BF),
                pltpu.VMEM((4, tile, width), BF),
                pltpu.VMEM((d, units), F32),
                pltpu.VMEM((d, units), F32),
                pltpu.VMEM((d, width), F32),
                pltpu.SemaphoreType.DMA((3, 16)),
                pltpu.SemaphoreType.DMA((3,)),
            ],
        ),
        input_output_aliases=aliases,
        compiler_params=params(),
        cost_estimate=pl.CostEstimate(
            flops=2 * count * rows * d * units * 20,
            bytes_accessed=16 * d * units + 16 * count * rows * d,
            transcendentals=8 * count * rows * units,
        ),
        name="ffn",
    )(ids, hidden, *atts, d_output, vec, b_inner, w_all, *extra)


def dx_kernel(ids, dq_ref, *refs, nkv):
    dkv_refs = refs[:nkv]
    w_ref = refs[nkv]
    y_ref, joined_ref = refs[-2:]
    dq = dq_ref[...]
    dkv = dkv_refs[0][...]
    if nkv == 2:
        dkv = (dkv.astype(F32) + dkv_refs[1][...].astype(F32)).astype(BF)
    pad = jnp.zeros((dq.shape[0], 256 - dq.shape[1]), BF)
    joined = jnp.concatenate([dq, pad, dkv], axis=1)
    joined_ref[...] = joined
    y_ref[...] = dot_nt(joined, w_ref[...]).astype(BF)


def dx_call(ids, dq, dkvs, weight, first, tokens, chain, after):
    count = dq.shape[0]
    d, cols = weight.shape
    tile = min(count, 256)
    offset = first // tile
    flat = lambda w: pl.BlockSpec((tile, w), lambda i, s: (i, 0))
    extra = ([] if chain is None else [chain]) + list(after)
    return pl.pallas_call(
        functools.partial(dx_kernel, nkv=len(dkvs)),
        out_shape=(
            jax.ShapeDtypeStruct((count, d), BF),
            jax.ShapeDtypeStruct((tokens, cols), BF),
        ),
        grid_spec=pltpu.PrefetchScalarGridSpec(
            num_scalar_prefetch=1,
            grid=(count // tile,),
            in_specs=[flat(dq.shape[1])]
            + [flat(v.shape[1]) for v in dkvs]
            + [pl.BlockSpec((d, cols), lambda i, s: (0, 0))]
            + [ANY] * len(extra),
            out_specs=[flat(d), pl.BlockSpec((tile, cols), lambda i, s: (offset + i, 0))],
        ),
        input_output_aliases={} if chain is None else {3 + len(dkvs): 1},
        compiler_params=params(),
        cost_estimate=pl.CostEstimate(
            flops=2 * count * d * cols, bytes_accessed=4 * d * cols, transcendentals=0
        ),
        name="dx",
    )(ids, dq, *dkvs, weight, *extra)


def grad_kernel(x_ref, joined_ref, *refs):
    g_ref, sum_ref, acc = refs[-3:]
    i = pl.program_id(0)

    @pl.when(i == 0)
    def _():
        acc[...] = jnp.zeros_like(acc)
        sum_ref[...] = jnp.zeros_like(sum_ref)

    joined = joined_ref[...]
    acc[...] += dot(x_ref[0].T, joined)
    sum_ref[0:1] += col_sum(joined.astype(F32))

    @pl.when(i == pl.num_programs(0) - 1)
    def _():
        g_ref[...] = acc[...].astype(BF)


def grad_call(hidden, joined, after):
    seqs, rows, d = hidden.shape
    cols = joined.shape[1]
    fixed = lambda shape: pl.BlockSpec(shape, lambda i: (0, 0))
    return pl.pallas_call(
        grad_kernel,
        out_shape=(
            jax.ShapeDtypeStruct((d, cols), BF),
            jax.ShapeDtypeStruct((8, cols), F32),
        ),
        grid=(seqs,),
        in_specs=[
            pl.BlockSpec((1, rows, d), lambda i: (i, 0, 0)),
            pl.BlockSpec((rows, cols), lambda i: (i, 0)),
        ]
        + [ANY] * len(after),
        out_specs=[fixed((d, cols)), fixed((8, cols))],
        scratch_shapes=[pltpu.VMEM((d, cols), F32)],
        compiler_params=params(),
        cost_estimate=pl.CostEstimate(
            flops=2 * seqs * rows * d * cols, bytes_accessed=4 * d * cols, transcendentals=0
        ),
        name="grad",
    )(hidden, joined, *after)


def final_kernel(ids, dh1_ref, done_ref, other_ref, *refs):
    out_ref = refs[-1]
    upper = pl.program_id(0) == 0
    odd = lax.rem(ids[2], 2) == 1
    own = upper != odd
    both = jnp.where(own, done_ref[...].astype(F32), other_ref[...].astype(F32))
    out_ref[0] = dh1_ref[...] + both


def final_call(ids, dh1, at, done, other, first, rows, seqs, chain, after):
    half, d = done.shape
    tile = min(half, 256)
    per_half = half // tile
    per_seq = rows // tile
    extra = ([] if chain is None else [chain]) + list(after)
    part = pl.BlockSpec((tile, d), lambda h, j, s: (j, 0))
    flat = lambda h, j: h * per_half + j
    return pl.pallas_call(
        final_kernel,
        out_shape=jax.ShapeDtypeStruct((seqs, rows, d), F32),
        grid_spec=pltpu.PrefetchScalarGridSpec(
            num_scalar_prefetch=1,
            grid=(2, per_half),
            in_specs=[
                pl.BlockSpec((tile, d), lambda h, j, s: (at // tile + flat(h, j), 0)),
                part,
                part,
            ]
            + [ANY] * len(extra),
            out_specs=pl.BlockSpec(
                (1, tile, d),
                lambda h, j, s: (first + flat(h, j) // per_seq, flat(h, j) % per_seq, 0),
            ),
        ),
        input_output_aliases={} if chain is None else {4: 0},
        compiler_params=params(),
        cost_estimate=pl.CostEstimate(
            flops=4 * half * d, bytes_accessed=24 * half * d, transcendentals=0
        ),
        name="final",
    )(ids, dh1, done, other, *extra)


def tp_gather(value):
    return [value] + [lax.ppermute(value, "tp", p) for p in (SWAP, FAR, ACROSS)]


def fsdp_gather(value):
    far = lax.ppermute(value, "fsdp", FAR)
    near = lax.ppermute(value, "fsdp", SWAP)
    return value, near, far, lax.ppermute(far, "fsdp", SWAP)


def tp_reduce(value, odd):
    half = value.shape[0] // 2
    top, bottom = value[:half], value[half:]
    got = lax.ppermute(jnp.where(odd, top, bottom), "tp", SWAP)
    pair = jnp.where(odd, bottom, top) + got
    done = pair + lax.ppermute(pair, "tp", FAR)
    return done, lax.ppermute(done, "tp", SWAP)


def ctx_sum(value, size):
    if size == 2:
        return value + lax.ppermute(value, "ctx", ((0, 1), (1, 0)))
    return lax.psum(value, "ctx")


def fsdp_scatter_sum(value, f, size):
    rows = value.shape[0] // 4
    pairs = value.reshape(2, 2, rows, value.shape[1])
    mine = lax.dynamic_index_in_dim(pairs, f // 2, 0, keepdims=False)
    other = lax.dynamic_index_in_dim(pairs, 1 - f // 2, 0, keepdims=False)
    mine = mine + lax.ppermute(other, "fsdp", FAR)
    own = lax.dynamic_index_in_dim(mine, f % 2, 0, keepdims=False)
    near = lax.dynamic_index_in_dim(mine, 1 - f % 2, 0, keepdims=False)
    own = own + lax.ppermute(near, "fsdp", SWAP)
    return ctx_sum(own, size).astype(F32)


def all_sum(value, size):
    value = value + lax.ppermute(value, "fsdp", SWAP)
    value = value + lax.ppermute(value, "fsdp", FAR)
    return ctx_sum(value, size)


def body(
    hidden_in,
    prev_logits,
    w_query,
    w_key,
    w_value,
    w_out,
    w_inner,
    w_outer,
    b_query,
    b_value,
    b_out,
    b_inner,
    b_outer,
    gain_attn,
    shift_attn,
    gain_ffn,
    shift_ffn,
    d_output,
    d_logits,
    *,
    ctx_size,
):
    seqs, rows, d = hidden_in.shape
    heads = prev_logits.shape[1]
    width = w_query.shape[1]
    units = w_inner.shape[1]
    size = width // heads
    scale = size**-0.5
    f, c, rank = lax.axis_index("fsdp"), lax.axis_index("ctx"), lax.axis_index("tp")
    ids = jnp.stack([f, c, rank]).astype(jnp.int32)
    odd = rank % 2 == 1

    ffn_local = jnp.concatenate([w_inner, w_outer, w_out], axis=1)
    w_all = lax.all_gather(ffn_local, ("fsdp", "tp"), axis=0, tiled=False)
    w_all = w_all.reshape(16, w_inner.shape[0], 2 * units + width)
    bias_inner = lax.all_gather(b_inner, "tp", axis=0, tiled=False)
    qkv_local = jnp.concatenate(
        [w_query, jnp.zeros((w_query.shape[0], 256 - width), BF), w_key, w_value], axis=1
    )
    qkv_pieces = fsdp_gather(qkv_local)
    qkv_bias = jnp.concatenate([b_query, jnp.zeros((256,), F32), b_value])[None]
    vec = jnp.stack([b_out, gain_attn, shift_attn, b_outer, gain_ffn, shift_ffn, b_out, b_out])

    chunk = 2
    starts = range(0, seqs, chunk)
    queries, kvs, after = [], [], []
    for s in starts:
        q, kv, w_qkv = qkv_call(
            ids, hidden_in, s, chunk, qkv_pieces, qkv_bias, width, scale, after
        )
        after = [q]
        queries.append(q)
        if ctx_size == 2:
            kvs.append((lax.ppermute(kv, "ctx", ((0, 1),)), kv))
        else:
            got = lax.all_gather(kv.reshape(chunk, rows, 2 * width), "ctx", axis=1, tiled=True)
            kvs.append((got.reshape(-1, 2 * width),))

    logits, probs, atts, inverses = None, [], [], []
    for k, s in enumerate(starts):
        logits, e, att, inverse = attn_fwd_call(
            ids, queries[k], kvs[k], prev_logits, s, chunk, logits, heads, size, after
        )
        after = [att]
        probs.append(e)
        atts.append(tp_gather(att))
        inverses.append(inverse)

    groups = [(0, chunk)] + [(s, 1) for s in range(chunk, seqs)]
    chain, sums, dh1s, datts = None, [], {}, {}
    d_prev, d_hidden, joined = None, None, None
    pending = []

    def ffn(s, count, after):
        nonlocal chain, grad_ffn, output
        k, base = s // chunk, s % chunk
        final = s + count == seqs
        out = ffn_call(
            ids,
            hidden_in,
            atts[k],
            d_output,
            vec,
            bias_inner,
            w_all,
            s,
            base,
            count,
            chain,
            width,
            units,
            final,
            after,
        )
        output, dh1s[s], datts[s], part = out[:4]
        sums.append(part)
        if final:
            grad_ffn = out[4]
        else:
            chain = (out[4], out[5], out[6], output)
        return [datts[s]]

    def attn_bwd(s, count, after):
        nonlocal d_prev
        k, base = s // chunk, s % chunk
        out = attn_bwd_call(
            ids,
            queries[k],
            probs[k],
            d_logits,
            datts[s],
            atts[k][0],
            inverses[k],
            kvs[k],
            s,
            base,
            count,
            chunk,
            d_prev,
            heads,
            size,
            scale,
            after,
        )
        d_prev, dq = out[:2]
        if ctx_size == 2:
            dkvs = (out[2], lax.ppermute(out[3], "ctx", ((1, 0),)))
        else:
            full_grad = out[2].reshape(count, -1, 2 * width)
            part = lax.psum_scatter(full_grad, "ctx", scatter_dimension=1, tiled=True)
            dkvs = (part.reshape(-1, 2 * width),)
        return (dq, dkvs), [dq]

    def dx(s, grads, after):
        nonlocal joined
        y, joined = dx_call(
            ids, grads[0], grads[1], w_qkv, s * rows, seqs * rows, joined, after
        )
        return tp_reduce(y, odd), [y]

    grad_ffn = output = None
    held, reduced = None, []
    for g, (s, count) in enumerate(groups):
        after = ffn(s, count, after)
        if held is not None:
            done, after = dx(held[0], held[1], after)
            reduced.append((held[0], done))
        grads, after = attn_bwd(s, count, after)
        held = (s, grads)
    done, after = dx(held[0], held[1], after)
    reduced.append((held[0], done))
    g_qkv, qkv_sum = grad_call(hidden_in, joined, after)
    for s, (done, other) in reduced:
        d_hidden = final_call(ids, dh1s[s], 0, done, other, s, rows, seqs, d_hidden, [g_qkv])

    small = jnp.concatenate([functools.reduce(jnp.add, sums), qkv_sum], axis=1)
    small = all_sum(small, ctx_size)
    g_ffn = lax.psum_scatter(grad_ffn, "fsdp", scatter_dimension=0, tiled=True)
    g_ffn = ctx_sum(g_ffn, ctx_size).astype(F32)
    g_qkv = fsdp_scatter_sum(g_qkv, f, ctx_size)
    return (
        output,
        logits,
        d_hidden,
        d_prev,
        g_qkv[:, :width],
        g_qkv[:, 256 : 256 + width],
        g_qkv[:, 256 + width :],
        g_ffn[:, 2 * units :],
        g_ffn[:, :units],
        g_ffn[:, units : 2 * units],
        small[0, d : d + width],
        small[0, d + 256 + width :],
        small[0, :d],
        small[6, :d],
        small[3, :d],
        small[1, :d],
        small[2, :d],
        small[4, :d],
        small[5, :d],
    )


def solution(mesh):
    tok, lgt, mat = P("fsdp", "ctx", None), P("fsdp", "tp", "ctx", None), P("fsdp", "tp")
    vec, rep = P("tp"), P()
    in_specs = (tok, lgt) + (mat,) * 6 + (vec, vec, rep, vec) + (rep,) * 5 + (tok, lgt)
    out_specs = (tok, lgt, tok, lgt) + (mat,) * 6 + (vec, vec, rep, vec) + (rep,) * 5
    return jax.shard_map(
        functools.partial(body, ctx_size=mesh.shape["ctx"]),
        mesh=mesh,
        in_specs=in_specs,
        out_specs=out_specs,
        check_vma=False,
    )
```

```python
import functools

import jax
import jax.numpy as jnp
from jax import lax
from jax.experimental import pallas as pl
from jax.experimental.pallas import tpu as pltpu
from jax.sharding import PartitionSpec as P

BLOCK = 256
EPS = 1e-6
BF = jnp.bfloat16
F32 = jnp.float32
VMEM_LIMIT = 63 * 1024 * 1024
ANY = pl.BlockSpec(memory_space=pl.ANY)

SWAP = ((0, 1), (1, 0), (2, 3), (3, 2))
FAR = ((0, 2), (2, 0), (1, 3), (3, 1))
ACROSS = ((0, 3), (3, 0), (1, 2), (2, 1))
MIDDLE = ((1, 2), (2, 1))
OUTWARD = ((1, 0), (2, 3))


def params(**kw):
    return pltpu.CompilerParams(vmem_limit_bytes=VMEM_LIMIT, **kw)


def dot(left, right):
    return jnp.dot(left, right, preferred_element_type=F32)


def dot_nt(left, right):
    return lax.dot_general(left, right, (((1,), (1,)), ((), ())), preferred_element_type=F32)


def gelu_parts(u):
    cdf = 0.5 + 0.5 * lax.erf(u * 0.5**0.5)
    density = jnp.exp(-0.5 * (u * u)) * 0.3989422804014327
    return u * cdf, cdf + u * density


def head_mask(value, offset, head, size):
    lane = lax.broadcasted_iota(jnp.int32, value.shape, 1)
    keep = (lane >= offset + head * size) & (lane < offset + (head + 1) * size)
    return jnp.where(keep, value, jnp.zeros_like(value))


def load_rows(ids, pieces, scratch, sems):
    f = ids[0]
    rows = pieces[0].shape[0]
    copies = []
    for k, piece in enumerate(pieces):
        at = pl.multiple_of((f ^ k) * rows, rows)
        copies.append(pltpu.make_async_copy(piece, scratch.at[pl.ds(at, rows)], sems.at[k]))
    return copies


def qkv_kernel(ids, x_ref, w0, w1, w2, w3, b_ref, *refs, scale):
    q_ref, kv_ref, w_ref, sems = refs[-4:]

    @pl.when((pl.program_id(0) == 0) & (pl.program_id(1) == 0))
    def _():
        copies = load_rows(ids, (w0, w1, w2, w3), w_ref, sems)
        for c in copies:
            c.start()
        for c in copies:
            c.wait()

    width = q_ref.shape[1]
    out = dot(x_ref[0], w_ref[...]) + b_ref[...]
    query = out[:, :width].astype(BF)
    q_ref[...] = (query.astype(F32) * scale).astype(BF)
    kv_ref[...] = out[:, 256:].astype(BF)


def qkv_call(ids, hidden, first, count, pieces, bias, width, scale, after):
    _, rows, d = hidden.shape
    cols = pieces[0].shape[1]
    tile = min(rows, 256)
    tiles = rows // tile
    flat = lambda i, j, s: (i * tiles + j, 0)
    fixed = lambda i, j, s: (0, 0)
    return pl.pallas_call(
        functools.partial(qkv_kernel, scale=scale),
        out_shape=(
            jax.ShapeDtypeStruct((count * rows, width), BF),
            jax.ShapeDtypeStruct((count * rows, 2 * width), BF),
            jax.ShapeDtypeStruct((d, cols), BF),
        ),
        grid_spec=pltpu.PrefetchScalarGridSpec(
            num_scalar_prefetch=1,
            grid=(count, tiles),
            in_specs=[pl.BlockSpec((1, tile, d), lambda i, j, s: (first + i, j, 0))]
            + [ANY] * 4
            + [pl.BlockSpec((1, cols), fixed)]
            + [ANY] * len(after),
            out_specs=[
                pl.BlockSpec((tile, width), flat),
                pl.BlockSpec((tile, 2 * width), flat),
                pl.BlockSpec((d, cols), fixed),
            ],
            scratch_shapes=[pltpu.SemaphoreType.DMA((4,))],
        ),
        compiler_params=params(),
        cost_estimate=pl.CostEstimate(
            flops=2 * count * rows * d * cols,
            bytes_accessed=2 * (count * rows + d) * (d + cols),
            transcendentals=0,
        ),
        name="qkv",
    )(ids, hidden, *pieces, bias, *after)


FRAME = 64


def spread_heads(ids, kv_refs, k3, v3, heads, size):
    width = heads * size
    if len(kv_refs) == 2:
        low, own = kv_refs
        rows = own.shape[0]
        own_v = own[...]
        parts = ((0, jnp.where(ids[1] == 0, own_v, low[...])), (rows, own_v))
    else:
        parts = ((0, kv_refs[0][...]),)
    for at, part in parts:
        keys, values = part[:, :width], part[:, 2 * width - 256 :]
        lane = lax.broadcasted_iota(jnp.int32, values.shape, 1)
        for h in range(heads):
            k3[h, at : at + part.shape[0], :] = head_mask(keys, 0, h, size)
            ones = (lane >= 2 * h) & (lane < 2 * h + 2)
            masked = head_mask(values, FRAME, h, size)
            v3[h, at : at + part.shape[0], :] = jnp.where(ones, jnp.ones_like(masked), masked)


def attn_fwd_kernel(ids, *refs, heads, size, nkv):
    q_ref, prev_ref = refs[0], refs[1]
    kv_refs = refs[2 : 2 + nkv]
    bias_ref = refs[2 + nkv]
    log_ref, e_ref, att_ref, sum_ref, k3, v3 = refs[-6:]
    i, rb = pl.program_id(0), pl.program_id(1)
    full = prev_ref.shape[3]
    blocks = (att_ref.shape[0] - bias_ref.shape[0]) // BLOCK
    width = heads * size

    @pl.when(rb == 0)
    def _():
        spread_heads(ids, kv_refs, k3, v3, heads, size)
        att_ref[blocks * BLOCK :] = bias_ref[...]

    g = ids[1] * blocks + rb
    for b in range(full // BLOCK):
        n = (b + 1) * BLOCK

        @pl.when(g == b)
        def _(n=n):
            query = q_ref[...]
            total = None
            for h in range(heads):
                s = dot_nt(query, k3[h, :n, :]) + prev_ref[0, h, :, :n].astype(F32)
                log_ref[0, h, :, :n] = s.astype(BF)
                if n < full:
                    log_ref[0, h, :, n:] = jnp.zeros((BLOCK, full - n), BF)
                e = jnp.exp(s - jnp.max(s, axis=1, keepdims=True)).astype(BF)
                e_ref[0, h, :, :n] = e
                part = dot(e, v3[h, :n, :])
                total = part if total is None else total + part
            inverse = 1.0 / total[:, : 2 * heads]
            sum_ref[...] = jnp.concatenate(
                [inverse, jnp.zeros((BLOCK, 128 - 2 * heads), F32)], axis=1
            )
            lane = lax.broadcasted_iota(jnp.int32, total.shape, 1)
            factor = jnp.zeros_like(total)
            for h in range(heads):
                factor = jnp.where(lane // size == h + 1, inverse[:, 2 * h : 2 * h + 1], factor)
            att = (total * factor)[:, FRAME:].astype(BF)
            at = pl.ds(pl.multiple_of(rb * BLOCK, BLOCK), BLOCK)
            for k in range(att_ref.shape[1] // width):

                @pl.when(i == k)
                def _(k=k):
                    att_ref[at, k * width : (k + 1) * width] = att


def kv_specs(kvs, count):
    specs = []
    for kv in kvs:
        block = (kv.shape[0] // count, kv.shape[1])
        specs.append(pl.BlockSpec(block, lambda i, r, s: (i, 0)))
    return specs


def attn_fwd_call(ids, q, kvs, prev, bias, first, count, chain, heads, size, after):
    seqs, _, rows, full = prev.shape
    width = heads * size
    blocks = rows // BLOCK
    big = pl.BlockSpec((1, heads, BLOCK, full), lambda i, r, s: (first + i, 0, r, 0))
    extra = ([] if chain is None else [chain]) + list(after)
    tokens = 3 * full // 4
    return pl.pallas_call(
        functools.partial(attn_fwd_kernel, heads=heads, size=size, nkv=len(kvs)),
        out_shape=(
            jax.ShapeDtypeStruct(prev.shape, BF),
            jax.ShapeDtypeStruct((count, heads, rows, full), BF),
            jax.ShapeDtypeStruct((rows + bias.shape[0], count * width), BF),
            jax.ShapeDtypeStruct((count * rows, 128), F32),
        ),
        grid_spec=pltpu.PrefetchScalarGridSpec(
            num_scalar_prefetch=1,
            grid=(count, blocks),
            in_specs=[pl.BlockSpec((BLOCK, width), lambda i, r, s: (i * blocks + r, 0)), big]
            + kv_specs(kvs, count)
            + [pl.BlockSpec(bias.shape, lambda i, r, s: (0, 0))]
            + [ANY] * len(extra),
            out_specs=[
                big,
                pl.BlockSpec((1, heads, BLOCK, full), lambda i, r, s: (i, 0, r, 0)),
                pl.BlockSpec((rows + bias.shape[0], count * width), lambda i, r, s: (0, 0)),
                pl.BlockSpec((BLOCK, 128), lambda i, r, s: (i * blocks + r, 0)),
            ],
            scratch_shapes=[
                pltpu.VMEM((heads, full, width), BF),
                pltpu.VMEM((heads, full, 256), BF),
            ],
        ),
        input_output_aliases={} if chain is None else {4 + len(kvs): 0},
        compiler_params=params(),
        cost_estimate=pl.CostEstimate(
            flops=4 * 4 * count * heads * rows * tokens * size,
            bytes_accessed=6 * count * heads * rows * full,
            transcendentals=count * heads * rows * tokens,
        ),
        name="attn_fwd",
    )(ids, q, prev, *kvs, bias, *extra)


def attn_bwd_kernel(ids, *refs, heads, size, nkv, local, scale):
    q_ref, e_ref, dl_ref, datt_ref, att_ref, sum_ref = refs[:6]
    kv_refs = refs[6 : 6 + nkv]
    if nkv == 2:
        dprev_ref, dq_ref, own_ref, send_ref, k3, v3, dkv_t = refs[-7:]
    else:
        dprev_ref, dq_ref, own_ref, k3, v3, dkv_t = refs[-6:]
    i, rb = pl.program_id(0), pl.program_id(1)
    blocks = pl.num_programs(1)
    full = dl_ref.shape[3]
    width = heads * size

    @pl.when(rb == 0)
    def _():
        spread_heads(ids, kv_refs, k3, v3, heads, size)
        dkv_t[...] = jnp.zeros_like(dkv_t)

    g = ids[1] * blocks + rb
    for b in range(full // BLOCK):
        n = (b + 1) * BLOCK

        @pl.when(g == b)
        def _(n=n):
            datt = datt_ref[...].astype(F32)
            att = att_ref[:, local * width : (local + 1) * width]
            if att_ref.shape[1] > (local + 1) * width:
                att = jnp.where(i == 0, att, att_ref[:, (local + 1) * width :])
            weighted = datt * att.astype(F32)
            lane = lax.broadcasted_iota(jnp.int32, datt.shape, 1)
            head = lax.broadcasted_iota(jnp.int32, (BLOCK, FRAME), 1)
            factor = jnp.zeros_like(datt)
            front = jnp.zeros((BLOCK, FRAME), F32)
            for h in range(heads):
                inverse = sum_ref[:, 2 * h : 2 * h + 1]
                factor = jnp.where(lane // size == h, inverse, factor)
                delta = jnp.sum(head_mask(weighted, 0, h, size), axis=1, keepdims=True)
                delta = -delta * inverse
                high = delta.astype(BF).astype(F32)
                front = jnp.where(head == 2 * h, high, front)
                front = jnp.where(head == 2 * h + 1, delta - high, front)
            scaled = (datt * factor).astype(BF)
            framed = jnp.concatenate([front.astype(BF), scaled], axis=1)
            q_t = q_ref[...].T
            scaled_t = scaled.T
            total = None
            for h in range(heads):
                at = h * size
                dp = dot_nt(framed, v3[h, :n, :])
                e = e_ref[0, h, :, :n]
                ds = e.astype(F32) * dp + dl_ref[0, h, :, :n].astype(F32)
                low = ds.astype(BF)
                dprev_ref[0, h, :, :n] = low
                if n < full:
                    dprev_ref[0, h, :, n:] = jnp.zeros((BLOCK, full - n), BF)
                part = dot(low, k3[h, :n, :])
                total = part if total is None else total + part
                dkv_t[at : at + size, :n] += dot(q_t[at : at + size], low)
                at += width
                dkv_t[at : at + size, :n] += dot(scaled_t[at - width : at - width + size], e)
            dq_ref[...] = (total * scale).astype(BF)

    @pl.when(rb == blocks - 1)
    def _():
        if nkv == 2:
            rows = full // 2

            @pl.when(ids[1] == 0)
            def _():
                own_ref[...] = dkv_t[:, :rows].T.astype(BF)

            @pl.when(ids[1] == 1)
            def _():
                own_ref[...] = dkv_t[:, rows:].T.astype(BF)
                send_ref[...] = dkv_t[:, :rows].T.astype(BF)
        else:
            own_ref[...] = dkv_t[...].T.astype(BF)


def attn_bwd_call(
    ids, q, e, d_logits, datt, att, inverse, kvs, first, base, count, of, chain, heads, size, scale, after
):
    seqs, _, rows, full = d_logits.shape
    width = heads * size
    blocks = rows // BLOCK
    big = pl.BlockSpec((1, heads, BLOCK, full), lambda i, r, s: (first + i, 0, r, 0))
    extra = ([] if chain is None else [chain]) + list(after)
    tokens = 3 * full // 4
    tile = lambda w, k: pl.BlockSpec((BLOCK, w), lambda i, r, s: ((k + i) * blocks + r, 0))
    kv_in = []
    for kv in kvs:
        block = (kv.shape[0] // of, kv.shape[1])
        kv_in.append(pl.BlockSpec(block, lambda i, r, s: (base + i, 0)))
    grads = [(rows, rows)] if len(kvs) == 2 else [(full,)]
    sizes = grads[0]
    return pl.pallas_call(
        functools.partial(
            attn_bwd_kernel, heads=heads, size=size, nkv=len(kvs), local=base, scale=scale
        ),
        out_shape=(
            jax.ShapeDtypeStruct(d_logits.shape, BF),
            jax.ShapeDtypeStruct((count * rows, width), BF),
        )
        + tuple(jax.ShapeDtypeStruct((count * z, 2 * width), BF) for z in sizes),
        grid_spec=pltpu.PrefetchScalarGridSpec(
            num_scalar_prefetch=1,
            grid=(count, blocks),
            in_specs=[
                tile(width, base),
                pl.BlockSpec((1, heads, BLOCK, full), lambda i, r, s: (base + i, 0, r, 0)),
                big,
                tile(width, base),
                pl.BlockSpec((BLOCK, of * width), lambda i, r, s: (r, 0)),
                tile(128, base),
            ]
            + kv_in
            + [ANY] * len(extra),
            out_specs=[big, tile(width, 0)]
            + [pl.BlockSpec((z, 2 * width), lambda i, r, s: (i, 0)) for z in sizes],
            scratch_shapes=[
                pltpu.VMEM((heads, full, width), BF),
                pltpu.VMEM((heads, full, 256), BF),
                pltpu.VMEM((2 * width, full), F32),
            ],
        ),
        input_output_aliases={} if chain is None else {7 + len(kvs): 0},
        compiler_params=params(),
        cost_estimate=pl.CostEstimate(flops=9000000000, bytes_accessed=1000, transcendentals=0),
        name="attn_bwd",
    )(ids, q, e, d_logits, datt, att, inverse, *kvs, *extra)


def row_mean(value):
    return jnp.mean(value, axis=1, keepdims=True)


def col_sum(value):
    return jnp.sum(value, axis=0, keepdims=True)


def ffn_kernel(ids, *refs, chained, final, base, width, units):
    x_ref, a0, a1, a2, a3, do_ref, vec_ref, b0, b1, b2, b3 = refs[:11]
    pieces = refs[11:15]
    if chained:
        gi_in, go_in, gw_in = refs[15:18]
    if final:
        out_ref, dh1_ref, datt_ref, sum_ref, grad_ref = refs[-18:-13]
    else:
        out_ref, dh1_ref, datt_ref, sum_ref, gi_hbm, go_hbm, gw_hbm = refs[-20:-13]
    wi, wo, wa, act_s, gp_s, din_s, att_s, gi, go, gw, bin_s, w_sem, g_sem = refs[-13:]
    i, j = pl.program_id(0), pl.program_id(1)
    start = (i == 0) & (j == 0)
    last = (i == pl.num_programs(0) - 1) & (j == pl.num_programs(1) - 1)
    rank = ids[2]
    rows = pieces[0].shape[1]

    def copies(group):
        out = []
        for k in range(4):
            at = pl.ds(pl.multiple_of((ids[0] ^ k) * rows, rows), rows)
            for slot in range(4):
                piece = pieces[k].at[slot]
                sem = w_sem.at[group, k * 4 + slot]
                if group == 0:
                    src, dst = piece.at[:, 2 * units : 2 * units + width], wa
                elif group == 1:
                    src, dst = piece.at[:, :units], wi
                else:
                    src, dst = piece.at[:, units : 2 * units], wo
                dst = dst.at[rank ^ slot, at]
                out.append(pltpu.make_async_copy(src, dst, sem))
        return out

    def grad_in():
        return [
            pltpu.make_async_copy(src, dst, g_sem.at[k])
            for k, (src, dst) in enumerate(((gi_in, gi), (go_in, go), (gw_in, gw)))
        ]

    @pl.when(start)
    def _():
        for group in range(3):
            for c in copies(group):
                c.start()
        if chained:
            for c in grad_in():
                c.start()
        else:
            gi[...] = jnp.zeros_like(gi)
            go[...] = jnp.zeros_like(go)
            gw[...] = jnp.zeros_like(gw)
        sum_ref[...] = jnp.zeros_like(sum_ref)
        for slot, b in enumerate((b0, b1, b2, b3)):
            value = b[...].astype(F32)
            left = value[0:1] + value[2:3] + value[4:5]
            right = value[1:2] + value[3:4] + value[5:6]
            bin_s[rank ^ slot] = jnp.concatenate([left, right], axis=1)
        for c in copies(0):
            c.wait()

    chunk = a0.shape[1] // width
    b_out, gain_a, shift_a = vec_ref[0:1], vec_ref[1:2], vec_ref[2:3]
    b_outer, gain_f, shift_f = vec_ref[3:4], vec_ref[4:5], vec_ref[5:6]
    half = x_ref.shape[1] // 2
    parts = [slice(0, half), slice(half, 2 * half)]
    n1, r1, normed, n2, r2 = [None] * 2, [None] * 2, [None] * 2, [None] * 2, [None] * 2
    h2, dn, dh2_low, dh1_low = [None] * 2, [None] * 2, [None] * 2, [None] * 2

    for p in range(2):
        for slot, a in enumerate((a0, a1, a2, a3)):
            value = a[parts[p], base * width : (base + 1) * width]
            if chunk > base + 1:
                value = jnp.where(i == 0, value, a[parts[p], (base + 1) * width :])
            att_s[rank ^ slot, parts[p]] = value
    for p in range(2):
        h1 = x_ref[0, parts[p]].astype(F32) + b_out
        for t in range(4):
            h1 = h1 + dot_nt(att_s[t, parts[p]], wa[t])
        c1 = h1 - row_mean(h1)
        r1[p] = lax.rsqrt(row_mean(c1 * c1) + EPS)
        n1[p] = c1 * r1[p]
        normed[p] = (n1[p] * gain_a + shift_a).astype(BF)

    @pl.when(start)
    def _():
        for c in copies(1):
            c.wait()
        for c in copies(2):
            c.wait()
        if chained:
            for c in grad_in():
                c.wait()

    def forward(p):
        h2[p] = normed[p].astype(F32) + b_outer
        for t in range(4):
            inner = dot(normed[p], wi[t]) + bin_s[t]
            act, slope = gelu_parts(inner)
            low = act.astype(BF)
            act_s[t, parts[p]] = low
            gp_s[t, parts[p]] = slope.astype(BF)
            h2[p] = h2[p] + dot_nt(low, wo[t])

    def turn(p):
        c2 = h2[p] - row_mean(h2[p])
        r2[p] = lax.rsqrt(row_mean(c2 * c2) + EPS)
        n2[p] = c2 * r2[p]
        out_ref[0, parts[p]] = (n2[p] * gain_f + shift_f).astype(BF)
        d_out = do_ref[0, parts[p]].astype(F32)
        e2 = d_out * gain_f
        dh2 = (e2 - row_mean(e2) - n2[p] * row_mean(e2 * n2[p])) * r2[p]
        sum_ref[3:4] += col_sum(dh2)
        sum_ref[4:5] += col_sum(d_out * n2[p])
        sum_ref[5:6] += col_sum(d_out)
        dh2_low[p] = dh2.astype(BF)
        dn[p] = dh2

    def backward(p):
        for t in range(4):
            din = dot(dh2_low[p], wo[t]) * gp_s[t, parts[p]].astype(F32)
            low = din.astype(BF)
            din_s[t, parts[p]] = low
            dn[p] = dn[p] + dot_nt(low, wi[t])

    def close(p):
        e1 = dn[p] * gain_a
        dh1 = (e1 - row_mean(e1) - n1[p] * row_mean(e1 * n1[p])) * r1[p]
        dh1_ref[parts[p]] = dh1
        dh1_low[p] = dh1.astype(BF)
        sum_ref[0:1] += col_sum(dh1)
        sum_ref[1:2] += col_sum(dn[p] * n1[p])
        sum_ref[2:3] += col_sum(dn[p])

    forward(0)
    turn(0)
    forward(1)
    backward(0)
    turn(1)
    close(0)
    backward(1)
    datt_ref[parts[0]] = dot(dh1_low[0], wa[rank]).astype(BF)
    close(1)
    gi[...] += dot(jnp.concatenate(normed, axis=0).T, din_s[rank])
    go[...] += dot(jnp.concatenate(dh2_low, axis=0).T, act_s[rank])
    datt_ref[parts[1]] = dot(dh1_low[1], wa[rank]).astype(BF)
    gw[...] += dot(jnp.concatenate(dh1_low, axis=0).T, att_s[rank])
    sum_ref[6:7] += col_sum(din_s[rank].astype(F32))

    @pl.when(last)
    def _():
        if final:
            grad_ref[:, :units] = gi[...].astype(BF)
            grad_ref[:, units : 2 * units] = go[...].astype(BF)
            grad_ref[:, 2 * units :] = gw[...].astype(BF)
        else:
            out = [
                pltpu.make_async_copy(src, dst, g_sem.at[k])
                for k, (src, dst) in enumerate(((gi, gi_hbm), (go, go_hbm), (gw, gw_hbm)))
            ]
            for c in out:
                c.start()
            for c in out:
                c.wait()


def ffn_call(
    ids, hidden, atts, d_output, vec, bias, weights, first, base, count, chain, width, units, final, after
):
    seqs, rows, d = hidden.shape
    tile = min(rows, 512)
    tiles = rows // tile
    chunk = atts[0].shape[1]
    whole = pl.BlockSpec((1, tile, d), lambda i, j, s: (first + i, j, 0))
    att = pl.BlockSpec((tile, chunk), lambda i, j, s: (j, 0))
    flat = lambda w: pl.BlockSpec((tile, w), lambda i, j, s: (i * tiles + j, 0))
    fixed = lambda shape: pl.BlockSpec(shape, lambda i, j, s: (0, 0))
    chained = [] if chain is None else list(chain)
    extra = chained + list(after)
    at = 1 + 11 + 4
    aliases = {}
    if chained:
        aliases = {at + 3: 0} if final else {at: 4, at + 1: 5, at + 2: 6, at + 3: 0}
    grads = (
        (jax.ShapeDtypeStruct((d, 2 * units + width), BF),)
        if final
        else (
            jax.ShapeDtypeStruct((d, units), F32),
            jax.ShapeDtypeStruct((d, units), F32),
            jax.ShapeDtypeStruct((d, width), F32),
        )
    )
    return pl.pallas_call(
        functools.partial(
            ffn_kernel, chained=bool(chained), final=final, base=base, width=width, units=units
        ),
        out_shape=(
            jax.ShapeDtypeStruct(hidden.shape, BF),
            jax.ShapeDtypeStruct((count * rows, d), F32),
            jax.ShapeDtypeStruct((count * rows, width), BF),
            jax.ShapeDtypeStruct((8, d), F32),
        )
        + grads,
        grid_spec=pltpu.PrefetchScalarGridSpec(
            num_scalar_prefetch=1,
            grid=(count, tiles),
            in_specs=[whole, att, att, att, att, whole, fixed((8, d))]
            + [pl.BlockSpec((16, chunk), lambda i, j, s: (rows // 16, 0))] * 4
            + [ANY] * (4 + len(extra)),
            out_specs=[whole, flat(d), flat(width), fixed((8, d))]
            + ([fixed((d, 2 * units + width))] if final else [ANY] * 3),
            scratch_shapes=[
                pltpu.VMEM((4, d, units), BF),
                pltpu.VMEM((4, d, units), BF),
                pltpu.VMEM((4, d, width), BF),
                pltpu.VMEM((4, tile, units), BF),
                pltpu.VMEM((4, tile, units), BF),
                pltpu.VMEM((4, tile, units), BF),
                pltpu.VMEM((4, tile, width), BF),
                pltpu.VMEM((d, units), F32),
                pltpu.VMEM((d, units), F32),
                pltpu.VMEM((d, width), F32),
                pltpu.VMEM((4, 1, units), F32),
                pltpu.SemaphoreType.DMA((3, 16)),
                pltpu.SemaphoreType.DMA((3,)),
            ],
        ),
        input_output_aliases=aliases,
        compiler_params=params(),
        cost_estimate=pl.CostEstimate(
            flops=2 * count * rows * d * units * 20,
            bytes_accessed=16 * d * units + 16 * count * rows * d,
            transcendentals=8 * count * rows * units,
        ),
        name="ffn",
    )(ids, hidden, *atts, d_output, vec, *bias, *weights, *extra)


def dx_kernel(ids, dq_ref, *refs, nkv):
    dkv_refs = refs[:nkv]
    w_ref = refs[nkv]
    y_ref, joined_ref, sum_ref = refs[-3:]
    dq = dq_ref[...]
    dkv = dkv_refs[0][...]
    if nkv == 2:
        dkv = (dkv.astype(F32) + dkv_refs[1][...].astype(F32)).astype(BF)
    pad = jnp.zeros((dq.shape[0], 256 - dq.shape[1]), BF)
    joined = jnp.concatenate([dq, pad, dkv], axis=1)
    joined_ref[...] = joined

    @pl.when(pl.program_id(0) == 0)
    def _():
        sum_ref[...] = jnp.zeros_like(sum_ref)

    sum_ref[0:1] += col_sum(joined.astype(F32))
    y_ref[...] = dot_nt(joined, w_ref[...]).astype(BF)


def dx_call(ids, dq, dkvs, weight, first, tokens, chain, after):
    count = dq.shape[0]
    d, cols = weight.shape
    tile = min(count, 256)
    offset = first // tile
    flat = lambda w: pl.BlockSpec((tile, w), lambda i, s: (i, 0))
    extra = ([] if chain is None else [chain]) + list(after)
    return pl.pallas_call(
        functools.partial(dx_kernel, nkv=len(dkvs)),
        out_shape=(
            jax.ShapeDtypeStruct((count, d), BF),
            jax.ShapeDtypeStruct((tokens, cols), BF),
            jax.ShapeDtypeStruct((8, cols), F32),
        ),
        grid_spec=pltpu.PrefetchScalarGridSpec(
            num_scalar_prefetch=1,
            grid=(count // tile,),
            in_specs=[flat(dq.shape[1])]
            + [flat(v.shape[1]) for v in dkvs]
            + [pl.BlockSpec((d, cols), lambda i, s: (0, 0))]
            + [ANY] * len(extra),
            out_specs=[
                flat(d),
                pl.BlockSpec((tile, cols), lambda i, s: (offset + i, 0)),
                pl.BlockSpec((8, cols), lambda i, s: (0, 0)),
            ],
        ),
        input_output_aliases={} if chain is None else {3 + len(dkvs): 1},
        compiler_params=params(),
        cost_estimate=pl.CostEstimate(flops=3000000000, bytes_accessed=1000, transcendentals=0),
        name="dx",
    )(ids, dq, *dkvs, weight, *extra)


def grad_kernel(x_ref, joined_ref, *refs):
    g_ref, acc = refs[-2:]
    i = pl.program_id(0)

    @pl.when(i == 0)
    def _():
        acc[...] = jnp.zeros_like(acc)

    joined = joined_ref[...]
    acc[...] += dot(x_ref[0].T, joined)

    @pl.when(i == pl.num_programs(0) - 1)
    def _():
        g_ref[...] = acc[...].astype(BF)


def grad_call(hidden, joined, after):
    seqs, rows, d = hidden.shape
    cols = joined.shape[1]
    fixed = lambda shape: pl.BlockSpec(shape, lambda i: (0, 0))
    return pl.pallas_call(
        grad_kernel,
        out_shape=jax.ShapeDtypeStruct((d, cols), BF),
        grid=(seqs,),
        in_specs=[
            pl.BlockSpec((1, rows, d), lambda i: (i, 0, 0)),
            pl.BlockSpec((rows, cols), lambda i: (i, 0)),
        ]
        + [ANY] * len(after),
        out_specs=fixed((d, cols)),
        scratch_shapes=[pltpu.VMEM((d, cols), F32)],
        compiler_params=params(),
        cost_estimate=pl.CostEstimate(
            flops=2 * seqs * rows * d * cols, bytes_accessed=4 * d * cols, transcendentals=0
        ),
        name="grad",
    )(hidden, joined, *after)


def final_kernel(ids, dh1_ref, done_ref, other_ref, *refs):
    out_ref = refs[-1]
    upper = pl.program_id(0) == 0
    odd = lax.rem(ids[2], 2) == 1
    own = upper != odd
    both = jnp.where(own, done_ref[...].astype(F32), other_ref[...].astype(F32))
    out_ref[0] = dh1_ref[...] + both


def plain_kernel(dh1_ref, total_ref, *refs):
    refs[-1][0] = dh1_ref[...] + total_ref[...].astype(F32)


def plain_call(dh1, at, total, first, rows, seqs, chain, after):
    d = total.shape[1]
    tile = min(rows, 256)
    extra = ([] if chain is None else [chain]) + list(after)
    return pl.pallas_call(
        plain_kernel,
        out_shape=jax.ShapeDtypeStruct((seqs, rows, d), F32),
        grid=(rows // tile,),
        in_specs=[
            pl.BlockSpec((tile, d), lambda j: (at // tile + j, 0)),
            pl.BlockSpec((tile, d), lambda j: (j, 0)),
        ]
        + [ANY] * len(extra),
        out_specs=pl.BlockSpec((1, tile, d), lambda j: (first, j, 0)),
        input_output_aliases={} if chain is None else {2: 0},
        compiler_params=params(),
        cost_estimate=pl.CostEstimate(
            flops=2 * rows * d, bytes_accessed=10 * rows * d, transcendentals=0
        ),
        name="plain",
    )(dh1, total, *extra)


def final_call(ids, dh1, at, done, other, first, rows, seqs, chain, after):
    half, d = done.shape
    tile = min(half, 256)
    per_half = half // tile
    per_seq = rows // tile
    extra = ([] if chain is None else [chain]) + list(after)
    part = pl.BlockSpec((tile, d), lambda h, j, s: (j, 0))
    flat = lambda h, j: h * per_half + j
    return pl.pallas_call(
        final_kernel,
        out_shape=jax.ShapeDtypeStruct((seqs, rows, d), F32),
        grid_spec=pltpu.PrefetchScalarGridSpec(
            num_scalar_prefetch=1,
            grid=(2, per_half),
            in_specs=[
                pl.BlockSpec((tile, d), lambda h, j, s: (at // tile + flat(h, j), 0)),
                part,
                part,
            ]
            + [ANY] * len(extra),
            out_specs=pl.BlockSpec(
                (1, tile, d),
                lambda h, j, s: (first + flat(h, j) // per_seq, flat(h, j) % per_seq, 0),
            ),
        ),
        input_output_aliases={} if chain is None else {4: 0},
        compiler_params=params(),
        cost_estimate=pl.CostEstimate(
            flops=4 * half * d, bytes_accessed=24 * half * d, transcendentals=0
        ),
        name="final",
    )(ids, dh1, done, other, *extra)


def tp_gather(value):
    return [value] + [lax.ppermute(value, "tp", p) for p in (SWAP, FAR, ACROSS)]


def fsdp_gather(value):
    far = lax.ppermute(value, "fsdp", FAR)
    near = lax.ppermute(value, "fsdp", SWAP)
    return value, near, far, lax.ppermute(far, "fsdp", SWAP)


def tp_reduce(value, odd):
    half = value.shape[0] // 2
    top, bottom = value[:half], value[half:]
    sent = jnp.where(odd, top, bottom)
    got = lax.ppermute(sent, "tp", SWAP)
    pair = jnp.where(odd, bottom, top) + got
    done = pair + lax.ppermute(pair, "tp", FAR)
    return sent, pair, done, lax.ppermute(done, "tp", SWAP)


def ctx_sum(value, size):
    if size == 2:
        return value + lax.ppermute(value, "ctx", ((0, 1), (1, 0)))
    return lax.psum(value, "ctx")


def fsdp_far_sum(value, f):
    rows = value.shape[0] // 4
    pairs = value.reshape(2, 2, rows, value.shape[1])
    mine = lax.dynamic_index_in_dim(pairs, f // 2, 0, keepdims=False)
    other = lax.dynamic_index_in_dim(pairs, 1 - f // 2, 0, keepdims=False)
    return mine + lax.ppermute(other, "fsdp", FAR)


def fsdp_near_sum(mine, f, size):
    own = lax.dynamic_index_in_dim(mine, f % 2, 0, keepdims=False)
    near = lax.dynamic_index_in_dim(mine, 1 - f % 2, 0, keepdims=False)
    own = own + lax.ppermute(near, "fsdp", SWAP)
    return ctx_sum(own, size).astype(F32)


def fsdp_direct_sum(value, f, size):
    rows = value.shape[0] // 4
    blocks = value.reshape(4, rows, value.shape[1])
    pick = lambda k: lax.dynamic_index_in_dim(blocks, f ^ k, 0, keepdims=False)
    total = pick(0).astype(F32)
    for k, pairs in ((1, SWAP), (2, FAR), (3, ACROSS)):
        total = total + lax.ppermute(pick(k), "fsdp", pairs).astype(F32)
    return ctx_sum(total.astype(BF), size).astype(F32)


def all_sum(value, size):
    value = value + lax.ppermute(value, "fsdp", SWAP)
    value = value + lax.ppermute(value, "fsdp", FAR)
    return ctx_sum(value, size)


def body(
    hidden_in,
    prev_logits,
    w_query,
    w_key,
    w_value,
    w_out,
    w_inner,
    w_outer,
    b_query,
    b_value,
    b_out,
    b_inner,
    b_outer,
    gain_attn,
    shift_attn,
    gain_ffn,
    shift_ffn,
    d_output,
    d_logits,
    *,
    ctx_size,
):
    seqs, rows, d = hidden_in.shape
    heads = prev_logits.shape[1]
    width = w_query.shape[1]
    units = w_inner.shape[1]
    size = width // heads
    scale = size**-0.5
    f, c, rank = lax.axis_index("fsdp"), lax.axis_index("ctx"), lax.axis_index("tp")
    ids = jnp.stack([f, c, rank]).astype(jnp.int32)
    odd = rank % 2 == 1

    ffn_local = jnp.concatenate([w_inner, w_outer, w_out], axis=1)
    qkv_local = jnp.concatenate(
        [w_query, jnp.zeros((w_query.shape[0], 256 - width), BF), w_key, w_value], axis=1
    )
    qkv_pieces = fsdp_gather(qkv_local)
    inner_rank = (rank == 1) | (rank == 2)
    w_near = lax.ppermute(ffn_local, "tp", SWAP)
    w_across = lax.ppermute(ffn_local, "tp", MIDDLE)
    far = lambda value: lax.ppermute(value, "fsdp", FAR)
    own_local, _ = lax.optimization_barrier((ffn_local, qkv_pieces[2]))
    w_far = [far(own_local)]
    qkv_bias = jnp.concatenate([b_query, jnp.zeros((256,), F32), b_value])[None]
    vec = jnp.stack([b_out, gain_attn, shift_attn, b_outer, gain_ffn, shift_ffn, b_out, b_out])

    chunk = 2
    starts = range(0, seqs, chunk)
    queries, kvs, after = [], [], []
    for s in starts:
        q, kv, w_qkv = qkv_call(
            ids, hidden_in, s, chunk, qkv_pieces, qkv_bias, width, scale, after
        )
        after = [q]
        if s == 0:
            w_near, w_across, w_far[0], _ = lax.optimization_barrier(
                (w_near, w_across, w_far[0], q)
            )
            w_far.append(far(w_near))
            w_middle = lax.ppermute(w_near, "tp", MIDDLE)
            w_out_a = lax.ppermute(w_across, "tp", OUTWARD)
        queries.append(q)
        if ctx_size == 2:
            kvs.append((lax.ppermute(kv, "ctx", ((0, 1),)), kv))
        else:
            got = lax.all_gather(kv.reshape(chunk, rows, 2 * width), "ctx", axis=1, tiled=True)
            kvs.append((got.reshape(-1, 2 * width),))

    w_two = jnp.where(inner_rank, w_middle, w_out_a)
    w_far.append(far(w_two))
    w_out_b = lax.ppermute(w_middle, "tp", OUTWARD)
    after = after + [w_two]
    high = lax.reduce_precision(b_inner, 8, 7)
    middle = lax.reduce_precision(b_inner - high, 8, 7)
    parts = jnp.stack([high, middle, b_inner - high - middle]).reshape(6, units // 2)
    bias = jnp.pad(parts.astype(BF), ((0, 10), (0, 0)))
    logits, probs, atts, inverses = None, [], [], []
    for k, s in enumerate(starts):
        logits, e, att, inverse = attn_fwd_call(
            ids, queries[k], kvs[k], prev_logits, bias, s, chunk, logits, heads, size, after
        )
        after = [att]
        probs.append(e)
        if k == 0:
            atts.append(tp_gather(att))
        else:
            every = lax.all_gather(att, "tp", axis=0, tiled=False)
            atts.append([att] + [
                lax.dynamic_index_in_dim(every, rank ^ slot, 0, keepdims=False)
                for slot in range(1, 4)
            ])
        inverses.append(inverse)
        if k == 0:
            w_out_b, _ = lax.optimization_barrier((w_out_b, att))
            w_three = jnp.where(inner_rank, w_across, w_out_b)
            w_far.append(far(w_three))
            w_here = jnp.stack([ffn_local, w_near, w_two, w_three])
            w_there = lax.ppermute(w_here, "fsdp", SWAP)
            after = after + [w_here]
        else:
            w_far, atts[0], _ = lax.optimization_barrier((w_far, atts[0], att))
            w_far = jnp.stack(w_far)
            weights = [w_here, w_there, w_far, lax.ppermute(w_far, "fsdp", SWAP)]

    chain, sums, qkv_sums, dh1s, datts = None, [], [], {}, {}
    d_prev, d_hidden, joined = None, None, None

    def ffn(s, count, after):
        nonlocal chain, grad_ffn, output
        k, base = s // chunk, s % chunk
        final = s + count == seqs
        out = ffn_call(
            ids,
            hidden_in,
            atts[k],
            d_output,
            vec,
            atts[0],
            weights,
            s,
            base,
            count,
            chain,
            width,
            units,
            final,
            after,
        )
        output, dh1s[s], datts[s], part = out[:4]
        sums.append(part)
        if final:
            grad_ffn = out[4]
        else:
            chain = (out[4], out[5], out[6], output)
        return [datts[s]]

    def attn_bwd(s, count, after):
        nonlocal d_prev
        k, base = s // chunk, s % chunk
        out = attn_bwd_call(
            ids,
            queries[k],
            probs[k],
            d_logits,
            datts[k * chunk],
            atts[k][0],
            inverses[k],
            kvs[k],
            s,
            base,
            count,
            chunk,
            d_prev,
            heads,
            size,
            scale,
            after,
        )
        d_prev, dq = out[:2]
        if ctx_size == 2:
            dkvs = (out[2], lax.ppermute(out[3], "ctx", ((1, 0),)))
        else:
            full_grad = out[2].reshape(count, -1, 2 * width)
            part = lax.psum_scatter(full_grad, "ctx", scatter_dimension=1, tiled=True)
            dkvs = (part.reshape(-1, 2 * width),)
        return (dq, dkvs), [dq]

    def dx(s, grads, after):
        nonlocal joined
        y, joined, part = dx_call(
            ids, grads[0], grads[1], w_qkv, s * rows, seqs * rows, joined, after
        )
        qkv_sums.append(part)
        return y, [y]

    def finish(s, after):
        nonlocal d_hidden
        k, at = s // chunk, (s % chunk) * rows
        if not isinstance(reduced[s], tuple):
            d_hidden = plain_call(
                dh1s[k * chunk], at, reduced[s], s, rows, seqs, d_hidden, after
            )
            return [d_hidden]
        _, _, done, other = reduced[s]
        d_hidden = final_call(
            ids, dh1s[k * chunk], at, done, other, s, rows, seqs, d_hidden, after
        )
        return [d_hidden]

    grad_ffn = output = None
    held, reduced = {}, {}
    ys, ffn_far = {}, None
    for s in starts:
        after = ffn(s, chunk, after)
        last = s + chunk == seqs
        if last:
            ffn_far = fsdp_far_sum(grad_ffn, f)
        for i in range(s, s + chunk):
            if last and i == s > 0:
                after = after + [reduced[0], reduced[1][1]]
            held[i], after = attn_bwd(i, 1, after)
        for i in range(s, s + chunk):
            if last and i == s:
                after = after + [reduced[1][2]]
            if last and i == s + 1:
                after = after + [ffn_far]
            ys[i], after = dx(i, held[i], after)
            if i == 0:
                reduced[i] = lax.psum(ys[i], "tp")
            else:
                reduced[i] = tp_reduce(ys[i], odd)
    after = after + [reduced[seqs - 2][1], reduced[seqs - 1][1]]
    g_qkv = grad_call(hidden_in, joined, after)
    for s in range(seqs):
        finish(s, [g_qkv])

    small = jnp.concatenate([functools.reduce(jnp.add, sums), functools.reduce(jnp.add, qkv_sums)], axis=1)
    small, _ = lax.optimization_barrier((small, reduced[seqs - 2][2]))
    small = all_sum(small, ctx_size)
    g_ffn = fsdp_near_sum(ffn_far, f, ctx_size)
    g_qkv = fsdp_direct_sum(g_qkv, f, ctx_size)
    return (
        output,
        logits,
        d_hidden,
        d_prev,
        g_qkv[:, :width],
        g_qkv[:, 256 : 256 + width],
        g_qkv[:, 256 + width :],
        g_ffn[:, 2 * units :],
        g_ffn[:, :units],
        g_ffn[:, units : 2 * units],
        small[0, d : d + width],
        small[0, d + 256 + width :],
        small[0, :d],
        small[6, :d],
        small[3, :d],
        small[1, :d],
        small[2, :d],
        small[4, :d],
        small[5, :d],
    )


def solution(mesh):
    tok, lgt, mat = P("fsdp", "ctx", None), P("fsdp", "tp", "ctx", None), P("fsdp", "tp")
    vec, rep = P("tp"), P()
    in_specs = (tok, lgt) + (mat,) * 6 + (vec, vec, rep, vec) + (rep,) * 5 + (tok, lgt)
    out_specs = (tok, lgt, tok, lgt) + (mat,) * 6 + (vec, vec, rep, vec) + (rep,) * 5
    return jax.shard_map(
        functools.partial(body, ctx_size=mesh.shape["ctx"]),
        mesh=mesh,
        in_specs=in_specs,
        out_specs=out_specs,
        check_vma=False,
    )
```

```python
import functools

import jax
import jax.numpy as jnp
from jax import lax
from jax.experimental import pallas as pl
from jax.experimental.pallas import tpu as pltpu
from jax.sharding import PartitionSpec as P

BLOCK = 256
EPS = 1e-6
BF = jnp.bfloat16
F32 = jnp.float32
VMEM_LIMIT = 63 * 1024 * 1024
ANY = pl.BlockSpec(memory_space=pl.ANY)

SWAP = ((0, 1), (1, 0), (2, 3), (3, 2))
FAR = ((0, 2), (2, 0), (1, 3), (3, 1))
ACROSS = ((0, 3), (3, 0), (1, 2), (2, 1))
MIDDLE = ((1, 2), (2, 1))
OUTWARD = ((1, 0), (2, 3))


def params(**kw):
    return pltpu.CompilerParams(vmem_limit_bytes=VMEM_LIMIT, **kw)


def dot(left, right):
    return jnp.dot(left, right, preferred_element_type=F32)


def dot_nt(left, right):
    return lax.dot_general(left, right, (((1,), (1,)), ((), ())), preferred_element_type=F32)


def gelu_parts(u):
    cdf = 0.5 + 0.5 * lax.erf(u * 0.5**0.5)
    density = jnp.exp(-0.5 * (u * u)) * 0.3989422804014327
    return u * cdf, cdf + u * density


def head_mask(value, offset, head, size):
    lane = lax.broadcasted_iota(jnp.int32, value.shape, 1)
    keep = (lane >= offset + head * size) & (lane < offset + (head + 1) * size)
    return jnp.where(keep, value, jnp.zeros_like(value))


def load_rows(ids, pieces, scratch, sems):
    f = ids[0]
    rows = pieces[0].shape[0]
    copies = []
    for k, piece in enumerate(pieces):
        at = pl.multiple_of((f ^ k) * rows, rows)
        copies.append(pltpu.make_async_copy(piece, scratch.at[pl.ds(at, rows)], sems.at[k]))
    return copies


def qkv_kernel(ids, x_ref, w0, w1, w2, w3, b_ref, *refs, scale):
    q_ref, kv_ref, w_ref, sems = refs[-4:]

    @pl.when((pl.program_id(0) == 0) & (pl.program_id(1) == 0))
    def _():
        copies = load_rows(ids, (w0, w1, w2, w3), w_ref, sems)
        for c in copies:
            c.start()
        for c in copies:
            c.wait()

    width = q_ref.shape[1]
    out = dot(x_ref[0], w_ref[...]) + b_ref[...]
    query = out[:, :width].astype(BF)
    q_ref[...] = (query.astype(F32) * scale).astype(BF)
    kv_ref[...] = out[:, 256:].astype(BF)


def qkv_call(ids, hidden, first, count, pieces, bias, width, scale, after):
    _, rows, d = hidden.shape
    cols = pieces[0].shape[1]
    tile = min(rows, 256)
    tiles = rows // tile
    flat = lambda i, j, s: (i * tiles + j, 0)
    fixed = lambda i, j, s: (0, 0)
    return pl.pallas_call(
        functools.partial(qkv_kernel, scale=scale),
        out_shape=(
            jax.ShapeDtypeStruct((count * rows, width), BF),
            jax.ShapeDtypeStruct((count * rows, 2 * width), BF),
            jax.ShapeDtypeStruct((d, cols), BF),
        ),
        grid_spec=pltpu.PrefetchScalarGridSpec(
            num_scalar_prefetch=1,
            grid=(count, tiles),
            in_specs=[pl.BlockSpec((1, tile, d), lambda i, j, s: (first + i, j, 0))]
            + [ANY] * 4
            + [pl.BlockSpec((1, cols), fixed)]
            + [ANY] * len(after),
            out_specs=[
                pl.BlockSpec((tile, width), flat),
                pl.BlockSpec((tile, 2 * width), flat),
                pl.BlockSpec((d, cols), fixed),
            ],
            scratch_shapes=[pltpu.SemaphoreType.DMA((4,))],
        ),
        compiler_params=params(),
        cost_estimate=pl.CostEstimate(
            flops=2 * count * rows * d * cols,
            bytes_accessed=2 * (count * rows + d) * (d + cols),
            transcendentals=0,
        ),
        name="qkv",
    )(ids, hidden, *pieces, bias, *after)


FRAME = 64


def spread_heads(ids, kv_refs, k3, v3, heads, size):
    width = heads * size
    if len(kv_refs) == 2:
        low, own = kv_refs
        rows = own.shape[0]
        own_v = own[...]
        parts = ((0, jnp.where(ids[1] == 0, own_v, low[...])), (rows, own_v))
    else:
        parts = ((0, kv_refs[0][...]),)
    for at, part in parts:
        keys, values = part[:, :width], part[:, 2 * width - 256 :]
        lane = lax.broadcasted_iota(jnp.int32, values.shape, 1)
        for h in range(heads):
            k3[h, at : at + part.shape[0], :] = head_mask(keys, 0, h, size)
            ones = (lane >= 2 * h) & (lane < 2 * h + 2)
            masked = head_mask(values, FRAME, h, size)
            v3[h, at : at + part.shape[0], :] = jnp.where(ones, jnp.ones_like(masked), masked)


def attn_fwd_kernel(ids, *refs, heads, size, nkv):
    q_ref, prev_ref = refs[0], refs[1]
    kv_refs = refs[2 : 2 + nkv]
    bias_ref = refs[2 + nkv]
    log_ref, e_ref, att_ref, sum_ref, k3, v3 = refs[-6:]
    i, rb = pl.program_id(0), pl.program_id(1)
    full = prev_ref.shape[3]
    blocks = (att_ref.shape[0] - bias_ref.shape[0]) // BLOCK
    width = heads * size

    @pl.when(rb == 0)
    def _():
        spread_heads(ids, kv_refs, k3, v3, heads, size)
        att_ref[blocks * BLOCK :] = bias_ref[...]

    g = ids[1] * blocks + rb
    for b in range(full // BLOCK):
        n = (b + 1) * BLOCK

        @pl.when(g == b)
        def _(n=n):
            query = q_ref[...]
            total = None
            for h in range(heads):
                s = dot_nt(query, k3[h, :n, :]) + prev_ref[0, h, :, :n].astype(F32)
                log_ref[0, h, :, :n] = s.astype(BF)
                if n < full:
                    log_ref[0, h, :, n:] = jnp.zeros((BLOCK, full - n), BF)
                e = jnp.exp(s - jnp.max(s, axis=1, keepdims=True)).astype(BF)
                e_ref[0, h, :, :n] = e
                part = dot(e, v3[h, :n, :])
                total = part if total is None else total + part
            inverse = 1.0 / total[:, : 2 * heads]
            sum_ref[...] = jnp.concatenate(
                [inverse, jnp.zeros((BLOCK, 128 - 2 * heads), F32)], axis=1
            )
            lane = lax.broadcasted_iota(jnp.int32, total.shape, 1)
            factor = jnp.zeros_like(total)
            for h in range(heads):
                factor = jnp.where(lane // size == h + 1, inverse[:, 2 * h : 2 * h + 1], factor)
            att = (total * factor)[:, FRAME:].astype(BF)
            at = pl.ds(pl.multiple_of(rb * BLOCK, BLOCK), BLOCK)
            for k in range(att_ref.shape[1] // width):

                @pl.when(i == k)
                def _(k=k):
                    att_ref[at, k * width : (k + 1) * width] = att


def kv_specs(kvs, count):
    specs = []
    for kv in kvs:
        block = (kv.shape[0] // count, kv.shape[1])
        specs.append(pl.BlockSpec(block, lambda i, r, s: (i, 0)))
    return specs


def attn_fwd_call(ids, q, kvs, prev, bias, first, count, chain, heads, size, after):
    seqs, _, rows, full = prev.shape
    width = heads * size
    blocks = rows // BLOCK
    big = pl.BlockSpec((1, heads, BLOCK, full), lambda i, r, s: (first + i, 0, r, 0))
    extra = ([] if chain is None else [chain]) + list(after)
    tokens = 3 * full // 4
    return pl.pallas_call(
        functools.partial(attn_fwd_kernel, heads=heads, size=size, nkv=len(kvs)),
        out_shape=(
            jax.ShapeDtypeStruct(prev.shape, BF),
            jax.ShapeDtypeStruct((count, heads, rows, full), BF),
            jax.ShapeDtypeStruct((rows + bias.shape[0], count * width), BF),
            jax.ShapeDtypeStruct((count * rows, 128), F32),
        ),
        grid_spec=pltpu.PrefetchScalarGridSpec(
            num_scalar_prefetch=1,
            grid=(count, blocks),
            in_specs=[pl.BlockSpec((BLOCK, width), lambda i, r, s: (i * blocks + r, 0)), big]
            + kv_specs(kvs, count)
            + [pl.BlockSpec(bias.shape, lambda i, r, s: (0, 0))]
            + [ANY] * len(extra),
            out_specs=[
                big,
                pl.BlockSpec((1, heads, BLOCK, full), lambda i, r, s: (i, 0, r, 0)),
                pl.BlockSpec((rows + bias.shape[0], count * width), lambda i, r, s: (0, 0)),
                pl.BlockSpec((BLOCK, 128), lambda i, r, s: (i * blocks + r, 0)),
            ],
            scratch_shapes=[
                pltpu.VMEM((heads, full, width), BF),
                pltpu.VMEM((heads, full, 256), BF),
            ],
        ),
        input_output_aliases={} if chain is None else {4 + len(kvs): 0},
        compiler_params=params(),
        cost_estimate=pl.CostEstimate(
            flops=4 * 4 * count * heads * rows * tokens * size,
            bytes_accessed=6 * count * heads * rows * full,
            transcendentals=count * heads * rows * tokens,
        ),
        name="attn_fwd",
    )(ids, q, prev, *kvs, bias, *extra)


def attn_bwd_kernel(ids, *refs, heads, size, nkv, local, scale):
    q_ref, e_ref, dl_ref, datt_ref, att_ref, sum_ref = refs[:6]
    kv_refs = refs[6 : 6 + nkv]
    if nkv == 2:
        dprev_ref, dq_ref, own_ref, send_ref, k3, v3, dkv_t = refs[-7:]
    else:
        dprev_ref, dq_ref, own_ref, k3, v3, dkv_t = refs[-6:]
    i, rb = pl.program_id(0), pl.program_id(1)
    blocks = pl.num_programs(1)
    full = dl_ref.shape[3]
    width = heads * size

    @pl.when(rb == 0)
    def _():
        spread_heads(ids, kv_refs, k3, v3, heads, size)
        dkv_t[...] = jnp.zeros_like(dkv_t)

    g = ids[1] * blocks + rb
    for b in range(full // BLOCK):
        n = (b + 1) * BLOCK

        @pl.when(g == b)
        def _(n=n):
            datt = datt_ref[...].astype(F32)
            att = att_ref[:, local * width : (local + 1) * width]
            if att_ref.shape[1] > (local + 1) * width:
                att = jnp.where(i == 0, att, att_ref[:, (local + 1) * width :])
            weighted = datt * att.astype(F32)
            lane = lax.broadcasted_iota(jnp.int32, datt.shape, 1)
            head = lax.broadcasted_iota(jnp.int32, (BLOCK, FRAME), 1)
            factor = jnp.zeros_like(datt)
            front = jnp.zeros((BLOCK, FRAME), F32)
            for h in range(heads):
                inverse = sum_ref[:, 2 * h : 2 * h + 1]
                factor = jnp.where(lane // size == h, inverse, factor)
                delta = jnp.sum(head_mask(weighted, 0, h, size), axis=1, keepdims=True)
                delta = -delta * inverse
                high = delta.astype(BF).astype(F32)
                front = jnp.where(head == 2 * h, high, front)
                front = jnp.where(head == 2 * h + 1, delta - high, front)
            scaled = (datt * factor).astype(BF)
            framed = jnp.concatenate([front.astype(BF), scaled], axis=1)
            q_t = q_ref[...].T
            scaled_t = scaled.T
            total = None
            for h in range(heads):
                at = h * size
                dp = dot_nt(framed, v3[h, :n, :])
                e = e_ref[0, h, :, :n]
                ds = e.astype(F32) * dp + dl_ref[0, h, :, :n].astype(F32)
                low = ds.astype(BF)
                dprev_ref[0, h, :, :n] = low
                if n < full:
                    dprev_ref[0, h, :, n:] = jnp.zeros((BLOCK, full - n), BF)
                part = dot(low, k3[h, :n, :])
                total = part if total is None else total + part
                dkv_t[at : at + size, :n] += dot(q_t[at : at + size], low)
                at += width
                dkv_t[at : at + size, :n] += dot(scaled_t[at - width : at - width + size], e)
            dq_ref[...] = (total * scale).astype(BF)

    @pl.when(rb == blocks - 1)
    def _():
        if nkv == 2:
            rows = full // 2

            @pl.when(ids[1] == 0)
            def _():
                own_ref[...] = dkv_t[:, :rows].T.astype(BF)

            @pl.when(ids[1] == 1)
            def _():
                own_ref[...] = dkv_t[:, rows:].T.astype(BF)
                send_ref[...] = dkv_t[:, :rows].T.astype(BF)
        else:
            own_ref[...] = dkv_t[...].T.astype(BF)


def attn_bwd_call(
    ids, q, e, d_logits, datt, att, inverse, kvs, first, base, count, of, chain, heads, size, scale, after
):
    seqs, _, rows, full = d_logits.shape
    width = heads * size
    blocks = rows // BLOCK
    big = pl.BlockSpec((1, heads, BLOCK, full), lambda i, r, s: (first + i, 0, r, 0))
    extra = ([] if chain is None else [chain]) + list(after)
    tokens = 3 * full // 4
    tile = lambda w, k: pl.BlockSpec((BLOCK, w), lambda i, r, s: ((k + i) * blocks + r, 0))
    kv_in = []
    for kv in kvs:
        block = (kv.shape[0] // of, kv.shape[1])
        kv_in.append(pl.BlockSpec(block, lambda i, r, s: (base + i, 0)))
    grads = [(rows, rows)] if len(kvs) == 2 else [(full,)]
    sizes = grads[0]
    return pl.pallas_call(
        functools.partial(
            attn_bwd_kernel, heads=heads, size=size, nkv=len(kvs), local=base, scale=scale
        ),
        out_shape=(
            jax.ShapeDtypeStruct(d_logits.shape, BF),
            jax.ShapeDtypeStruct((count * rows, width), BF),
        )
        + tuple(jax.ShapeDtypeStruct((count * z, 2 * width), BF) for z in sizes),
        grid_spec=pltpu.PrefetchScalarGridSpec(
            num_scalar_prefetch=1,
            grid=(count, blocks),
            in_specs=[
                tile(width, base),
                pl.BlockSpec((1, heads, BLOCK, full), lambda i, r, s: (base + i, 0, r, 0)),
                big,
                tile(width, base),
                pl.BlockSpec((BLOCK, of * width), lambda i, r, s: (r, 0)),
                tile(128, base),
            ]
            + kv_in
            + [ANY] * len(extra),
            out_specs=[big, tile(width, 0)]
            + [pl.BlockSpec((z, 2 * width), lambda i, r, s: (i, 0)) for z in sizes],
            scratch_shapes=[
                pltpu.VMEM((heads, full, width), BF),
                pltpu.VMEM((heads, full, 256), BF),
                pltpu.VMEM((2 * width, full), F32),
            ],
        ),
        input_output_aliases={} if chain is None else {7 + len(kvs): 0},
        compiler_params=params(),
        cost_estimate=pl.CostEstimate(flops=9000000000, bytes_accessed=1000, transcendentals=0),
        name="attn_bwd",
    )(ids, q, e, d_logits, datt, att, inverse, *kvs, *extra)


def row_mean(value):
    return jnp.mean(value, axis=1, keepdims=True)


def col_sum(value):
    return jnp.sum(value, axis=0, keepdims=True)


def ffn_kernel(ids, *refs, chained, final, base, width, units):
    x_ref, a0, a1, a2, a3, do_ref, vec_ref, b0, b1, b2, b3 = refs[:11]
    pieces = refs[11:15]
    if chained:
        gi_in, go_in, gw_in = refs[15:18]
    if final:
        out_ref, dh1_ref, datt_ref, sum_ref, grad_ref = refs[-18:-13]
    else:
        out_ref, dh1_ref, datt_ref, sum_ref, gi_hbm, go_hbm, gw_hbm = refs[-20:-13]
    wi, wo, wa, act_s, gp_s, din_s, att_s, gi, go, gw, bin_s, w_sem, g_sem = refs[-13:]
    i, j = pl.program_id(0), pl.program_id(1)
    start = (i == 0) & (j == 0)
    last = (i == pl.num_programs(0) - 1) & (j == pl.num_programs(1) - 1)
    rank = ids[2]
    rows = pieces[0].shape[1]

    def copies(group):
        out = []
        for k in range(4):
            at = pl.ds(pl.multiple_of((ids[0] ^ k) * rows, rows), rows)
            for slot in range(4):
                piece = pieces[k].at[slot]
                sem = w_sem.at[group, k * 4 + slot]
                if group == 0:
                    src, dst = piece.at[:, 2 * units : 2 * units + width], wa
                elif group == 1:
                    src, dst = piece.at[:, :units], wi
                else:
                    src, dst = piece.at[:, units : 2 * units], wo
                dst = dst.at[rank ^ slot, at]
                out.append(pltpu.make_async_copy(src, dst, sem))
        return out

    def grad_in():
        return [
            pltpu.make_async_copy(src, dst, g_sem.at[k])
            for k, (src, dst) in enumerate(((gi_in, gi), (go_in, go), (gw_in, gw)))
        ]

    @pl.when(start)
    def _():
        for group in range(3):
            for c in copies(group):
                c.start()
        if chained:
            for c in grad_in():
                c.start()
        else:
            gi[...] = jnp.zeros_like(gi)
            go[...] = jnp.zeros_like(go)
            gw[...] = jnp.zeros_like(gw)
        sum_ref[...] = jnp.zeros_like(sum_ref)
        for slot, b in enumerate((b0, b1, b2, b3)):
            value = b[...].astype(F32)
            left = value[0:1] + value[2:3] + value[4:5]
            right = value[1:2] + value[3:4] + value[5:6]
            bin_s[rank ^ slot] = jnp.concatenate([left, right], axis=1)
        for c in copies(0):
            c.wait()

    chunk = a0.shape[1] // width
    b_out, gain_a, shift_a = vec_ref[0:1], vec_ref[1:2], vec_ref[2:3]
    b_outer, gain_f, shift_f = vec_ref[3:4], vec_ref[4:5], vec_ref[5:6]
    half = x_ref.shape[1] // 2
    parts = [slice(0, half), slice(half, 2 * half)]
    n1, r1, normed, n2, r2 = [None] * 2, [None] * 2, [None] * 2, [None] * 2, [None] * 2
    h2, dn, dh2_low, dh1_low = [None] * 2, [None] * 2, [None] * 2, [None] * 2

    for p in range(2):
        for slot, a in enumerate((a0, a1, a2, a3)):
            value = a[parts[p], base * width : (base + 1) * width]
            if chunk > base + 1:
                value = jnp.where(i == 0, value, a[parts[p], (base + 1) * width :])
            att_s[rank ^ slot, parts[p]] = value
    for p in range(2):
        h1 = x_ref[0, parts[p]].astype(F32) + b_out
        for t in range(4):
            h1 = h1 + dot_nt(att_s[t, parts[p]], wa[t])
        c1 = h1 - row_mean(h1)
        r1[p] = lax.rsqrt(row_mean(c1 * c1) + EPS)
        n1[p] = c1 * r1[p]
        normed[p] = (n1[p] * gain_a + shift_a).astype(BF)

    @pl.when(start)
    def _():
        for c in copies(1):
            c.wait()
        for c in copies(2):
            c.wait()
        if chained:
            for c in grad_in():
                c.wait()

    def forward(p):
        h2[p] = normed[p].astype(F32) + b_outer
        for t in range(4):
            inner = dot(normed[p], wi[t]) + bin_s[t]
            act, slope = gelu_parts(inner)
            low = act.astype(BF)
            act_s[t, parts[p]] = low
            gp_s[t, parts[p]] = slope.astype(BF)
            h2[p] = h2[p] + dot_nt(low, wo[t])

    def turn(p):
        c2 = h2[p] - row_mean(h2[p])
        r2[p] = lax.rsqrt(row_mean(c2 * c2) + EPS)
        n2[p] = c2 * r2[p]
        out_ref[0, parts[p]] = (n2[p] * gain_f + shift_f).astype(BF)
        d_out = do_ref[0, parts[p]].astype(F32)
        e2 = d_out * gain_f
        dh2 = (e2 - row_mean(e2) - n2[p] * row_mean(e2 * n2[p])) * r2[p]
        sum_ref[3:4] += col_sum(dh2)
        sum_ref[4:5] += col_sum(d_out * n2[p])
        sum_ref[5:6] += col_sum(d_out)
        dh2_low[p] = dh2.astype(BF)
        dn[p] = dh2

    def backward(p):
        for t in range(4):
            din = dot(dh2_low[p], wo[t]) * gp_s[t, parts[p]].astype(F32)
            low = din.astype(BF)
            din_s[t, parts[p]] = low
            dn[p] = dn[p] + dot_nt(low, wi[t])

    def close(p):
        e1 = dn[p] * gain_a
        dh1 = (e1 - row_mean(e1) - n1[p] * row_mean(e1 * n1[p])) * r1[p]
        dh1_ref[parts[p]] = dh1
        dh1_low[p] = dh1.astype(BF)
        sum_ref[0:1] += col_sum(dh1)
        sum_ref[1:2] += col_sum(dn[p] * n1[p])
        sum_ref[2:3] += col_sum(dn[p])

    forward(0)
    turn(0)
    forward(1)
    backward(0)
    turn(1)
    close(0)
    backward(1)
    datt_ref[parts[0]] = dot(dh1_low[0], wa[rank]).astype(BF)
    close(1)
    gi[...] += dot(jnp.concatenate(normed, axis=0).T, din_s[rank])
    go[...] += dot(jnp.concatenate(dh2_low, axis=0).T, act_s[rank])
    datt_ref[parts[1]] = dot(dh1_low[1], wa[rank]).astype(BF)
    gw[...] += dot(jnp.concatenate(dh1_low, axis=0).T, att_s[rank])
    sum_ref[6:7] += col_sum(din_s[rank].astype(F32))

    @pl.when(last)
    def _():
        if final:
            grad_ref[:, :units] = gi[...].astype(BF)
            grad_ref[:, units : 2 * units] = go[...].astype(BF)
            grad_ref[:, 2 * units :] = gw[...].astype(BF)
        else:
            out = [
                pltpu.make_async_copy(src, dst, g_sem.at[k])
                for k, (src, dst) in enumerate(((gi, gi_hbm), (go, go_hbm), (gw, gw_hbm)))
            ]
            for c in out:
                c.start()
            for c in out:
                c.wait()


def ffn_call(
    ids, hidden, atts, d_output, vec, bias, weights, first, base, count, chain, width, units, final, after
):
    seqs, rows, d = hidden.shape
    tile = min(rows, 512)
    tiles = rows // tile
    chunk = atts[0].shape[1]
    whole = pl.BlockSpec((1, tile, d), lambda i, j, s: (first + i, j, 0))
    att = pl.BlockSpec((tile, chunk), lambda i, j, s: (j, 0))
    flat = lambda w: pl.BlockSpec((tile, w), lambda i, j, s: (i * tiles + j, 0))
    fixed = lambda shape: pl.BlockSpec(shape, lambda i, j, s: (0, 0))
    chained = [] if chain is None else list(chain)
    extra = chained + list(after)
    at = 1 + 11 + 4
    aliases = {}
    if chained:
        aliases = {at + 3: 0} if final else {at: 4, at + 1: 5, at + 2: 6, at + 3: 0}
    grads = (
        (jax.ShapeDtypeStruct((d, 2 * units + width), BF),)
        if final
        else (
            jax.ShapeDtypeStruct((d, units), F32),
            jax.ShapeDtypeStruct((d, units), F32),
            jax.ShapeDtypeStruct((d, width), F32),
        )
    )
    return pl.pallas_call(
        functools.partial(
            ffn_kernel, chained=bool(chained), final=final, base=base, width=width, units=units
        ),
        out_shape=(
            jax.ShapeDtypeStruct(hidden.shape, BF),
            jax.ShapeDtypeStruct((count * rows, d), F32),
            jax.ShapeDtypeStruct((count * rows, width), BF),
            jax.ShapeDtypeStruct((8, d), F32),
        )
        + grads,
        grid_spec=pltpu.PrefetchScalarGridSpec(
            num_scalar_prefetch=1,
            grid=(count, tiles),
            in_specs=[whole, att, att, att, att, whole, fixed((8, d))]
            + [pl.BlockSpec((16, chunk), lambda i, j, s: (rows // 16, 0))] * 4
            + [ANY] * (4 + len(extra)),
            out_specs=[whole, flat(d), flat(width), fixed((8, d))]
            + ([fixed((d, 2 * units + width))] if final else [ANY] * 3),
            scratch_shapes=[
                pltpu.VMEM((4, d, units), BF),
                pltpu.VMEM((4, d, units), BF),
                pltpu.VMEM((4, d, width), BF),
                pltpu.VMEM((4, tile, units), BF),
                pltpu.VMEM((4, tile, units), BF),
                pltpu.VMEM((4, tile, units), BF),
                pltpu.VMEM((4, tile, width), BF),
                pltpu.VMEM((d, units), F32),
                pltpu.VMEM((d, units), F32),
                pltpu.VMEM((d, width), F32),
                pltpu.VMEM((4, 1, units), F32),
                pltpu.SemaphoreType.DMA((3, 16)),
                pltpu.SemaphoreType.DMA((3,)),
            ],
        ),
        input_output_aliases=aliases,
        compiler_params=params(),
        cost_estimate=pl.CostEstimate(
            flops=2 * count * rows * d * units * 20,
            bytes_accessed=16 * d * units + 16 * count * rows * d,
            transcendentals=8 * count * rows * units,
        ),
        name="ffn",
    )(ids, hidden, *atts, d_output, vec, *bias, *weights, *extra)


def dx_kernel(ids, dq_ref, *refs, nkv):
    dkv_refs = refs[:nkv]
    w_ref = refs[nkv]
    y_ref, joined_ref, sum_ref = refs[-3:]
    dq = dq_ref[...]
    dkv = dkv_refs[0][...]
    if nkv == 2:
        dkv = (dkv.astype(F32) + dkv_refs[1][...].astype(F32)).astype(BF)
    pad = jnp.zeros((dq.shape[0], 256 - dq.shape[1]), BF)
    joined = jnp.concatenate([dq, pad, dkv], axis=1)
    joined_ref[...] = joined

    @pl.when(pl.program_id(0) == 0)
    def _():
        sum_ref[...] = jnp.zeros_like(sum_ref)

    sum_ref[0:1] += col_sum(joined.astype(F32))
    y_ref[...] = dot_nt(joined, w_ref[...]).astype(BF)


def dx_call(ids, dq, dkvs, weight, first, tokens, chain, after):
    count = dq.shape[0]
    d, cols = weight.shape
    tile = min(count, 256)
    offset = first // tile
    flat = lambda w: pl.BlockSpec((tile, w), lambda i, s: (i, 0))
    extra = ([] if chain is None else [chain]) + list(after)
    return pl.pallas_call(
        functools.partial(dx_kernel, nkv=len(dkvs)),
        out_shape=(
            jax.ShapeDtypeStruct((count, d), BF),
            jax.ShapeDtypeStruct((tokens, cols), BF),
            jax.ShapeDtypeStruct((8, cols), F32),
        ),
        grid_spec=pltpu.PrefetchScalarGridSpec(
            num_scalar_prefetch=1,
            grid=(count // tile,),
            in_specs=[flat(dq.shape[1])]
            + [flat(v.shape[1]) for v in dkvs]
            + [pl.BlockSpec((d, cols), lambda i, s: (0, 0))]
            + [ANY] * len(extra),
            out_specs=[
                flat(d),
                pl.BlockSpec((tile, cols), lambda i, s: (offset + i, 0)),
                pl.BlockSpec((8, cols), lambda i, s: (0, 0)),
            ],
        ),
        input_output_aliases={} if chain is None else {3 + len(dkvs): 1},
        compiler_params=params(),
        cost_estimate=pl.CostEstimate(flops=3000000000, bytes_accessed=1000, transcendentals=0),
        name="dx",
    )(ids, dq, *dkvs, weight, *extra)


def grad_kernel(x_ref, joined_ref, *refs):
    g_ref, acc = refs[-2:]
    i = pl.program_id(0)

    @pl.when(i == 0)
    def _():
        acc[...] = jnp.zeros_like(acc)

    joined = joined_ref[...]
    acc[...] += dot(x_ref[0].T, joined)

    @pl.when(i == pl.num_programs(0) - 1)
    def _():
        g_ref[...] = acc[...].astype(BF)


def grad_call(hidden, joined, after):
    seqs, rows, d = hidden.shape
    cols = joined.shape[1]
    fixed = lambda shape: pl.BlockSpec(shape, lambda i: (0, 0))
    return pl.pallas_call(
        grad_kernel,
        out_shape=jax.ShapeDtypeStruct((d, cols), BF),
        grid=(seqs,),
        in_specs=[
            pl.BlockSpec((1, rows, d), lambda i: (i, 0, 0)),
            pl.BlockSpec((rows, cols), lambda i: (i, 0)),
        ]
        + [ANY] * len(after),
        out_specs=fixed((d, cols)),
        scratch_shapes=[pltpu.VMEM((d, cols), F32)],
        compiler_params=params(),
        cost_estimate=pl.CostEstimate(
            flops=2 * seqs * rows * d * cols, bytes_accessed=4 * d * cols, transcendentals=0
        ),
        name="grad",
    )(hidden, joined, *after)


def final_kernel(ids, dh1_ref, done_ref, other_ref, *refs):
    out_ref = refs[-1]
    upper = pl.program_id(0) == 0
    odd = lax.rem(ids[2], 2) == 1
    own = upper != odd
    both = jnp.where(own, done_ref[...].astype(F32), other_ref[...].astype(F32))
    out_ref[0] = dh1_ref[...] + both


def plain_kernel(dh1_ref, total_ref, *refs):
    refs[-1][0] = dh1_ref[...] + total_ref[...].astype(F32)


def plain_call(dh1, at, total, first, rows, seqs, chain, after):
    d = total.shape[1]
    tile = min(rows, 256)
    extra = ([] if chain is None else [chain]) + list(after)
    return pl.pallas_call(
        plain_kernel,
        out_shape=jax.ShapeDtypeStruct((seqs, rows, d), F32),
        grid=(rows // tile,),
        in_specs=[
            pl.BlockSpec((tile, d), lambda j: (at // tile + j, 0)),
            pl.BlockSpec((tile, d), lambda j: (j, 0)),
        ]
        + [ANY] * len(extra),
        out_specs=pl.BlockSpec((1, tile, d), lambda j: (first, j, 0)),
        input_output_aliases={} if chain is None else {2: 0},
        compiler_params=params(),
        cost_estimate=pl.CostEstimate(
            flops=2 * rows * d, bytes_accessed=10 * rows * d, transcendentals=0
        ),
        name="plain",
    )(dh1, total, *extra)


def final_call(ids, dh1, at, done, other, first, rows, seqs, chain, after):
    half, d = done.shape
    tile = min(half, 256)
    per_half = half // tile
    per_seq = rows // tile
    extra = ([] if chain is None else [chain]) + list(after)
    part = pl.BlockSpec((tile, d), lambda h, j, s: (j, 0))
    flat = lambda h, j: h * per_half + j
    return pl.pallas_call(
        final_kernel,
        out_shape=jax.ShapeDtypeStruct((seqs, rows, d), F32),
        grid_spec=pltpu.PrefetchScalarGridSpec(
            num_scalar_prefetch=1,
            grid=(2, per_half),
            in_specs=[
                pl.BlockSpec((tile, d), lambda h, j, s: (at // tile + flat(h, j), 0)),
                part,
                part,
            ]
            + [ANY] * len(extra),
            out_specs=pl.BlockSpec(
                (1, tile, d),
                lambda h, j, s: (first + flat(h, j) // per_seq, flat(h, j) % per_seq, 0),
            ),
        ),
        input_output_aliases={} if chain is None else {4: 0},
        compiler_params=params(),
        cost_estimate=pl.CostEstimate(
            flops=4 * half * d, bytes_accessed=24 * half * d, transcendentals=0
        ),
        name="final",
    )(ids, dh1, done, other, *extra)


def tp_gather(value):
    return [value] + [lax.ppermute(value, "tp", p) for p in (SWAP, FAR, ACROSS)]


def fsdp_gather(value):
    far = lax.ppermute(value, "fsdp", FAR)
    near = lax.ppermute(value, "fsdp", SWAP)
    return value, near, far, lax.ppermute(far, "fsdp", SWAP)


def tp_reduce(value, odd):
    half = value.shape[0] // 2
    top, bottom = value[:half], value[half:]
    sent = jnp.where(odd, top, bottom)
    got = lax.ppermute(sent, "tp", SWAP)
    pair = jnp.where(odd, bottom, top) + got
    done = pair + lax.ppermute(pair, "tp", FAR)
    return sent, pair, done, lax.ppermute(done, "tp", SWAP)


def ctx_sum(value, size):
    if size == 2:
        return value + lax.ppermute(value, "ctx", ((0, 1), (1, 0)))
    return lax.psum(value, "ctx")


def fsdp_far_sum(value, f):
    rows = value.shape[0] // 4
    pairs = value.reshape(2, 2, rows, value.shape[1])
    mine = lax.dynamic_index_in_dim(pairs, f // 2, 0, keepdims=False)
    other = lax.dynamic_index_in_dim(pairs, 1 - f // 2, 0, keepdims=False)
    return mine + lax.ppermute(other, "fsdp", FAR)


def fsdp_near_sum(mine, f, size):
    own = lax.dynamic_index_in_dim(mine, f % 2, 0, keepdims=False)
    near = lax.dynamic_index_in_dim(mine, 1 - f % 2, 0, keepdims=False)
    own = own + lax.ppermute(near, "fsdp", SWAP)
    return ctx_sum(own, size).astype(F32)


def fsdp_direct_sum(value, f, size):
    rows = value.shape[0] // 4
    blocks = value.reshape(4, rows, value.shape[1])
    pick = lambda k: lax.dynamic_index_in_dim(blocks, f ^ k, 0, keepdims=False)
    total = pick(0).astype(F32)
    for k, pairs in ((1, SWAP), (2, FAR), (3, ACROSS)):
        total = total + lax.ppermute(pick(k), "fsdp", pairs).astype(F32)
    return ctx_sum(total.astype(BF), size).astype(F32)


def all_sum(value, size):
    value = value + lax.ppermute(value, "fsdp", SWAP)
    value = value + lax.ppermute(value, "fsdp", FAR)
    return ctx_sum(value, size)


def body(
    hidden_in,
    prev_logits,
    w_query,
    w_key,
    w_value,
    w_out,
    w_inner,
    w_outer,
    b_query,
    b_value,
    b_out,
    b_inner,
    b_outer,
    gain_attn,
    shift_attn,
    gain_ffn,
    shift_ffn,
    d_output,
    d_logits,
    *,
    ctx_size,
):
    seqs, rows, d = hidden_in.shape
    heads = prev_logits.shape[1]
    width = w_query.shape[1]
    units = w_inner.shape[1]
    size = width // heads
    scale = size**-0.5
    f, c, rank = lax.axis_index("fsdp"), lax.axis_index("ctx"), lax.axis_index("tp")
    ids = jnp.stack([f, c, rank]).astype(jnp.int32)
    odd = rank % 2 == 1

    ffn_local = jnp.concatenate([w_inner, w_outer, w_out], axis=1)
    qkv_local = jnp.concatenate(
        [w_query, jnp.zeros((w_query.shape[0], 256 - width), BF), w_key, w_value], axis=1
    )
    qkv_pieces = fsdp_gather(qkv_local)
    inner_rank = (rank == 1) | (rank == 2)
    w_near = lax.ppermute(ffn_local, "tp", SWAP)
    w_across = lax.ppermute(ffn_local, "tp", MIDDLE)
    far = lambda value: lax.ppermute(value, "fsdp", FAR)
    own_local, _ = lax.optimization_barrier((ffn_local, qkv_pieces[2]))
    w_far = [far(own_local)]
    qkv_bias = jnp.concatenate([b_query, jnp.zeros((256,), F32), b_value])[None]
    vec = jnp.stack([b_out, gain_attn, shift_attn, b_outer, gain_ffn, shift_ffn, b_out, b_out])

    chunk = 2
    starts = range(0, seqs, chunk)
    queries, kvs, after = [], [], []
    for s in starts:
        q, kv, w_qkv = qkv_call(
            ids, hidden_in, s, chunk, qkv_pieces, qkv_bias, width, scale, after
        )
        after = [q]
        if s == 0:
            w_near, w_across, w_far[0], _ = lax.optimization_barrier(
                (w_near, w_across, w_far[0], q)
            )
            w_far.append(far(w_near))
            w_middle = lax.ppermute(w_near, "tp", MIDDLE)
            w_out_a = lax.ppermute(w_across, "tp", OUTWARD)
        queries.append(q)
        if ctx_size == 2:
            kvs.append((lax.ppermute(kv, "ctx", ((0, 1),)), kv))
        else:
            got = lax.all_gather(kv.reshape(chunk, rows, 2 * width), "ctx", axis=1, tiled=True)
            kvs.append((got.reshape(-1, 2 * width),))

    w_two = jnp.where(inner_rank, w_middle, w_out_a)
    w_far.append(far(w_two))
    w_out_b = lax.ppermute(w_middle, "tp", OUTWARD)
    after = after + [w_two]
    high = lax.reduce_precision(b_inner, 8, 7)
    middle = lax.reduce_precision(b_inner - high, 8, 7)
    parts = jnp.stack([high, middle, b_inner - high - middle]).reshape(6, units // 2)
    bias = jnp.pad(parts.astype(BF), ((0, 10), (0, 0)))
    logits, probs, atts, inverses = None, [], [], []
    for k, s in enumerate(starts):
        logits, e, att, inverse = attn_fwd_call(
            ids, queries[k], kvs[k], prev_logits, bias, s, chunk, logits, heads, size, after
        )
        after = [att]
        probs.append(e)
        if k == 0:
            atts.append(tp_gather(att))
        else:
            every = lax.all_gather(att, "tp", axis=0, tiled=False)
            atts.append([att] + [
                lax.dynamic_index_in_dim(every, rank ^ slot, 0, keepdims=False)
                for slot in range(1, 4)
            ])
        inverses.append(inverse)
        if k == 0:
            w_out_b, _ = lax.optimization_barrier((w_out_b, att))
            w_three = jnp.where(inner_rank, w_across, w_out_b)
            w_far.append(far(w_three))
            w_here = jnp.stack([ffn_local, w_near, w_two, w_three])
            w_there = lax.ppermute(w_here, "fsdp", SWAP)
            after = after + [w_here]
        else:
            w_far, atts[0], _ = lax.optimization_barrier((w_far, atts[0], att))
            w_far = jnp.stack(w_far)
            weights = [w_here, w_there, w_far, lax.ppermute(w_far, "fsdp", SWAP)]

    chain, sums, qkv_sums, dh1s, datts = None, [], [], {}, {}
    d_prev, d_hidden, joined = None, None, None

    def ffn(s, count, after):
        nonlocal chain, grad_ffn, output
        k, base = s // chunk, s % chunk
        final = s + count == seqs
        out = ffn_call(
            ids,
            hidden_in,
            atts[k],
            d_output,
            vec,
            atts[0],
            weights,
            s,
            base,
            count,
            chain,
            width,
            units,
            final,
            after,
        )
        output, dh1s[s], datts[s], part = out[:4]
        sums.append(part)
        if final:
            grad_ffn = out[4]
        else:
            chain = (out[4], out[5], out[6], output)
        return [datts[s]]

    def attn_bwd(s, count, after):
        nonlocal d_prev
        k, base = s // chunk, s % chunk
        out = attn_bwd_call(
            ids,
            queries[k],
            probs[k],
            d_logits,
            datts[k * chunk],
            atts[k][0],
            inverses[k],
            kvs[k],
            s,
            base,
            count,
            chunk,
            d_prev,
            heads,
            size,
            scale,
            after,
        )
        d_prev, dq = out[:2]
        if ctx_size == 2:
            dkvs = (out[2], lax.ppermute(out[3], "ctx", ((1, 0),)))
        else:
            full_grad = out[2].reshape(count, -1, 2 * width)
            part = lax.psum_scatter(full_grad, "ctx", scatter_dimension=1, tiled=True)
            dkvs = (part.reshape(-1, 2 * width),)
        return (dq, dkvs), [dq]

    def dx(s, grads, after):
        nonlocal joined
        y, joined, part = dx_call(
            ids, grads[0], grads[1], w_qkv, s * rows, seqs * rows, joined, after
        )
        qkv_sums.append(part)
        return y, [y]

    def finish(s, after):
        nonlocal d_hidden
        k, at = s // chunk, (s % chunk) * rows
        if not isinstance(reduced[s], tuple):
            d_hidden = plain_call(
                dh1s[k * chunk], at, reduced[s], s, rows, seqs, d_hidden, after
            )
            return [d_hidden]
        _, _, done, other = reduced[s]
        d_hidden = final_call(
            ids, dh1s[k * chunk], at, done, other, s, rows, seqs, d_hidden, after
        )
        return [d_hidden]

    grad_ffn = output = None
    held, reduced = {}, {}
    ys, ffn_far = {}, None
    for s in starts:
        after = ffn(s, chunk, after)
        last = s + chunk == seqs
        if last:
            ffn_far = fsdp_far_sum(grad_ffn, f)
        if not last:
            for i in range(s, s + chunk):
                held[i], after = attn_bwd(i, 1, after)
        for i in range(s, s + chunk):
            if last:
                extra = [reduced[0], reduced[1][1]] if i == s else []
                held[i], after = attn_bwd(i, 1, after + extra)
                finish(i - s, after)
                after = after + [d_hidden, reduced[i - 1][1 if i > s else 2]]
            ys[i], after = dx(i, held[i], after)
            if i == 0:
                reduced[i] = lax.psum(ys[i], "tp")
            else:
                reduced[i] = tp_reduce(ys[i], odd)
    after = after + [reduced[seqs - 1][0]]
    g_qkv = grad_call(hidden_in, joined, after)
    for s in range(seqs - chunk, seqs):
        finish(s, [g_qkv])

    small = jnp.concatenate([functools.reduce(jnp.add, sums), functools.reduce(jnp.add, qkv_sums)], axis=1)
    g_ffn = fsdp_near_sum(ffn_far, f, ctx_size)
    g_qkv, g_ffn = lax.optimization_barrier((g_qkv, g_ffn))
    g_qkv = fsdp_direct_sum(g_qkv, f, ctx_size)
    small, _ = lax.optimization_barrier((small, reduced[seqs - 2][2]))
    small = all_sum(small, ctx_size)
    return (
        output,
        logits,
        d_hidden,
        d_prev,
        g_qkv[:, :width],
        g_qkv[:, 256 : 256 + width],
        g_qkv[:, 256 + width :],
        g_ffn[:, 2 * units :],
        g_ffn[:, :units],
        g_ffn[:, units : 2 * units],
        small[0, d : d + width],
        small[0, d + 256 + width :],
        small[0, :d],
        small[6, :d],
        small[3, :d],
        small[1, :d],
        small[2, :d],
        small[4, :d],
        small[5, :d],
    )


def solution(mesh):
    tok, lgt, mat = P("fsdp", "ctx", None), P("fsdp", "tp", "ctx", None), P("fsdp", "tp")
    vec, rep = P("tp"), P()
    in_specs = (tok, lgt) + (mat,) * 6 + (vec, vec, rep, vec) + (rep,) * 5 + (tok, lgt)
    out_specs = (tok, lgt, tok, lgt) + (mat,) * 6 + (vec, vec, rep, vec) + (rep,) * 5
    return jax.shard_map(
        functools.partial(body, ctx_size=mesh.shape["ctx"]),
        mesh=mesh,
        in_specs=in_specs,
        out_specs=out_specs,
        check_vma=False,
    )
```

```python
import functools

import jax
import jax.numpy as jnp
from jax import lax
from jax.experimental import pallas as pl
from jax.experimental.pallas import tpu as pltpu
from jax.sharding import PartitionSpec as P

BLOCK = 256
EPS = 1e-6
BF = jnp.bfloat16
F32 = jnp.float32
VMEM_LIMIT = 63 * 1024 * 1024
ANY = pl.BlockSpec(memory_space=pl.ANY)

SWAP = ((0, 1), (1, 0), (2, 3), (3, 2))
FAR = ((0, 2), (2, 0), (1, 3), (3, 1))
ACROSS = ((0, 3), (3, 0), (1, 2), (2, 1))
MIDDLE = ((1, 2), (2, 1))
OUTWARD = ((1, 0), (2, 3))


def params(**kw):
    return pltpu.CompilerParams(vmem_limit_bytes=VMEM_LIMIT, **kw)


def dot(left, right):
    return jnp.dot(left, right, preferred_element_type=F32)


def dot_nt(left, right):
    return lax.dot_general(left, right, (((1,), (1,)), ((), ())), preferred_element_type=F32)


def gelu_parts(u):
    cdf = 0.5 + 0.5 * lax.erf(u * 0.5**0.5)
    density = jnp.exp(-0.5 * (u * u)) * 0.3989422804014327
    return u * cdf, cdf + u * density


def head_mask(value, offset, head, size):
    lane = lax.broadcasted_iota(jnp.int32, value.shape, 1)
    keep = (lane >= offset + head * size) & (lane < offset + (head + 1) * size)
    return jnp.where(keep, value, jnp.zeros_like(value))


def load_rows(ids, pieces, scratch, sems):
    f = ids[0]
    rows = pieces[0].shape[0]
    copies = []
    for k, piece in enumerate(pieces):
        at = pl.multiple_of((f ^ k) * rows, rows)
        copies.append(pltpu.make_async_copy(piece, scratch.at[pl.ds(at, rows)], sems.at[k]))
    return copies


def qkv_kernel(ids, x_ref, w0, w1, w2, w3, b_ref, *refs, scale):
    q_ref, kv_ref, w_ref, sems = refs[-4:]

    @pl.when((pl.program_id(0) == 0) & (pl.program_id(1) == 0))
    def _():
        copies = load_rows(ids, (w0, w1, w2, w3), w_ref, sems)
        for c in copies:
            c.start()
        for c in copies:
            c.wait()

    width = q_ref.shape[1]
    out = dot(x_ref[0], w_ref[...]) + b_ref[...]
    query = out[:, :width].astype(BF)
    q_ref[...] = (query.astype(F32) * scale).astype(BF)
    kv_ref[...] = out[:, 256:].astype(BF)


def qkv_call(ids, hidden, first, count, pieces, bias, width, scale, after):
    _, rows, d = hidden.shape
    cols = pieces[0].shape[1]
    tile = min(rows, 256)
    tiles = rows // tile
    flat = lambda i, j, s: (i * tiles + j, 0)
    fixed = lambda i, j, s: (0, 0)
    return pl.pallas_call(
        functools.partial(qkv_kernel, scale=scale),
        out_shape=(
            jax.ShapeDtypeStruct((count * rows, width), BF),
            jax.ShapeDtypeStruct((count * rows, 2 * width), BF),
            jax.ShapeDtypeStruct((d, cols), BF),
        ),
        grid_spec=pltpu.PrefetchScalarGridSpec(
            num_scalar_prefetch=1,
            grid=(count, tiles),
            in_specs=[pl.BlockSpec((1, tile, d), lambda i, j, s: (first + i, j, 0))]
            + [ANY] * 4
            + [pl.BlockSpec((1, cols), fixed)]
            + [ANY] * len(after),
            out_specs=[
                pl.BlockSpec((tile, width), flat),
                pl.BlockSpec((tile, 2 * width), flat),
                pl.BlockSpec((d, cols), fixed),
            ],
            scratch_shapes=[pltpu.SemaphoreType.DMA((4,))],
        ),
        compiler_params=params(),
        cost_estimate=pl.CostEstimate(
            flops=2 * count * rows * d * cols,
            bytes_accessed=2 * (count * rows + d) * (d + cols),
            transcendentals=0,
        ),
        name="qkv",
    )(ids, hidden, *pieces, bias, *after)


FRAME = 64


def spread_heads(ids, kv_refs, k3, v3, heads, size):
    width = heads * size
    if len(kv_refs) == 2:
        low, own = kv_refs
        rows = own.shape[0]
        own_v = own[...]
        parts = ((0, jnp.where(ids[1] == 0, own_v, low[...])), (rows, own_v))
    else:
        parts = ((0, kv_refs[0][...]),)
    for at, part in parts:
        keys, values = part[:, :width], part[:, 2 * width - 256 :]
        lane = lax.broadcasted_iota(jnp.int32, values.shape, 1)
        for h in range(heads):
            k3[h, at : at + part.shape[0], :] = head_mask(keys, 0, h, size)
            ones = (lane >= 2 * h) & (lane < 2 * h + 2)
            masked = head_mask(values, FRAME, h, size)
            v3[h, at : at + part.shape[0], :] = jnp.where(ones, jnp.ones_like(masked), masked)


def attn_fwd_kernel(ids, *refs, heads, size, nkv):
    q_ref, prev_ref = refs[0], refs[1]
    kv_refs = refs[2 : 2 + nkv]
    bias_ref = refs[2 + nkv]
    log_ref, e_ref, att_ref, sum_ref, k3, v3 = refs[-6:]
    i, rb = pl.program_id(0), pl.program_id(1)
    full = prev_ref.shape[3]
    blocks = (att_ref.shape[0] - bias_ref.shape[0]) // BLOCK
    width = heads * size

    @pl.when(rb == 0)
    def _():
        spread_heads(ids, kv_refs, k3, v3, heads, size)
        att_ref[blocks * BLOCK :] = bias_ref[...]

    g = ids[1] * blocks + rb
    for b in range(full // BLOCK):
        n = (b + 1) * BLOCK

        @pl.when(g == b)
        def _(n=n):
            query = q_ref[...]
            total = None
            for h in range(heads):
                s = dot_nt(query, k3[h, :n, :]) + prev_ref[0, h, :, :n].astype(F32)
                log_ref[0, h, :, :n] = s.astype(BF)
                if n < full:
                    log_ref[0, h, :, n:] = jnp.zeros((BLOCK, full - n), BF)
                e = jnp.exp(s - jnp.max(s, axis=1, keepdims=True)).astype(BF)
                e_ref[0, h, :, :n] = e
                part = dot(e, v3[h, :n, :])
                total = part if total is None else total + part
            inverse = 1.0 / total[:, : 2 * heads]
            sum_ref[...] = jnp.concatenate(
                [inverse, jnp.zeros((BLOCK, 128 - 2 * heads), F32)], axis=1
            )
            lane = lax.broadcasted_iota(jnp.int32, total.shape, 1)
            factor = jnp.zeros_like(total)
            for h in range(heads):
                factor = jnp.where(lane // size == h + 1, inverse[:, 2 * h : 2 * h + 1], factor)
            att = (total * factor)[:, FRAME:].astype(BF)
            at = pl.ds(pl.multiple_of(rb * BLOCK, BLOCK), BLOCK)
            for k in range(att_ref.shape[1] // width):

                @pl.when(i == k)
                def _(k=k):
                    att_ref[at, k * width : (k + 1) * width] = att


def kv_specs(kvs, count):
    specs = []
    for kv in kvs:
        block = (kv.shape[0] // count, kv.shape[1])
        specs.append(pl.BlockSpec(block, lambda i, r, s: (i, 0)))
    return specs


def attn_fwd_call(ids, q, kvs, prev, bias, first, count, chain, heads, size, after):
    seqs, _, rows, full = prev.shape
    width = heads * size
    blocks = rows // BLOCK
    big = pl.BlockSpec((1, heads, BLOCK, full), lambda i, r, s: (first + i, 0, r, 0))
    extra = ([] if chain is None else [chain]) + list(after)
    tokens = 3 * full // 4
    return pl.pallas_call(
        functools.partial(attn_fwd_kernel, heads=heads, size=size, nkv=len(kvs)),
        out_shape=(
            jax.ShapeDtypeStruct(prev.shape, BF),
            jax.ShapeDtypeStruct((count, heads, rows, full), BF),
            jax.ShapeDtypeStruct((rows + bias.shape[0], count * width), BF),
            jax.ShapeDtypeStruct((count * rows, 128), F32),
        ),
        grid_spec=pltpu.PrefetchScalarGridSpec(
            num_scalar_prefetch=1,
            grid=(count, blocks),
            in_specs=[pl.BlockSpec((BLOCK, width), lambda i, r, s: (i * blocks + r, 0)), big]
            + kv_specs(kvs, count)
            + [pl.BlockSpec(bias.shape, lambda i, r, s: (0, 0))]
            + [ANY] * len(extra),
            out_specs=[
                big,
                pl.BlockSpec((1, heads, BLOCK, full), lambda i, r, s: (i, 0, r, 0)),
                pl.BlockSpec((rows + bias.shape[0], count * width), lambda i, r, s: (0, 0)),
                pl.BlockSpec((BLOCK, 128), lambda i, r, s: (i * blocks + r, 0)),
            ],
            scratch_shapes=[
                pltpu.VMEM((heads, full, width), BF),
                pltpu.VMEM((heads, full, 256), BF),
            ],
        ),
        input_output_aliases={} if chain is None else {4 + len(kvs): 0},
        compiler_params=params(),
        cost_estimate=pl.CostEstimate(
            flops=4 * 4 * count * heads * rows * tokens * size,
            bytes_accessed=6 * count * heads * rows * full,
            transcendentals=count * heads * rows * tokens,
        ),
        name="attn_fwd",
    )(ids, q, prev, *kvs, bias, *extra)


def attn_bwd_kernel(ids, *refs, heads, size, nkv, local, scale):
    q_ref, e_ref, dl_ref, datt_ref, att_ref, sum_ref = refs[:6]
    kv_refs = refs[6 : 6 + nkv]
    if nkv == 2:
        dprev_ref, dq_ref, own_ref, send_ref, k3, v3, dkv_t = refs[-7:]
    else:
        dprev_ref, dq_ref, own_ref, k3, v3, dkv_t = refs[-6:]
    i, rb = pl.program_id(0), pl.program_id(1)
    blocks = pl.num_programs(1)
    full = dl_ref.shape[3]
    width = heads * size

    @pl.when(rb == 0)
    def _():
        spread_heads(ids, kv_refs, k3, v3, heads, size)
        dkv_t[...] = jnp.zeros_like(dkv_t)

    g = ids[1] * blocks + rb
    for b in range(full // BLOCK):
        n = (b + 1) * BLOCK

        @pl.when(g == b)
        def _(n=n):
            datt = datt_ref[...].astype(F32)
            att = att_ref[:, local * width : (local + 1) * width]
            if att_ref.shape[1] > (local + 1) * width:
                att = jnp.where(i == 0, att, att_ref[:, (local + 1) * width :])
            weighted = datt * att.astype(F32)
            lane = lax.broadcasted_iota(jnp.int32, datt.shape, 1)
            head = lax.broadcasted_iota(jnp.int32, (BLOCK, FRAME), 1)
            factor = jnp.zeros_like(datt)
            front = jnp.zeros((BLOCK, FRAME), F32)
            for h in range(heads):
                inverse = sum_ref[:, 2 * h : 2 * h + 1]
                factor = jnp.where(lane // size == h, inverse, factor)
                delta = jnp.sum(head_mask(weighted, 0, h, size), axis=1, keepdims=True)
                delta = -delta * inverse
                high = delta.astype(BF).astype(F32)
                front = jnp.where(head == 2 * h, high, front)
                front = jnp.where(head == 2 * h + 1, delta - high, front)
            scaled = (datt * factor).astype(BF)
            framed = jnp.concatenate([front.astype(BF), scaled], axis=1)
            q_t = q_ref[...].T
            scaled_t = scaled.T
            total = None
            for h in range(heads):
                at = h * size
                dp = dot_nt(framed, v3[h, :n, :])
                e = e_ref[0, h, :, :n]
                ds = e.astype(F32) * dp + dl_ref[0, h, :, :n].astype(F32)
                low = ds.astype(BF)
                dprev_ref[0, h, :, :n] = low
                if n < full:
                    dprev_ref[0, h, :, n:] = jnp.zeros((BLOCK, full - n), BF)
                part = dot(low, k3[h, :n, :])
                total = part if total is None else total + part
                dkv_t[at : at + size, :n] += dot(q_t[at : at + size], low)
                at += width
                dkv_t[at : at + size, :n] += dot(scaled_t[at - width : at - width + size], e)
            dq_ref[...] = (total * scale).astype(BF)

    @pl.when(rb == blocks - 1)
    def _():
        if nkv == 2:
            rows = full // 2

            @pl.when(ids[1] == 0)
            def _():
                own_ref[...] = dkv_t[:, :rows].T.astype(BF)

            @pl.when(ids[1] == 1)
            def _():
                own_ref[...] = dkv_t[:, rows:].T.astype(BF)
                send_ref[...] = dkv_t[:, :rows].T.astype(BF)
        else:
            own_ref[...] = dkv_t[...].T.astype(BF)


def attn_bwd_call(
    ids, q, e, d_logits, datt, att, inverse, kvs, first, base, count, of, chain, heads, size, scale, after
):
    seqs, _, rows, full = d_logits.shape
    width = heads * size
    blocks = rows // BLOCK
    big = pl.BlockSpec((1, heads, BLOCK, full), lambda i, r, s: (first + i, 0, r, 0))
    extra = ([] if chain is None else [chain]) + list(after)
    tokens = 3 * full // 4
    tile = lambda w, k: pl.BlockSpec((BLOCK, w), lambda i, r, s: ((k + i) * blocks + r, 0))
    kv_in = []
    for kv in kvs:
        block = (kv.shape[0] // of, kv.shape[1])
        kv_in.append(pl.BlockSpec(block, lambda i, r, s: (base + i, 0)))
    grads = [(rows, rows)] if len(kvs) == 2 else [(full,)]
    sizes = grads[0]
    return pl.pallas_call(
        functools.partial(
            attn_bwd_kernel, heads=heads, size=size, nkv=len(kvs), local=base, scale=scale
        ),
        out_shape=(
            jax.ShapeDtypeStruct(d_logits.shape, BF),
            jax.ShapeDtypeStruct((count * rows, width), BF),
        )
        + tuple(jax.ShapeDtypeStruct((count * z, 2 * width), BF) for z in sizes),
        grid_spec=pltpu.PrefetchScalarGridSpec(
            num_scalar_prefetch=1,
            grid=(count, blocks),
            in_specs=[
                tile(width, base),
                pl.BlockSpec((1, heads, BLOCK, full), lambda i, r, s: (base + i, 0, r, 0)),
                big,
                tile(width, base),
                pl.BlockSpec((BLOCK, of * width), lambda i, r, s: (r, 0)),
                tile(128, base),
            ]
            + kv_in
            + [ANY] * len(extra),
            out_specs=[big, tile(width, 0)]
            + [pl.BlockSpec((z, 2 * width), lambda i, r, s: (i, 0)) for z in sizes],
            scratch_shapes=[
                pltpu.VMEM((heads, full, width), BF),
                pltpu.VMEM((heads, full, 256), BF),
                pltpu.VMEM((2 * width, full), F32),
            ],
        ),
        input_output_aliases={} if chain is None else {7 + len(kvs): 0},
        compiler_params=params(),
        cost_estimate=pl.CostEstimate(flops=9000000000, bytes_accessed=1000, transcendentals=0),
        name="attn_bwd",
    )(ids, q, e, d_logits, datt, att, inverse, *kvs, *extra)


def row_mean(value):
    return jnp.mean(value, axis=1, keepdims=True)


def col_sum(value):
    return jnp.sum(value, axis=0, keepdims=True)


def ffn_kernel(ids, *refs, chained, final, base, width, units):
    x_ref, a0, a1, a2, a3, do_ref, vec_ref, b0, b1, b2, b3 = refs[:11]
    pieces = refs[11:15]
    if chained:
        gi_in, go_in, gw_in = refs[15:18]
    if final:
        out_ref, dh1_ref, datt_ref, sum_ref, grad_ref = refs[-18:-13]
    else:
        out_ref, dh1_ref, datt_ref, sum_ref, gi_hbm, go_hbm, gw_hbm = refs[-20:-13]
    wi, wo, wa, act_s, gp_s, din_s, att_s, gi, go, gw, bin_s, w_sem, g_sem = refs[-13:]
    i, j = pl.program_id(0), pl.program_id(1)
    start = (i == 0) & (j == 0)
    last = (i == pl.num_programs(0) - 1) & (j == pl.num_programs(1) - 1)
    rank = ids[2]
    rows = pieces[0].shape[1]

    def copies(group):
        out = []
        for k in range(4):
            at = pl.ds(pl.multiple_of((ids[0] ^ k) * rows, rows), rows)
            for slot in range(4):
                piece = pieces[k].at[slot]
                sem = w_sem.at[group, k * 4 + slot]
                if group == 0:
                    src, dst = piece.at[:, 2 * units : 2 * units + width], wa
                elif group == 1:
                    src, dst = piece.at[:, :units], wi
                else:
                    src, dst = piece.at[:, units : 2 * units], wo
                dst = dst.at[rank ^ slot, at]
                out.append(pltpu.make_async_copy(src, dst, sem))
        return out

    def grad_in():
        return [
            pltpu.make_async_copy(src, dst, g_sem.at[k])
            for k, (src, dst) in enumerate(((gi_in, gi), (go_in, go), (gw_in, gw)))
        ]

    @pl.when(start)
    def _():
        for group in range(3):
            for c in copies(group):
                c.start()
        if chained:
            for c in grad_in():
                c.start()
        else:
            gi[...] = jnp.zeros_like(gi)
            go[...] = jnp.zeros_like(go)
            gw[...] = jnp.zeros_like(gw)
        sum_ref[...] = jnp.zeros_like(sum_ref)
        for slot, b in enumerate((b0, b1, b2, b3)):
            value = b[...].astype(F32)
            left = value[0:1] + value[2:3] + value[4:5]
            right = value[1:2] + value[3:4] + value[5:6]
            bin_s[rank ^ slot] = jnp.concatenate([left, right], axis=1)
        for c in copies(0):
            c.wait()

    chunk = a0.shape[1] // width
    b_out, gain_a, shift_a = vec_ref[0:1], vec_ref[1:2], vec_ref[2:3]
    b_outer, gain_f, shift_f = vec_ref[3:4], vec_ref[4:5], vec_ref[5:6]
    half = x_ref.shape[1] // 2
    parts = [slice(0, half), slice(half, 2 * half)]
    n1, r1, normed, n2, r2 = [None] * 2, [None] * 2, [None] * 2, [None] * 2, [None] * 2
    h2, dn, dh2_low, dh1_low = [None] * 2, [None] * 2, [None] * 2, [None] * 2

    for p in range(2):
        for slot, a in enumerate((a0, a1, a2, a3)):
            value = a[parts[p], base * width : (base + 1) * width]
            if chunk > base + 1:
                value = jnp.where(i == 0, value, a[parts[p], (base + 1) * width :])
            att_s[rank ^ slot, parts[p]] = value
    for p in range(2):
        h1 = x_ref[0, parts[p]].astype(F32) + b_out
        for t in range(4):
            h1 = h1 + dot_nt(att_s[t, parts[p]], wa[t])
        c1 = h1 - row_mean(h1)
        r1[p] = lax.rsqrt(row_mean(c1 * c1) + EPS)
        n1[p] = c1 * r1[p]
        normed[p] = (n1[p] * gain_a + shift_a).astype(BF)

    @pl.when(start)
    def _():
        for c in copies(1):
            c.wait()
        for c in copies(2):
            c.wait()
        if chained:
            for c in grad_in():
                c.wait()

    def forward(p):
        h2[p] = normed[p].astype(F32) + b_outer
        for t in range(4):
            inner = dot(normed[p], wi[t]) + bin_s[t]
            act, slope = gelu_parts(inner)
            low = act.astype(BF)
            act_s[t, parts[p]] = low
            gp_s[t, parts[p]] = slope.astype(BF)
            h2[p] = h2[p] + dot_nt(low, wo[t])

    def turn(p):
        c2 = h2[p] - row_mean(h2[p])
        r2[p] = lax.rsqrt(row_mean(c2 * c2) + EPS)
        n2[p] = c2 * r2[p]
        out_ref[0, parts[p]] = (n2[p] * gain_f + shift_f).astype(BF)
        d_out = do_ref[0, parts[p]].astype(F32)
        e2 = d_out * gain_f
        dh2 = (e2 - row_mean(e2) - n2[p] * row_mean(e2 * n2[p])) * r2[p]
        sum_ref[3:4] += col_sum(dh2)
        sum_ref[4:5] += col_sum(d_out * n2[p])
        sum_ref[5:6] += col_sum(d_out)
        dh2_low[p] = dh2.astype(BF)
        dn[p] = dh2

    def backward(p):
        for t in range(4):
            din = dot(dh2_low[p], wo[t]) * gp_s[t, parts[p]].astype(F32)
            low = din.astype(BF)
            din_s[t, parts[p]] = low
            dn[p] = dn[p] + dot_nt(low, wi[t])

    def close(p):
        e1 = dn[p] * gain_a
        dh1 = (e1 - row_mean(e1) - n1[p] * row_mean(e1 * n1[p])) * r1[p]
        dh1_ref[parts[p]] = dh1
        dh1_low[p] = dh1.astype(BF)
        sum_ref[0:1] += col_sum(dh1)
        sum_ref[1:2] += col_sum(dn[p] * n1[p])
        sum_ref[2:3] += col_sum(dn[p])

    forward(0)
    turn(0)
    forward(1)
    backward(0)
    turn(1)
    close(0)
    backward(1)
    datt_ref[parts[0]] = dot(dh1_low[0], wa[rank]).astype(BF)
    close(1)
    gi[...] += dot(jnp.concatenate(normed, axis=0).T, din_s[rank])
    go[...] += dot(jnp.concatenate(dh2_low, axis=0).T, act_s[rank])
    datt_ref[parts[1]] = dot(dh1_low[1], wa[rank]).astype(BF)
    gw[...] += dot(jnp.concatenate(dh1_low, axis=0).T, att_s[rank])
    sum_ref[6:7] += col_sum(din_s[rank].astype(F32))

    @pl.when(last)
    def _():
        if final:
            grad_ref[:, :units] = gi[...].astype(BF)
            grad_ref[:, units : 2 * units] = go[...].astype(BF)
            grad_ref[:, 2 * units :] = gw[...].astype(BF)
        else:
            out = [
                pltpu.make_async_copy(src, dst, g_sem.at[k])
                for k, (src, dst) in enumerate(((gi, gi_hbm), (go, go_hbm), (gw, gw_hbm)))
            ]
            for c in out:
                c.start()
            for c in out:
                c.wait()


def ffn_call(
    ids, hidden, atts, d_output, vec, bias, weights, first, base, count, chain, width, units, final, after
):
    seqs, rows, d = hidden.shape
    tile = min(rows, 512)
    tiles = rows // tile
    chunk = atts[0].shape[1]
    whole = pl.BlockSpec((1, tile, d), lambda i, j, s: (first + i, j, 0))
    att = pl.BlockSpec((tile, chunk), lambda i, j, s: (j, 0))
    flat = lambda w: pl.BlockSpec((tile, w), lambda i, j, s: (i * tiles + j, 0))
    fixed = lambda shape: pl.BlockSpec(shape, lambda i, j, s: (0, 0))
    chained = [] if chain is None else list(chain)
    extra = chained + list(after)
    at = 1 + 11 + 4
    aliases = {}
    if chained:
        aliases = {at + 3: 0} if final else {at: 4, at + 1: 5, at + 2: 6, at + 3: 0}
    grads = (
        (jax.ShapeDtypeStruct((d, 2 * units + width), BF),)
        if final
        else (
            jax.ShapeDtypeStruct((d, units), F32),
            jax.ShapeDtypeStruct((d, units), F32),
            jax.ShapeDtypeStruct((d, width), F32),
        )
    )
    return pl.pallas_call(
        functools.partial(
            ffn_kernel, chained=bool(chained), final=final, base=base, width=width, units=units
        ),
        out_shape=(
            jax.ShapeDtypeStruct(hidden.shape, BF),
            jax.ShapeDtypeStruct((count * rows, d), F32),
            jax.ShapeDtypeStruct((count * rows, width), BF),
            jax.ShapeDtypeStruct((8, d), F32),
        )
        + grads,
        grid_spec=pltpu.PrefetchScalarGridSpec(
            num_scalar_prefetch=1,
            grid=(count, tiles),
            in_specs=[whole, att, att, att, att, whole, fixed((8, d))]
            + [pl.BlockSpec((16, chunk), lambda i, j, s: (rows // 16, 0))] * 4
            + [ANY] * (4 + len(extra)),
            out_specs=[whole, flat(d), flat(width), fixed((8, d))]
            + ([fixed((d, 2 * units + width))] if final else [ANY] * 3),
            scratch_shapes=[
                pltpu.VMEM((4, d, units), BF),
                pltpu.VMEM((4, d, units), BF),
                pltpu.VMEM((4, d, width), BF),
                pltpu.VMEM((4, tile, units), BF),
                pltpu.VMEM((4, tile, units), BF),
                pltpu.VMEM((4, tile, units), BF),
                pltpu.VMEM((4, tile, width), BF),
                pltpu.VMEM((d, units), F32),
                pltpu.VMEM((d, units), F32),
                pltpu.VMEM((d, width), F32),
                pltpu.VMEM((4, 1, units), F32),
                pltpu.SemaphoreType.DMA((3, 16)),
                pltpu.SemaphoreType.DMA((3,)),
            ],
        ),
        input_output_aliases=aliases,
        compiler_params=params(),
        cost_estimate=pl.CostEstimate(
            flops=2 * count * rows * d * units * 20,
            bytes_accessed=16 * d * units + 16 * count * rows * d,
            transcendentals=8 * count * rows * units,
        ),
        name="ffn",
    )(ids, hidden, *atts, d_output, vec, *bias, *weights, *extra)


def dx_kernel(ids, dq_ref, *refs, nkv):
    dkv_refs = refs[:nkv]
    w_ref = refs[nkv]
    y_ref, joined_ref, sum_ref = refs[-3:]
    dq = dq_ref[...]
    dkv = dkv_refs[0][...]
    if nkv == 2:
        dkv = (dkv.astype(F32) + dkv_refs[1][...].astype(F32)).astype(BF)
    pad = jnp.zeros((dq.shape[0], 256 - dq.shape[1]), BF)
    joined = jnp.concatenate([dq, pad, dkv], axis=1)
    joined_ref[...] = joined

    @pl.when(pl.program_id(0) == 0)
    def _():
        sum_ref[...] = jnp.zeros_like(sum_ref)

    sum_ref[0:1] += col_sum(joined.astype(F32))
    y_ref[...] = dot_nt(joined, w_ref[...]).astype(BF)


def dx_call(ids, dq, dkvs, weight, first, tokens, chain, after):
    count = dq.shape[0]
    d, cols = weight.shape
    tile = min(count, 256)
    offset = first // tile
    flat = lambda w: pl.BlockSpec((tile, w), lambda i, s: (i, 0))
    extra = ([] if chain is None else [chain]) + list(after)
    return pl.pallas_call(
        functools.partial(dx_kernel, nkv=len(dkvs)),
        out_shape=(
            jax.ShapeDtypeStruct((count, d), BF),
            jax.ShapeDtypeStruct((tokens, cols), BF),
            jax.ShapeDtypeStruct((8, cols), F32),
        ),
        grid_spec=pltpu.PrefetchScalarGridSpec(
            num_scalar_prefetch=1,
            grid=(count // tile,),
            in_specs=[flat(dq.shape[1])]
            + [flat(v.shape[1]) for v in dkvs]
            + [pl.BlockSpec((d, cols), lambda i, s: (0, 0))]
            + [ANY] * len(extra),
            out_specs=[
                flat(d),
                pl.BlockSpec((tile, cols), lambda i, s: (offset + i, 0)),
                pl.BlockSpec((8, cols), lambda i, s: (0, 0)),
            ],
        ),
        input_output_aliases={} if chain is None else {3 + len(dkvs): 1},
        compiler_params=params(),
        cost_estimate=pl.CostEstimate(flops=3000000000, bytes_accessed=1000, transcendentals=0),
        name="dx",
    )(ids, dq, *dkvs, weight, *extra)


def grad_kernel(x_ref, joined_ref, *refs):
    g_ref, acc = refs[-2:]
    i = pl.program_id(0)

    @pl.when(i == 0)
    def _():
        acc[...] = jnp.zeros_like(acc)

    joined = joined_ref[...]
    acc[...] += dot(x_ref[0].T, joined)

    @pl.when(i == pl.num_programs(0) - 1)
    def _():
        g_ref[...] = acc[...].astype(BF)


def grad_call(hidden, joined, after):
    seqs, rows, d = hidden.shape
    cols = joined.shape[1]
    fixed = lambda shape: pl.BlockSpec(shape, lambda i: (0, 0))
    return pl.pallas_call(
        grad_kernel,
        out_shape=jax.ShapeDtypeStruct((d, cols), BF),
        grid=(seqs,),
        in_specs=[
            pl.BlockSpec((1, rows, d), lambda i: (i, 0, 0)),
            pl.BlockSpec((rows, cols), lambda i: (i, 0)),
        ]
        + [ANY] * len(after),
        out_specs=fixed((d, cols)),
        scratch_shapes=[pltpu.VMEM((d, cols), F32)],
        compiler_params=params(),
        cost_estimate=pl.CostEstimate(
            flops=2 * seqs * rows * d * cols, bytes_accessed=4 * d * cols, transcendentals=0
        ),
        name="grad",
    )(hidden, joined, *after)


def final_kernel(ids, dh1_ref, done_ref, other_ref, *refs):
    out_ref = refs[-1]
    upper = pl.program_id(0) == 0
    odd = lax.rem(ids[2], 2) == 1
    own = upper != odd
    both = jnp.where(own, done_ref[...].astype(F32), other_ref[...].astype(F32))
    out_ref[0] = dh1_ref[...] + both


def plain_kernel(dh1_ref, total_ref, *refs):
    refs[-1][0] = dh1_ref[...] + total_ref[...].astype(F32)


def plain_call(dh1, at, total, first, rows, seqs, chain, after):
    d = total.shape[1]
    tile = min(rows, 256)
    extra = ([] if chain is None else [chain]) + list(after)
    return pl.pallas_call(
        plain_kernel,
        out_shape=jax.ShapeDtypeStruct((seqs, rows, d), F32),
        grid=(rows // tile,),
        in_specs=[
            pl.BlockSpec((tile, d), lambda j: (at // tile + j, 0)),
            pl.BlockSpec((tile, d), lambda j: (j, 0)),
        ]
        + [ANY] * len(extra),
        out_specs=pl.BlockSpec((1, tile, d), lambda j: (first, j, 0)),
        input_output_aliases={} if chain is None else {2: 0},
        compiler_params=params(),
        cost_estimate=pl.CostEstimate(
            flops=2 * rows * d, bytes_accessed=10 * rows * d, transcendentals=0
        ),
        name="plain",
    )(dh1, total, *extra)


def final_call(ids, dh1, at, done, other, first, rows, seqs, chain, after):
    half, d = done.shape
    tile = min(half, 256)
    per_half = half // tile
    per_seq = rows // tile
    extra = ([] if chain is None else [chain]) + list(after)
    part = pl.BlockSpec((tile, d), lambda h, j, s: (j, 0))
    flat = lambda h, j: h * per_half + j
    return pl.pallas_call(
        final_kernel,
        out_shape=jax.ShapeDtypeStruct((seqs, rows, d), F32),
        grid_spec=pltpu.PrefetchScalarGridSpec(
            num_scalar_prefetch=1,
            grid=(2, per_half),
            in_specs=[
                pl.BlockSpec((tile, d), lambda h, j, s: (at // tile + flat(h, j), 0)),
                part,
                part,
            ]
            + [ANY] * len(extra),
            out_specs=pl.BlockSpec(
                (1, tile, d),
                lambda h, j, s: (first + flat(h, j) // per_seq, flat(h, j) % per_seq, 0),
            ),
        ),
        input_output_aliases={} if chain is None else {4: 0},
        compiler_params=params(),
        cost_estimate=pl.CostEstimate(
            flops=4 * half * d, bytes_accessed=24 * half * d, transcendentals=0
        ),
        name="final",
    )(ids, dh1, done, other, *extra)


def tp_gather(value):
    return [value] + [lax.ppermute(value, "tp", p) for p in (SWAP, FAR, ACROSS)]


def fsdp_gather(value):
    far = lax.ppermute(value, "fsdp", FAR)
    near = lax.ppermute(value, "fsdp", SWAP)
    return value, near, far, lax.ppermute(far, "fsdp", SWAP)


def tp_reduce(value, odd):
    half = value.shape[0] // 2
    top, bottom = value[:half], value[half:]
    sent = jnp.where(odd, top, bottom)
    got = lax.ppermute(sent, "tp", SWAP)
    pair = jnp.where(odd, bottom, top) + got
    done = pair + lax.ppermute(pair, "tp", FAR)
    return sent, pair, done, lax.ppermute(done, "tp", SWAP)


def ctx_sum(value, size):
    if size == 2:
        return value + lax.ppermute(value, "ctx", ((0, 1), (1, 0)))
    return lax.psum(value, "ctx")


def fsdp_far_sum(value, f):
    rows = value.shape[0] // 4
    pairs = value.reshape(2, 2, rows, value.shape[1])
    mine = lax.dynamic_index_in_dim(pairs, f // 2, 0, keepdims=False)
    other = lax.dynamic_index_in_dim(pairs, 1 - f // 2, 0, keepdims=False)
    return mine + lax.ppermute(other, "fsdp", FAR)


def fsdp_near_sum(mine, f, size):
    own = lax.dynamic_index_in_dim(mine, f % 2, 0, keepdims=False)
    near = lax.dynamic_index_in_dim(mine, 1 - f % 2, 0, keepdims=False)
    own = own + lax.ppermute(near, "fsdp", SWAP)
    return ctx_sum(own, size).astype(F32)


def fsdp_direct_sum(value, f, size):
    rows = value.shape[0] // 4
    blocks = value.reshape(4, rows, value.shape[1])
    pick = lambda k: lax.dynamic_index_in_dim(blocks, f ^ k, 0, keepdims=False)
    total = pick(0).astype(F32)
    for k, pairs in ((1, SWAP), (2, FAR), (3, ACROSS)):
        total = total + lax.ppermute(pick(k), "fsdp", pairs).astype(F32)
    return ctx_sum(total.astype(BF), size).astype(F32)


def all_sum(value, size):
    value = value + lax.ppermute(value, "fsdp", SWAP)
    value = value + lax.ppermute(value, "fsdp", FAR)
    return ctx_sum(value, size)


def body(
    hidden_in,
    prev_logits,
    w_query,
    w_key,
    w_value,
    w_out,
    w_inner,
    w_outer,
    b_query,
    b_value,
    b_out,
    b_inner,
    b_outer,
    gain_attn,
    shift_attn,
    gain_ffn,
    shift_ffn,
    d_output,
    d_logits,
    *,
    ctx_size,
):
    seqs, rows, d = hidden_in.shape
    heads = prev_logits.shape[1]
    width = w_query.shape[1]
    units = w_inner.shape[1]
    size = width // heads
    scale = size**-0.5
    f, c, rank = lax.axis_index("fsdp"), lax.axis_index("ctx"), lax.axis_index("tp")
    ids = jnp.stack([f, c, rank]).astype(jnp.int32)
    odd = rank % 2 == 1

    ffn_local = jnp.concatenate([w_inner, w_outer, w_out], axis=1)
    qkv_local = jnp.concatenate(
        [w_query, jnp.zeros((w_query.shape[0], 256 - width), BF), w_key, w_value], axis=1
    )
    qkv_pieces = fsdp_gather(qkv_local)
    inner_rank = (rank == 1) | (rank == 2)
    w_near = lax.ppermute(ffn_local, "tp", SWAP)
    w_across = lax.ppermute(ffn_local, "tp", MIDDLE)
    far = lambda value: lax.ppermute(value, "fsdp", FAR)
    own_local, _ = lax.optimization_barrier((ffn_local, qkv_pieces[2]))
    w_far = [far(own_local)]
    qkv_bias = jnp.concatenate([b_query, jnp.zeros((256,), F32), b_value])[None]
    vec = jnp.stack([b_out, gain_attn, shift_attn, b_outer, gain_ffn, shift_ffn, b_out, b_out])

    chunk = 2
    starts = range(0, seqs, chunk)
    queries, kvs, after = [], [], []
    for s in starts:
        q, kv, w_qkv = qkv_call(
            ids, hidden_in, s, chunk, qkv_pieces, qkv_bias, width, scale, after
        )
        after = [q]
        if s == 0:
            w_near, w_across, w_far[0], _ = lax.optimization_barrier(
                (w_near, w_across, w_far[0], q)
            )
            w_far.append(far(w_near))
            w_middle = lax.ppermute(w_near, "tp", MIDDLE)
            w_out_a = lax.ppermute(w_across, "tp", OUTWARD)
        queries.append(q)
        if ctx_size == 2:
            kvs.append((lax.ppermute(kv, "ctx", ((0, 1),)), kv))
        else:
            got = lax.all_gather(kv.reshape(chunk, rows, 2 * width), "ctx", axis=1, tiled=True)
            kvs.append((got.reshape(-1, 2 * width),))

    w_two = jnp.where(inner_rank, w_middle, w_out_a)
    w_far.append(far(w_two))
    w_out_b = lax.ppermute(w_middle, "tp", OUTWARD)
    after = after + [w_two]
    high = lax.reduce_precision(b_inner, 8, 7)
    middle = lax.reduce_precision(b_inner - high, 8, 7)
    parts = jnp.stack([high, middle, b_inner - high - middle]).reshape(6, units // 2)
    bias = jnp.pad(parts.astype(BF), ((0, 10), (0, 0)))
    logits, probs, atts, inverses = None, [], [], []
    for k, s in enumerate(starts):
        logits, e, att, inverse = attn_fwd_call(
            ids, queries[k], kvs[k], prev_logits, bias, s, chunk, logits, heads, size, after
        )
        after = [att]
        probs.append(e)
        if k == 0:
            atts.append(tp_gather(att))
        else:
            every = lax.all_gather(att, "tp", axis=0, tiled=False)
            atts.append([att] + [
                lax.dynamic_index_in_dim(every, rank ^ slot, 0, keepdims=False)
                for slot in range(1, 4)
            ])
        inverses.append(inverse)
        if k == 0:
            w_out_b, _ = lax.optimization_barrier((w_out_b, att))
            w_three = jnp.where(inner_rank, w_across, w_out_b)
            w_far.append(far(w_three))
            w_here = jnp.stack([ffn_local, w_near, w_two, w_three])
            w_there = lax.ppermute(w_here, "fsdp", SWAP)
            after = after + [w_here]
        else:
            w_far, atts[0], _ = lax.optimization_barrier((w_far, atts[0], att))
            w_far = jnp.stack(w_far)
            weights = [w_here, w_there, w_far, lax.ppermute(w_far, "fsdp", SWAP)]

    chain, sums, qkv_sums, dh1s, datts = None, [], [], {}, {}
    d_prev, d_hidden, joined = None, None, None

    def ffn(s, count, after):
        nonlocal chain, grad_ffn, output
        k, base = s // chunk, s % chunk
        final = s + count == seqs
        out = ffn_call(
            ids,
            hidden_in,
            atts[k],
            d_output,
            vec,
            atts[0],
            weights,
            s,
            base,
            count,
            chain,
            width,
            units,
            final,
            after,
        )
        output, dh1s[s], datts[s], part = out[:4]
        sums.append(part)
        if final:
            grad_ffn = out[4]
        else:
            chain = (out[4], out[5], out[6], output)
        return [datts[s]]

    def attn_bwd(s, count, after):
        nonlocal d_prev
        k, base = s // chunk, s % chunk
        out = attn_bwd_call(
            ids,
            queries[k],
            probs[k],
            d_logits,
            datts[k * chunk],
            atts[k][0],
            inverses[k],
            kvs[k],
            s,
            base,
            count,
            chunk,
            d_prev,
            heads,
            size,
            scale,
            after,
        )
        d_prev, dq = out[:2]
        if ctx_size == 2:
            dkvs = (out[2], lax.ppermute(out[3], "ctx", ((1, 0),)))
        else:
            full_grad = out[2].reshape(count, -1, 2 * width)
            part = lax.psum_scatter(full_grad, "ctx", scatter_dimension=1, tiled=True)
            dkvs = (part.reshape(-1, 2 * width),)
        return (dq, dkvs), [dq]

    def dx(s, grads, after):
        nonlocal joined
        y, joined, part = dx_call(
            ids, grads[0], grads[1], w_qkv, s * rows, seqs * rows, joined, after
        )
        qkv_sums.append(part)
        return y, [y]

    def finish(s, after):
        nonlocal d_hidden
        k, at = s // chunk, (s % chunk) * rows
        if not isinstance(reduced[s], tuple):
            d_hidden = plain_call(
                dh1s[k * chunk], at, reduced[s], s, rows, seqs, d_hidden, after
            )
            return [d_hidden]
        _, _, done, other = reduced[s]
        d_hidden = final_call(
            ids, dh1s[k * chunk], at, done, other, s, rows, seqs, d_hidden, after
        )
        return [d_hidden]

    grad_ffn = output = None
    held, reduced = {}, {}
    ys, ffn_far = {}, None
    for s in starts:
        after = ffn(s, chunk, after)
        last = s + chunk == seqs
        if last:
            ffn_far = fsdp_far_sum(grad_ffn, f)
        if not last:
            for i in range(s, s + chunk):
                held[i], after = attn_bwd(i, 1, after)
        for i in range(s, s + chunk):
            if last:
                extra = [reduced[0], reduced[1][1]] if i == s else []
                held[i], after = attn_bwd(i, 1, after + extra)
                finish(i - s, after)
                after = after + [d_hidden, reduced[i - 1][1 if i > s else 2]]
            ys[i], after = dx(i, held[i], after)
            if i == 0:
                reduced[i] = lax.psum(ys[i], "tp")
            else:
                reduced[i] = tp_reduce(ys[i], odd)
    after = after + [reduced[seqs - 1][1]]
    g_qkv = grad_call(hidden_in, joined, after)
    for s in range(seqs - chunk, seqs):
        finish(s, [g_qkv])

    small = jnp.concatenate([functools.reduce(jnp.add, sums), functools.reduce(jnp.add, qkv_sums)], axis=1)
    g_ffn = fsdp_near_sum(ffn_far, f, ctx_size)
    g_qkv, g_ffn = lax.optimization_barrier((g_qkv, g_ffn))
    g_qkv = fsdp_direct_sum(g_qkv, f, ctx_size)
    small, _ = lax.optimization_barrier((small, reduced[seqs - 2][2]))
    small = all_sum(small, ctx_size)
    return (
        output,
        logits,
        d_hidden,
        d_prev,
        g_qkv[:, :width],
        g_qkv[:, 256 : 256 + width],
        g_qkv[:, 256 + width :],
        g_ffn[:, 2 * units :],
        g_ffn[:, :units],
        g_ffn[:, units : 2 * units],
        small[0, d : d + width],
        small[0, d + 256 + width :],
        small[0, :d],
        small[6, :d],
        small[3, :d],
        small[1, :d],
        small[2, :d],
        small[4, :d],
        small[5, :d],
    )


def solution(mesh):
    tok, lgt, mat = P("fsdp", "ctx", None), P("fsdp", "tp", "ctx", None), P("fsdp", "tp")
    vec, rep = P("tp"), P()
    in_specs = (tok, lgt) + (mat,) * 6 + (vec, vec, rep, vec) + (rep,) * 5 + (tok, lgt)
    out_specs = (tok, lgt, tok, lgt) + (mat,) * 6 + (vec, vec, rep, vec) + (rep,) * 5
    return jax.shard_map(
        functools.partial(body, ctx_size=mesh.shape["ctx"]),
        mesh=mesh,
        in_specs=in_specs,
        out_specs=out_specs,
        check_vma=False,
    )
```

```python
import functools

import jax
import jax.numpy as jnp
from jax import lax
from jax.experimental import pallas as pl
from jax.experimental.pallas import tpu as pltpu
from jax.sharding import PartitionSpec as P

BLOCK = 256
EPS = 1e-6
BF = jnp.bfloat16
F32 = jnp.float32
VMEM_LIMIT = 63 * 1024 * 1024
ANY = pl.BlockSpec(memory_space=pl.ANY)

SWAP = ((0, 1), (1, 0), (2, 3), (3, 2))
FAR = ((0, 2), (2, 0), (1, 3), (3, 1))
ACROSS = ((0, 3), (3, 0), (1, 2), (2, 1))
MIDDLE = ((1, 2), (2, 1))
OUTWARD = ((1, 0), (2, 3))


def params(**kw):
    return pltpu.CompilerParams(vmem_limit_bytes=VMEM_LIMIT, **kw)


def dot(left, right):
    return jnp.dot(left, right, preferred_element_type=F32)


def dot_nt(left, right):
    return lax.dot_general(left, right, (((1,), (1,)), ((), ())), preferred_element_type=F32)


def gelu_parts(u):
    cdf = 0.5 + 0.5 * lax.erf(u * 0.5**0.5)
    density = jnp.exp(-0.5 * (u * u)) * 0.3989422804014327
    return u * cdf, cdf + u * density


def head_mask(value, offset, head, size):
    lane = lax.broadcasted_iota(jnp.int32, value.shape, 1)
    keep = (lane >= offset + head * size) & (lane < offset + (head + 1) * size)
    return jnp.where(keep, value, jnp.zeros_like(value))


def load_rows(ids, pieces, scratch, sems):
    f = ids[0]
    rows = pieces[0].shape[0]
    copies = []
    for k, piece in enumerate(pieces):
        at = pl.multiple_of((f ^ k) * rows, rows)
        copies.append(pltpu.make_async_copy(piece, scratch.at[pl.ds(at, rows)], sems.at[k]))
    return copies


def qkv_kernel(ids, x_ref, w0, w1, w2, w3, b_ref, *refs, scale):
    q_ref, kv_ref, w_ref, sems = refs[-4:]

    @pl.when((pl.program_id(0) == 0) & (pl.program_id(1) == 0))
    def _():
        copies = load_rows(ids, (w0, w1, w2, w3), w_ref, sems)
        for c in copies:
            c.start()
        for c in copies:
            c.wait()

    width = q_ref.shape[1]
    out = dot(x_ref[0], w_ref[...]) + b_ref[...]
    query = out[:, :width].astype(BF)
    q_ref[...] = (query.astype(F32) * scale).astype(BF)
    kv_ref[...] = out[:, 256:].astype(BF)


def qkv_call(ids, hidden, first, count, pieces, bias, width, scale, after):
    _, rows, d = hidden.shape
    cols = pieces[0].shape[1]
    tile = min(rows, 256)
    tiles = rows // tile
    flat = lambda i, j, s: (i * tiles + j, 0)
    fixed = lambda i, j, s: (0, 0)
    return pl.pallas_call(
        functools.partial(qkv_kernel, scale=scale),
        out_shape=(
            jax.ShapeDtypeStruct((count * rows, width), BF),
            jax.ShapeDtypeStruct((count * rows, 2 * width), BF),
            jax.ShapeDtypeStruct((d, cols), BF),
        ),
        grid_spec=pltpu.PrefetchScalarGridSpec(
            num_scalar_prefetch=1,
            grid=(count, tiles),
            in_specs=[pl.BlockSpec((1, tile, d), lambda i, j, s: (first + i, j, 0))]
            + [ANY] * 4
            + [pl.BlockSpec((1, cols), fixed)]
            + [ANY] * len(after),
            out_specs=[
                pl.BlockSpec((tile, width), flat),
                pl.BlockSpec((tile, 2 * width), flat),
                pl.BlockSpec((d, cols), fixed),
            ],
            scratch_shapes=[pltpu.SemaphoreType.DMA((4,))],
        ),
        compiler_params=params(),
        cost_estimate=pl.CostEstimate(
            flops=2 * count * rows * d * cols,
            bytes_accessed=2 * (count * rows + d) * (d + cols),
            transcendentals=0,
        ),
        name="qkv",
    )(ids, hidden, *pieces, bias, *after)


FRAME = 64


def spread_heads(ids, kv_refs, k3, v3, heads, size):
    width = heads * size
    if len(kv_refs) == 2:
        low, own = kv_refs
        rows = own.shape[0]
        own_v = own[...]
        parts = ((0, jnp.where(ids[1] == 0, own_v, low[...])), (rows, own_v))
    else:
        parts = ((0, kv_refs[0][...]),)
    for at, part in parts:
        keys, values = part[:, :width], part[:, 2 * width - 256 :]
        lane = lax.broadcasted_iota(jnp.int32, values.shape, 1)
        for h in range(heads):
            k3[h, at : at + part.shape[0], :] = head_mask(keys, 0, h, size)
            ones = (lane >= 2 * h) & (lane < 2 * h + 2)
            masked = head_mask(values, FRAME, h, size)
            v3[h, at : at + part.shape[0], :] = jnp.where(ones, jnp.ones_like(masked), masked)


def attn_fwd_kernel(ids, *refs, heads, size, nkv):
    q_ref, prev_ref = refs[0], refs[1]
    kv_refs = refs[2 : 2 + nkv]
    bias_ref = refs[2 + nkv]
    log_ref, e_ref, att_ref, sum_ref, k3, v3 = refs[-6:]
    i, rb = pl.program_id(0), pl.program_id(1)
    full = prev_ref.shape[3]
    blocks = (att_ref.shape[0] - bias_ref.shape[0]) // BLOCK
    width = heads * size

    @pl.when(rb == 0)
    def _():
        spread_heads(ids, kv_refs, k3, v3, heads, size)
        att_ref[blocks * BLOCK :] = bias_ref[...]

    g = ids[1] * blocks + rb
    for b in range(full // BLOCK):
        n = (b + 1) * BLOCK

        @pl.when(g == b)
        def _(n=n):
            query = q_ref[...]
            total = None
            for h in range(heads):
                s = dot_nt(query, k3[h, :n, :]) + prev_ref[0, h, :, :n].astype(F32)
                log_ref[0, h, :, :n] = s.astype(BF)
                if n < full:
                    log_ref[0, h, :, n:] = jnp.zeros((BLOCK, full - n), BF)
                e = jnp.exp(s - jnp.max(s, axis=1, keepdims=True)).astype(BF)
                e_ref[0, h, :, :n] = e
                part = dot(e, v3[h, :n, :])
                total = part if total is None else total + part
            inverse = 1.0 / total[:, : 2 * heads]
            sum_ref[...] = jnp.concatenate(
                [inverse, jnp.zeros((BLOCK, 128 - 2 * heads), F32)], axis=1
            )
            lane = lax.broadcasted_iota(jnp.int32, total.shape, 1)
            factor = jnp.zeros_like(total)
            for h in range(heads):
                factor = jnp.where(lane // size == h + 1, inverse[:, 2 * h : 2 * h + 1], factor)
            att = (total * factor)[:, FRAME:].astype(BF)
            at = pl.ds(pl.multiple_of(rb * BLOCK, BLOCK), BLOCK)
            for k in range(att_ref.shape[1] // width):

                @pl.when(i == k)
                def _(k=k):
                    att_ref[at, k * width : (k + 1) * width] = att


def kv_specs(kvs, count):
    specs = []
    for kv in kvs:
        block = (kv.shape[0] // count, kv.shape[1])
        specs.append(pl.BlockSpec(block, lambda i, r, s: (i, 0)))
    return specs


def attn_fwd_call(ids, q, kvs, prev, bias, first, count, chain, heads, size, after):
    seqs, _, rows, full = prev.shape
    width = heads * size
    blocks = rows // BLOCK
    big = pl.BlockSpec((1, heads, BLOCK, full), lambda i, r, s: (first + i, 0, r, 0))
    extra = ([] if chain is None else [chain]) + list(after)
    tokens = 3 * full // 4
    return pl.pallas_call(
        functools.partial(attn_fwd_kernel, heads=heads, size=size, nkv=len(kvs)),
        out_shape=(
            jax.ShapeDtypeStruct(prev.shape, BF),
            jax.ShapeDtypeStruct((count, heads, rows, full), BF),
            jax.ShapeDtypeStruct((rows + bias.shape[0], count * width), BF),
            jax.ShapeDtypeStruct((count * rows, 128), F32),
        ),
        grid_spec=pltpu.PrefetchScalarGridSpec(
            num_scalar_prefetch=1,
            grid=(count, blocks),
            in_specs=[pl.BlockSpec((BLOCK, width), lambda i, r, s: (i * blocks + r, 0)), big]
            + kv_specs(kvs, count)
            + [pl.BlockSpec(bias.shape, lambda i, r, s: (0, 0))]
            + [ANY] * len(extra),
            out_specs=[
                big,
                pl.BlockSpec((1, heads, BLOCK, full), lambda i, r, s: (i, 0, r, 0)),
                pl.BlockSpec((rows + bias.shape[0], count * width), lambda i, r, s: (0, 0)),
                pl.BlockSpec((BLOCK, 128), lambda i, r, s: (i * blocks + r, 0)),
            ],
            scratch_shapes=[
                pltpu.VMEM((heads, full, width), BF),
                pltpu.VMEM((heads, full, 256), BF),
            ],
        ),
        input_output_aliases={} if chain is None else {4 + len(kvs): 0},
        compiler_params=params(),
        cost_estimate=pl.CostEstimate(
            flops=4 * 4 * count * heads * rows * tokens * size,
            bytes_accessed=6 * count * heads * rows * full,
            transcendentals=count * heads * rows * tokens,
        ),
        name="attn_fwd",
    )(ids, q, prev, *kvs, bias, *extra)


def attn_bwd_kernel(ids, *refs, heads, size, nkv, local, scale):
    q_ref, e_ref, dl_ref, datt_ref, att_ref, sum_ref = refs[:6]
    kv_refs = refs[6 : 6 + nkv]
    if nkv == 2:
        dprev_ref, dq_ref, own_ref, send_ref, k3, v3, dkv_t = refs[-7:]
    else:
        dprev_ref, dq_ref, own_ref, k3, v3, dkv_t = refs[-6:]
    i, rb = pl.program_id(0), pl.program_id(1)
    blocks = pl.num_programs(1)
    full = dl_ref.shape[3]
    width = heads * size

    @pl.when(rb == 0)
    def _():
        spread_heads(ids, kv_refs, k3, v3, heads, size)
        dkv_t[...] = jnp.zeros_like(dkv_t)

    g = ids[1] * blocks + rb
    for b in range(full // BLOCK):
        n = (b + 1) * BLOCK

        @pl.when(g == b)
        def _(n=n):
            datt = datt_ref[...].astype(F32)
            att = att_ref[:, local * width : (local + 1) * width]
            if att_ref.shape[1] > (local + 1) * width:
                att = jnp.where(i == 0, att, att_ref[:, (local + 1) * width :])
            weighted = datt * att.astype(F32)
            lane = lax.broadcasted_iota(jnp.int32, datt.shape, 1)
            head = lax.broadcasted_iota(jnp.int32, (BLOCK, FRAME), 1)
            factor = jnp.zeros_like(datt)
            front = jnp.zeros((BLOCK, FRAME), F32)
            for h in range(heads):
                inverse = sum_ref[:, 2 * h : 2 * h + 1]
                factor = jnp.where(lane // size == h, inverse, factor)
                delta = jnp.sum(head_mask(weighted, 0, h, size), axis=1, keepdims=True)
                delta = -delta * inverse
                high = delta.astype(BF).astype(F32)
                front = jnp.where(head == 2 * h, high, front)
                front = jnp.where(head == 2 * h + 1, delta - high, front)
            scaled = (datt * factor).astype(BF)
            framed = jnp.concatenate([front.astype(BF), scaled], axis=1)
            q_t = q_ref[...].T
            scaled_t = scaled.T
            total = None
            for h in range(heads):
                at = h * size
                dp = dot_nt(framed, v3[h, :n, :])
                e = e_ref[0, h, :, :n]
                ds = e.astype(F32) * dp + dl_ref[0, h, :, :n].astype(F32)
                low = ds.astype(BF)
                dprev_ref[0, h, :, :n] = low
                if n < full:
                    dprev_ref[0, h, :, n:] = jnp.zeros((BLOCK, full - n), BF)
                part = dot(low, k3[h, :n, :])
                total = part if total is None else total + part
                dkv_t[at : at + size, :n] += dot(q_t[at : at + size], low)
                at += width
                dkv_t[at : at + size, :n] += dot(scaled_t[at - width : at - width + size], e)
            dq_ref[...] = (total * scale).astype(BF)

    @pl.when(rb == blocks - 1)
    def _():
        if nkv == 2:
            rows = full // 2

            @pl.when(ids[1] == 0)
            def _():
                own_ref[...] = dkv_t[:, :rows].T.astype(BF)

            @pl.when(ids[1] == 1)
            def _():
                own_ref[...] = dkv_t[:, rows:].T.astype(BF)
                send_ref[...] = dkv_t[:, :rows].T.astype(BF)
        else:
            own_ref[...] = dkv_t[...].T.astype(BF)


def attn_bwd_call(
    ids, q, e, d_logits, datt, att, inverse, kvs, first, base, count, of, chain, heads, size, scale, after
):
    seqs, _, rows, full = d_logits.shape
    width = heads * size
    blocks = rows // BLOCK
    big = pl.BlockSpec((1, heads, BLOCK, full), lambda i, r, s: (first + i, 0, r, 0))
    extra = ([] if chain is None else [chain]) + list(after)
    tokens = 3 * full // 4
    tile = lambda w, k: pl.BlockSpec((BLOCK, w), lambda i, r, s: ((k + i) * blocks + r, 0))
    kv_in = []
    for kv in kvs:
        block = (kv.shape[0] // of, kv.shape[1])
        kv_in.append(pl.BlockSpec(block, lambda i, r, s: (base + i, 0)))
    grads = [(rows, rows)] if len(kvs) == 2 else [(full,)]
    sizes = grads[0]
    return pl.pallas_call(
        functools.partial(
            attn_bwd_kernel, heads=heads, size=size, nkv=len(kvs), local=base, scale=scale
        ),
        out_shape=(
            jax.ShapeDtypeStruct(d_logits.shape, BF),
            jax.ShapeDtypeStruct((count * rows, width), BF),
        )
        + tuple(jax.ShapeDtypeStruct((count * z, 2 * width), BF) for z in sizes),
        grid_spec=pltpu.PrefetchScalarGridSpec(
            num_scalar_prefetch=1,
            grid=(count, blocks),
            in_specs=[
                tile(width, base),
                pl.BlockSpec((1, heads, BLOCK, full), lambda i, r, s: (base + i, 0, r, 0)),
                big,
                tile(width, base),
                pl.BlockSpec((BLOCK, of * width), lambda i, r, s: (r, 0)),
                tile(128, base),
            ]
            + kv_in
            + [ANY] * len(extra),
            out_specs=[big, tile(width, 0)]
            + [pl.BlockSpec((z, 2 * width), lambda i, r, s: (i, 0)) for z in sizes],
            scratch_shapes=[
                pltpu.VMEM((heads, full, width), BF),
                pltpu.VMEM((heads, full, 256), BF),
                pltpu.VMEM((2 * width, full), F32),
            ],
        ),
        input_output_aliases={} if chain is None else {7 + len(kvs): 0},
        compiler_params=params(),
        cost_estimate=pl.CostEstimate(flops=9000000000, bytes_accessed=1000, transcendentals=0),
        name="attn_bwd",
    )(ids, q, e, d_logits, datt, att, inverse, *kvs, *extra)


def row_mean(value):
    return jnp.mean(value, axis=1, keepdims=True)


def col_sum(value):
    return jnp.sum(value, axis=0, keepdims=True)


def ffn_kernel(ids, *refs, chained, final, base, width, units):
    x_ref, a0, a1, a2, a3, do_ref, vec_ref, b0, b1, b2, b3 = refs[:11]
    pieces = refs[11:15]
    if chained:
        gi_in, go_in, gw_in = refs[15:18]
    if final:
        out_ref, dh1_ref, datt_ref, sum_ref, grad_ref = refs[-18:-13]
    else:
        out_ref, dh1_ref, datt_ref, sum_ref, gi_hbm, go_hbm, gw_hbm = refs[-20:-13]
    wi, wo, wa, act_s, gp_s, din_s, att_s, gi, go, gw, bin_s, w_sem, g_sem = refs[-13:]
    i, j = pl.program_id(0), pl.program_id(1)
    start = (i == 0) & (j == 0)
    last = (i == pl.num_programs(0) - 1) & (j == pl.num_programs(1) - 1)
    rank = ids[2]
    rows = pieces[0].shape[1]

    def copies(group):
        out = []
        for k in range(4):
            at = pl.ds(pl.multiple_of((ids[0] ^ k) * rows, rows), rows)
            for slot in range(4):
                piece = pieces[k].at[slot]
                sem = w_sem.at[group, k * 4 + slot]
                if group == 0:
                    src, dst = piece.at[:, 2 * units : 2 * units + width], wa
                elif group == 1:
                    src, dst = piece.at[:, :units], wi
                else:
                    src, dst = piece.at[:, units : 2 * units], wo
                dst = dst.at[rank ^ slot, at]
                out.append(pltpu.make_async_copy(src, dst, sem))
        return out

    def grad_in():
        return [
            pltpu.make_async_copy(src, dst, g_sem.at[k])
            for k, (src, dst) in enumerate(((gi_in, gi), (go_in, go), (gw_in, gw)))
        ]

    @pl.when(start)
    def _():
        for group in range(3):
            for c in copies(group):
                c.start()
        if chained:
            for c in grad_in():
                c.start()
        else:
            gi[...] = jnp.zeros_like(gi)
            go[...] = jnp.zeros_like(go)
            gw[...] = jnp.zeros_like(gw)
        sum_ref[...] = jnp.zeros_like(sum_ref)
        for slot, b in enumerate((b0, b1, b2, b3)):
            value = b[...].astype(F32)
            left = value[0:1] + value[2:3] + value[4:5]
            right = value[1:2] + value[3:4] + value[5:6]
            bin_s[rank ^ slot] = jnp.concatenate([left, right], axis=1)
        for c in copies(0):
            c.wait()

    chunk = a0.shape[1] // width
    b_out, gain_a, shift_a = vec_ref[0:1], vec_ref[1:2], vec_ref[2:3]
    b_outer, gain_f, shift_f = vec_ref[3:4], vec_ref[4:5], vec_ref[5:6]
    half = x_ref.shape[1] // 2
    parts = [slice(0, half), slice(half, 2 * half)]
    n1, r1, normed, n2, r2 = [None] * 2, [None] * 2, [None] * 2, [None] * 2, [None] * 2
    h2, dn, dh2_low, dh1_low = [None] * 2, [None] * 2, [None] * 2, [None] * 2

    for p in range(2):
        for slot, a in enumerate((a0, a1, a2, a3)):
            value = a[parts[p], base * width : (base + 1) * width]
            if chunk > base + 1:
                value = jnp.where(i == 0, value, a[parts[p], (base + 1) * width :])
            att_s[rank ^ slot, parts[p]] = value
    for p in range(2):
        h1 = x_ref[0, parts[p]].astype(F32) + b_out
        for t in range(4):
            h1 = h1 + dot_nt(att_s[t, parts[p]], wa[t])
        c1 = h1 - row_mean(h1)
        r1[p] = lax.rsqrt(row_mean(c1 * c1) + EPS)
        n1[p] = c1 * r1[p]
        normed[p] = (n1[p] * gain_a + shift_a).astype(BF)

    @pl.when(start)
    def _():
        for c in copies(1):
            c.wait()
        for c in copies(2):
            c.wait()
        if chained:
            for c in grad_in():
                c.wait()

    def forward(p):
        h2[p] = normed[p].astype(F32) + b_outer
        for t in range(4):
            inner = dot(normed[p], wi[t]) + bin_s[t]
            act, slope = gelu_parts(inner)
            low = act.astype(BF)
            act_s[t, parts[p]] = low
            gp_s[t, parts[p]] = slope.astype(BF)
            h2[p] = h2[p] + dot_nt(low, wo[t])

    def turn(p):
        c2 = h2[p] - row_mean(h2[p])
        r2[p] = lax.rsqrt(row_mean(c2 * c2) + EPS)
        n2[p] = c2 * r2[p]
        out_ref[0, parts[p]] = (n2[p] * gain_f + shift_f).astype(BF)
        d_out = do_ref[0, parts[p]].astype(F32)
        e2 = d_out * gain_f
        dh2 = (e2 - row_mean(e2) - n2[p] * row_mean(e2 * n2[p])) * r2[p]
        sum_ref[3:4] += col_sum(dh2)
        sum_ref[4:5] += col_sum(d_out * n2[p])
        sum_ref[5:6] += col_sum(d_out)
        dh2_low[p] = dh2.astype(BF)
        dn[p] = dh2

    def backward(p):
        for t in range(4):
            din = dot(dh2_low[p], wo[t]) * gp_s[t, parts[p]].astype(F32)
            low = din.astype(BF)
            din_s[t, parts[p]] = low
            dn[p] = dn[p] + dot_nt(low, wi[t])

    def close(p):
        e1 = dn[p] * gain_a
        dh1 = (e1 - row_mean(e1) - n1[p] * row_mean(e1 * n1[p])) * r1[p]
        dh1_ref[parts[p]] = dh1
        dh1_low[p] = dh1.astype(BF)
        sum_ref[0:1] += col_sum(dh1)
        sum_ref[1:2] += col_sum(dn[p] * n1[p])
        sum_ref[2:3] += col_sum(dn[p])

    forward(0)
    turn(0)
    forward(1)
    backward(0)
    turn(1)
    close(0)
    backward(1)
    datt_ref[parts[0]] = dot(dh1_low[0], wa[rank]).astype(BF)
    close(1)
    gi[...] += dot(jnp.concatenate(normed, axis=0).T, din_s[rank])
    go[...] += dot(jnp.concatenate(dh2_low, axis=0).T, act_s[rank])
    datt_ref[parts[1]] = dot(dh1_low[1], wa[rank]).astype(BF)
    gw[...] += dot(jnp.concatenate(dh1_low, axis=0).T, att_s[rank])
    sum_ref[6:7] += col_sum(din_s[rank].astype(F32))

    @pl.when(last)
    def _():
        if final:
            grad_ref[:, :units] = gi[...].astype(BF)
            grad_ref[:, units : 2 * units] = go[...].astype(BF)
            grad_ref[:, 2 * units :] = gw[...].astype(BF)
        else:
            out = [
                pltpu.make_async_copy(src, dst, g_sem.at[k])
                for k, (src, dst) in enumerate(((gi, gi_hbm), (go, go_hbm), (gw, gw_hbm)))
            ]
            for c in out:
                c.start()
            for c in out:
                c.wait()


def ffn_call(
    ids, hidden, atts, d_output, vec, bias, weights, first, base, count, chain, width, units, final, after
):
    seqs, rows, d = hidden.shape
    tile = min(rows, 512)
    tiles = rows // tile
    chunk = atts[0].shape[1]
    whole = pl.BlockSpec((1, tile, d), lambda i, j, s: (first + i, j, 0))
    att = pl.BlockSpec((tile, chunk), lambda i, j, s: (j, 0))
    flat = lambda w: pl.BlockSpec((tile, w), lambda i, j, s: (i * tiles + j, 0))
    fixed = lambda shape: pl.BlockSpec(shape, lambda i, j, s: (0, 0))
    chained = [] if chain is None else list(chain)
    extra = chained + list(after)
    at = 1 + 11 + 4
    aliases = {}
    if chained:
        aliases = {at + 3: 0} if final else {at: 4, at + 1: 5, at + 2: 6, at + 3: 0}
    grads = (
        (jax.ShapeDtypeStruct((d, 2 * units + width), BF),)
        if final
        else (
            jax.ShapeDtypeStruct((d, units), F32),
            jax.ShapeDtypeStruct((d, units), F32),
            jax.ShapeDtypeStruct((d, width), F32),
        )
    )
    return pl.pallas_call(
        functools.partial(
            ffn_kernel, chained=bool(chained), final=final, base=base, width=width, units=units
        ),
        out_shape=(
            jax.ShapeDtypeStruct(hidden.shape, BF),
            jax.ShapeDtypeStruct((count * rows, d), F32),
            jax.ShapeDtypeStruct((count * rows, width), BF),
            jax.ShapeDtypeStruct((8, d), F32),
        )
        + grads,
        grid_spec=pltpu.PrefetchScalarGridSpec(
            num_scalar_prefetch=1,
            grid=(count, tiles),
            in_specs=[whole, att, att, att, att, whole, fixed((8, d))]
            + [pl.BlockSpec((16, chunk), lambda i, j, s: (rows // 16, 0))] * 4
            + [ANY] * (4 + len(extra)),
            out_specs=[whole, flat(d), flat(width), fixed((8, d))]
            + ([fixed((d, 2 * units + width))] if final else [ANY] * 3),
            scratch_shapes=[
                pltpu.VMEM((4, d, units), BF),
                pltpu.VMEM((4, d, units), BF),
                pltpu.VMEM((4, d, width), BF),
                pltpu.VMEM((4, tile, units), BF),
                pltpu.VMEM((4, tile, units), BF),
                pltpu.VMEM((4, tile, units), BF),
                pltpu.VMEM((4, tile, width), BF),
                pltpu.VMEM((d, units), F32),
                pltpu.VMEM((d, units), F32),
                pltpu.VMEM((d, width), F32),
                pltpu.VMEM((4, 1, units), F32),
                pltpu.SemaphoreType.DMA((3, 16)),
                pltpu.SemaphoreType.DMA((3,)),
            ],
        ),
        input_output_aliases=aliases,
        compiler_params=params(),
        cost_estimate=pl.CostEstimate(
            flops=2 * count * rows * d * units * 20,
            bytes_accessed=16 * d * units + 16 * count * rows * d,
            transcendentals=8 * count * rows * units,
        ),
        name="ffn",
    )(ids, hidden, *atts, d_output, vec, *bias, *weights, *extra)


def dx_kernel(ids, dq_ref, *refs, nkv):
    dkv_refs = refs[:nkv]
    w_ref = refs[nkv]
    y_ref, joined_ref, sum_ref = refs[-3:]
    dq = dq_ref[...]
    dkv = dkv_refs[0][...]
    if nkv == 2:
        dkv = (dkv.astype(F32) + dkv_refs[1][...].astype(F32)).astype(BF)
    pad = jnp.zeros((dq.shape[0], 256 - dq.shape[1]), BF)
    joined = jnp.concatenate([dq, pad, dkv], axis=1)
    joined_ref[...] = joined

    @pl.when(pl.program_id(0) == 0)
    def _():
        sum_ref[...] = jnp.zeros_like(sum_ref)

    sum_ref[0:1] += col_sum(joined.astype(F32))
    y_ref[...] = dot_nt(joined, w_ref[...]).astype(BF)


def dx_call(ids, dq, dkvs, weight, first, tokens, chain, after):
    count = dq.shape[0]
    d, cols = weight.shape
    tile = min(count, 256)
    offset = first // tile
    flat = lambda w: pl.BlockSpec((tile, w), lambda i, s: (i, 0))
    extra = ([] if chain is None else [chain]) + list(after)
    return pl.pallas_call(
        functools.partial(dx_kernel, nkv=len(dkvs)),
        out_shape=(
            jax.ShapeDtypeStruct((count, d), BF),
            jax.ShapeDtypeStruct((tokens, cols), BF),
            jax.ShapeDtypeStruct((8, cols), F32),
        ),
        grid_spec=pltpu.PrefetchScalarGridSpec(
            num_scalar_prefetch=1,
            grid=(count // tile,),
            in_specs=[flat(dq.shape[1])]
            + [flat(v.shape[1]) for v in dkvs]
            + [pl.BlockSpec((d, cols), lambda i, s: (0, 0))]
            + [ANY] * len(extra),
            out_specs=[
                flat(d),
                pl.BlockSpec((tile, cols), lambda i, s: (offset + i, 0)),
                pl.BlockSpec((8, cols), lambda i, s: (0, 0)),
            ],
        ),
        input_output_aliases={} if chain is None else {3 + len(dkvs): 1},
        compiler_params=params(),
        cost_estimate=pl.CostEstimate(flops=3000000000, bytes_accessed=1000, transcendentals=0),
        name="dx",
    )(ids, dq, *dkvs, weight, *extra)


def grad_kernel(x_ref, joined_ref, *refs):
    g_ref, acc = refs[-2:]
    i = pl.program_id(0)

    @pl.when(i == 0)
    def _():
        acc[...] = jnp.zeros_like(acc)

    joined = joined_ref[...]
    acc[...] += dot(x_ref[0].T, joined)

    @pl.when(i == pl.num_programs(0) - 1)
    def _():
        g_ref[...] = acc[...].astype(BF)


def grad_call(hidden, joined, after):
    seqs, rows, d = hidden.shape
    cols = joined.shape[1]
    fixed = lambda shape: pl.BlockSpec(shape, lambda i: (0, 0))
    return pl.pallas_call(
        grad_kernel,
        out_shape=jax.ShapeDtypeStruct((d, cols), BF),
        grid=(seqs,),
        in_specs=[
            pl.BlockSpec((1, rows, d), lambda i: (i, 0, 0)),
            pl.BlockSpec((rows, cols), lambda i: (i, 0)),
        ]
        + [ANY] * len(after),
        out_specs=fixed((d, cols)),
        scratch_shapes=[pltpu.VMEM((d, cols), F32)],
        compiler_params=params(),
        cost_estimate=pl.CostEstimate(
            flops=2 * seqs * rows * d * cols, bytes_accessed=4 * d * cols, transcendentals=0
        ),
        name="grad",
    )(hidden, joined, *after)


def final_kernel(ids, dh1_ref, done_ref, other_ref, *refs):
    out_ref = refs[-1]
    upper = pl.program_id(0) == 0
    odd = lax.rem(ids[2], 2) == 1
    own = upper != odd
    both = jnp.where(own, done_ref[...].astype(F32), other_ref[...].astype(F32))
    out_ref[0] = dh1_ref[...] + both


def plain_kernel(dh1_ref, total_ref, *refs):
    refs[-1][0] = dh1_ref[...] + total_ref[...].astype(F32)


def plain_call(dh1, at, total, first, rows, seqs, chain, after):
    d = total.shape[1]
    tile = min(rows, 128)
    extra = ([] if chain is None else [chain]) + list(after)
    return pl.pallas_call(
        plain_kernel,
        out_shape=jax.ShapeDtypeStruct((seqs, rows, d), F32),
        grid=(rows // tile,),
        in_specs=[
            pl.BlockSpec((tile, d), lambda j: (at // tile + j, 0)),
            pl.BlockSpec((tile, d), lambda j: (j, 0)),
        ]
        + [ANY] * len(extra),
        out_specs=pl.BlockSpec((1, tile, d), lambda j: (first, j, 0)),
        input_output_aliases={} if chain is None else {2: 0},
        compiler_params=params(),
        cost_estimate=pl.CostEstimate(
            flops=2 * rows * d, bytes_accessed=10 * rows * d, transcendentals=0
        ),
        name="plain",
    )(dh1, total, *extra)


def final_call(ids, dh1, at, done, other, first, rows, seqs, chain, after):
    half, d = done.shape
    tile = min(half, 128)
    per_half = half // tile
    per_seq = rows // tile
    extra = ([] if chain is None else [chain]) + list(after)
    part = pl.BlockSpec((tile, d), lambda h, j, s: (j, 0))
    flat = lambda h, j: h * per_half + j
    return pl.pallas_call(
        final_kernel,
        out_shape=jax.ShapeDtypeStruct((seqs, rows, d), F32),
        grid_spec=pltpu.PrefetchScalarGridSpec(
            num_scalar_prefetch=1,
            grid=(2, per_half),
            in_specs=[
                pl.BlockSpec((tile, d), lambda h, j, s: (at // tile + flat(h, j), 0)),
                part,
                part,
            ]
            + [ANY] * len(extra),
            out_specs=pl.BlockSpec(
                (1, tile, d),
                lambda h, j, s: (first + flat(h, j) // per_seq, flat(h, j) % per_seq, 0),
            ),
        ),
        input_output_aliases={} if chain is None else {4: 0},
        compiler_params=params(),
        cost_estimate=pl.CostEstimate(
            flops=4 * half * d, bytes_accessed=24 * half * d, transcendentals=0
        ),
        name="final",
    )(ids, dh1, done, other, *extra)


def tp_gather(value):
    return [value] + [lax.ppermute(value, "tp", p) for p in (SWAP, FAR, ACROSS)]


def fsdp_gather(value):
    far = lax.ppermute(value, "fsdp", FAR)
    near = lax.ppermute(value, "fsdp", SWAP)
    return value, near, far, lax.ppermute(far, "fsdp", SWAP)


def tp_reduce(value, odd):
    half = value.shape[0] // 2
    top, bottom = value[:half], value[half:]
    sent = jnp.where(odd, top, bottom)
    got = lax.ppermute(sent, "tp", SWAP)
    pair = jnp.where(odd, bottom, top) + got
    done = pair + lax.ppermute(pair, "tp", FAR)
    return sent, pair, done, lax.ppermute(done, "tp", SWAP)


def ctx_sum(value, size):
    if size == 2:
        return value + lax.ppermute(value, "ctx", ((0, 1), (1, 0)))
    return lax.psum(value, "ctx")


def fsdp_far_sum(value, f):
    rows = value.shape[0] // 4
    pairs = value.reshape(2, 2, rows, value.shape[1])
    mine = lax.dynamic_index_in_dim(pairs, f // 2, 0, keepdims=False)
    other = lax.dynamic_index_in_dim(pairs, 1 - f // 2, 0, keepdims=False)
    return mine + lax.ppermute(other, "fsdp", FAR)


def fsdp_near_sum(mine, f, size):
    own = lax.dynamic_index_in_dim(mine, f % 2, 0, keepdims=False)
    near = lax.dynamic_index_in_dim(mine, 1 - f % 2, 0, keepdims=False)
    own = own + lax.ppermute(near, "fsdp", SWAP)
    return ctx_sum(own, size).astype(F32)


def fsdp_direct_sum(value, f, size):
    rows = value.shape[0] // 4
    blocks = value.reshape(4, rows, value.shape[1])
    pick = lambda k: lax.dynamic_index_in_dim(blocks, f ^ k, 0, keepdims=False)
    total = pick(0).astype(F32)
    for k, pairs in ((1, SWAP), (2, FAR), (3, ACROSS)):
        total = total + lax.ppermute(pick(k), "fsdp", pairs).astype(F32)
    return ctx_sum(total.astype(BF), size).astype(F32)


def all_sum(value, size):
    value = value + lax.ppermute(value, "fsdp", SWAP)
    value = value + lax.ppermute(value, "fsdp", FAR)
    return ctx_sum(value, size)


def body(
    hidden_in,
    prev_logits,
    w_query,
    w_key,
    w_value,
    w_out,
    w_inner,
    w_outer,
    b_query,
    b_value,
    b_out,
    b_inner,
    b_outer,
    gain_attn,
    shift_attn,
    gain_ffn,
    shift_ffn,
    d_output,
    d_logits,
    *,
    ctx_size,
):
    seqs, rows, d = hidden_in.shape
    heads = prev_logits.shape[1]
    width = w_query.shape[1]
    units = w_inner.shape[1]
    size = width // heads
    scale = size**-0.5
    f, c, rank = lax.axis_index("fsdp"), lax.axis_index("ctx"), lax.axis_index("tp")
    ids = jnp.stack([f, c, rank]).astype(jnp.int32)
    odd = rank % 2 == 1

    ffn_local = jnp.concatenate([w_inner, w_outer, w_out], axis=1)
    qkv_local = jnp.concatenate(
        [w_query, jnp.zeros((w_query.shape[0], 256 - width), BF), w_key, w_value], axis=1
    )
    qkv_pieces = fsdp_gather(qkv_local)
    inner_rank = (rank == 1) | (rank == 2)
    w_near = lax.ppermute(ffn_local, "tp", SWAP)
    w_across = lax.ppermute(ffn_local, "tp", MIDDLE)
    far = lambda value: lax.ppermute(value, "fsdp", FAR)
    own_local, _ = lax.optimization_barrier((ffn_local, qkv_pieces[2]))
    w_far = [far(own_local)]
    qkv_bias = jnp.concatenate([b_query, jnp.zeros((256,), F32), b_value])[None]
    vec = jnp.stack([b_out, gain_attn, shift_attn, b_outer, gain_ffn, shift_ffn, b_out, b_out])

    chunk = 2
    starts = range(0, seqs, chunk)
    queries, kvs, after = [], [], []
    for s in starts:
        q, kv, w_qkv = qkv_call(
            ids, hidden_in, s, chunk, qkv_pieces, qkv_bias, width, scale, after
        )
        after = [q]
        if s == 0:
            w_near, w_across, w_far[0], _ = lax.optimization_barrier(
                (w_near, w_across, w_far[0], q)
            )
            w_far.append(far(w_near))
            w_middle = lax.ppermute(w_near, "tp", MIDDLE)
            w_out_a = lax.ppermute(w_across, "tp", OUTWARD)
        queries.append(q)
        if ctx_size == 2:
            kvs.append((lax.ppermute(kv, "ctx", ((0, 1),)), kv))
        else:
            got = lax.all_gather(kv.reshape(chunk, rows, 2 * width), "ctx", axis=1, tiled=True)
            kvs.append((got.reshape(-1, 2 * width),))

    w_two = jnp.where(inner_rank, w_middle, w_out_a)
    w_far.append(far(w_two))
    w_out_b = lax.ppermute(w_middle, "tp", OUTWARD)
    after = after + [w_two]
    high = lax.reduce_precision(b_inner, 8, 7)
    middle = lax.reduce_precision(b_inner - high, 8, 7)
    parts = jnp.stack([high, middle, b_inner - high - middle]).reshape(6, units // 2)
    bias = jnp.pad(parts.astype(BF), ((0, 10), (0, 0)))
    logits, probs, atts, inverses = None, [], [], []
    for k, s in enumerate(starts):
        logits, e, att, inverse = attn_fwd_call(
            ids, queries[k], kvs[k], prev_logits, bias, s, chunk, logits, heads, size, after
        )
        after = [att]
        probs.append(e)
        if k == 0:
            atts.append(tp_gather(att))
        else:
            every = lax.all_gather(att, "tp", axis=0, tiled=False)
            atts.append([att] + [
                lax.dynamic_index_in_dim(every, rank ^ slot, 0, keepdims=False)
                for slot in range(1, 4)
            ])
        inverses.append(inverse)
        if k == 0:
            w_out_b, _ = lax.optimization_barrier((w_out_b, att))
            w_three = jnp.where(inner_rank, w_across, w_out_b)
            w_far.append(far(w_three))
            w_here = jnp.stack([ffn_local, w_near, w_two, w_three])
            w_there = lax.ppermute(w_here, "fsdp", SWAP)
            after = after + [w_here]
        else:
            w_far, atts[0], _ = lax.optimization_barrier((w_far, atts[0], att))
            w_far = jnp.stack(w_far)
            weights = [w_here, w_there, w_far, lax.ppermute(w_far, "fsdp", SWAP)]

    chain, sums, qkv_sums, dh1s, datts = None, [], [], {}, {}
    d_prev, d_hidden, joined = None, None, None

    def ffn(s, count, after):
        nonlocal chain, grad_ffn, output
        k, base = s // chunk, s % chunk
        final = s + count == seqs
        out = ffn_call(
            ids,
            hidden_in,
            atts[k],
            d_output,
            vec,
            atts[0],
            weights,
            s,
            base,
            count,
            chain,
            width,
            units,
            final,
            after,
        )
        output, dh1s[s], datts[s], part = out[:4]
        sums.append(part)
        if final:
            grad_ffn = out[4]
        else:
            chain = (out[4], out[5], out[6], output)
        return [datts[s]]

    def attn_bwd(s, count, after):
        nonlocal d_prev
        k, base = s // chunk, s % chunk
        out = attn_bwd_call(
            ids,
            queries[k],
            probs[k],
            d_logits,
            datts[k * chunk],
            atts[k][0],
            inverses[k],
            kvs[k],
            s,
            base,
            count,
            chunk,
            d_prev,
            heads,
            size,
            scale,
            after,
        )
        d_prev, dq = out[:2]
        if ctx_size == 2:
            dkvs = (out[2], lax.ppermute(out[3], "ctx", ((1, 0),)))
        else:
            full_grad = out[2].reshape(count, -1, 2 * width)
            part = lax.psum_scatter(full_grad, "ctx", scatter_dimension=1, tiled=True)
            dkvs = (part.reshape(-1, 2 * width),)
        return (dq, dkvs), [dq]

    def dx(s, grads, after):
        nonlocal joined
        y, joined, part = dx_call(
            ids, grads[0], grads[1], w_qkv, s * rows, seqs * rows, joined, after
        )
        qkv_sums.append(part)
        return y, [y]

    def finish(s, after):
        nonlocal d_hidden
        k, at = s // chunk, (s % chunk) * rows
        if not isinstance(reduced[s], tuple):
            d_hidden = plain_call(
                dh1s[k * chunk], at, reduced[s], s, rows, seqs, d_hidden, after
            )
            return [d_hidden]
        _, _, done, other = reduced[s]
        d_hidden = final_call(
            ids, dh1s[k * chunk], at, done, other, s, rows, seqs, d_hidden, after
        )
        return [d_hidden]

    grad_ffn = output = None
    held, reduced = {}, {}
    ys, ffn_far = {}, None
    for s in starts:
        after = ffn(s, chunk, after)
        last = s + chunk == seqs
        if last:
            ffn_far = fsdp_far_sum(grad_ffn, f)
        if not last:
            for i in range(s, s + chunk):
                held[i], after = attn_bwd(i, 1, after)
        for i in range(s, s + chunk):
            if last:
                extra = [reduced[0], reduced[1][1]] if i == s else []
                held[i], after = attn_bwd(i, 1, after + extra)
                finish(i - s, after)
                after = after + [d_hidden, reduced[i - 1][1 if i > s else 2]]
            ys[i], after = dx(i, held[i], after)
            if i == 0:
                reduced[i] = lax.psum(ys[i], "tp")
            else:
                reduced[i] = tp_reduce(ys[i], odd)
    after = after + [reduced[seqs - 1][1]]
    g_qkv = grad_call(hidden_in, joined, after)
    for s in range(seqs - chunk, seqs):
        finish(s, [g_qkv])

    small = jnp.concatenate([functools.reduce(jnp.add, sums), functools.reduce(jnp.add, qkv_sums)], axis=1)
    g_ffn = fsdp_near_sum(ffn_far, f, ctx_size)
    g_qkv, g_ffn = lax.optimization_barrier((g_qkv, g_ffn))
    g_qkv = fsdp_direct_sum(g_qkv, f, ctx_size)
    small, _ = lax.optimization_barrier((small, reduced[seqs - 2][2]))
    small = all_sum(small, ctx_size)
    return (
        output,
        logits,
        d_hidden,
        d_prev,
        g_qkv[:, :width],
        g_qkv[:, 256 : 256 + width],
        g_qkv[:, 256 + width :],
        g_ffn[:, 2 * units :],
        g_ffn[:, :units],
        g_ffn[:, units : 2 * units],
        small[0, d : d + width],
        small[0, d + 256 + width :],
        small[0, :d],
        small[6, :d],
        small[3, :d],
        small[1, :d],
        small[2, :d],
        small[4, :d],
        small[5, :d],
    )


def solution(mesh):
    tok, lgt, mat = P("fsdp", "ctx", None), P("fsdp", "tp", "ctx", None), P("fsdp", "tp")
    vec, rep = P("tp"), P()
    in_specs = (tok, lgt) + (mat,) * 6 + (vec, vec, rep, vec) + (rep,) * 5 + (tok, lgt)
    out_specs = (tok, lgt, tok, lgt) + (mat,) * 6 + (vec, vec, rep, vec) + (rep,) * 5
    return jax.shard_map(
        functools.partial(body, ctx_size=mesh.shape["ctx"]),
        mesh=mesh,
        in_specs=in_specs,
        out_specs=out_specs,
        check_vma=False,
    )
```
